32 devices in a mesh: row: 16 (over z, y, core), col: 2 (over x).
Axes of the slice: x: 2, y: 2, z: 4, core: 2. Of those that a mesh axis runs over, the one named last changes fastest.
Arguments:
- damping: bfloat16 [1536, 128, 1536], P('col', 'row'), may hold values from -60 to 60
- block_seeds: int32 [32], replicated, may hold values from 1 to 65520
Outputs:
- basis: float32 [32, 1536, 32], P('row', 'col')
The draws below stay inside these ranges and needn't reach their ends.
All inputs are finite; a program needn't handle non-finite values.
Results may differ from the reference program's by a relative error of at most 0.0057.
Values may be sent and summed in bfloat16 or wider, within the bound.
No kernel may reach another device: no remote copies, remote signals or barrier semaphores. Data moves between devices by JAX's collectives and lax.ppermute only.
A program may use at most 192 MiB of HBM per device.

```python
import math
import jax
import jax.numpy as jnp
from jax import lax

NF = 128
M = 1536
P_SIZE = 32
NB = 32
NSTEPS = 12


def draw_damping(key, part):
    col_idx = jnp.arange(M, dtype=jnp.float32)[:, None, None]
    col_scale = jnp.exp(jnp.log(3.0) * col_idx / M)
    values = jnp.clip(jax.random.normal(key, (M, NF, M), jnp.float32), -5.0, 5.0)
    return (values * col_scale).astype(jnp.bfloat16)


def with_ends(entries, own_key, least, largest):
    index_at = [jax.random.randint(jax.random.fold_in(own_key, axis), (), 0, length) for axis, length in enumerate(entries.shape)]
    longest = entries.shape.index(max(entries.shape))
    neighbour = index_at[:longest] + [(index_at[longest] + 1) % entries.shape[longest]] + index_at[longest + 1:]
    return entries.at[tuple(index_at)].set(least).at[tuple(neighbour)].set(largest)


def setup_inputs(seed: int = 0) -> dict:
    arg_keys = jax.random.split(jax.random.key(seed), 3)
    return {
        "damping": draw_damping(jax.random.fold_in(arg_keys[2], 71), 0),
        "block_seeds": with_ends(jax.random.randint(arg_keys[1], (NB,), 1, 65521), jax.random.fold_in(arg_keys[1], 1), 1, 65520).astype(jnp.int32),
    }


def lag_table():
    lag_idx = jnp.arange(2 * NB, dtype=jnp.float32)[:, None]
    freq_idx = jnp.arange(NF, dtype=jnp.float32)[None, :]
    window = jnp.exp(-math.log(3.0) * lag_idx / NB)
    cos_table = jnp.cos(math.pi * (freq_idx + 0.5) * lag_idx / NF) * window * math.sqrt(2.0 / NF) / math.sqrt(NB * M)
    return cos_table.astype(jnp.bfloat16)

def probe_blocks(block_seeds, start_col, number):
    prime_mod = 65521
    column = (start_col + jnp.arange(number, dtype=jnp.int32))[None, :, None]
    probe_col = jnp.arange(P_SIZE, dtype=jnp.int32)[None, None, :]
    seed_col = block_seeds.astype(jnp.int32)[:, None, None]
    inner_part = seed_col * (column + 1) % prime_mod * (column + 3) % prime_mod
    phase_val = (inner_part * (probe_col + 1) + seed_col * (probe_col + 1) % prime_mod * (probe_col + 2)) % prime_mod
    return jnp.cos(2.0 * math.pi * phase_val.astype(jnp.float32) / prime_mod).astype(jnp.bfloat16)

def hankel_stack(blocks, group_len):
    extent = blocks.shape[0] + group_len - 1
    padded = jnp.pad(blocks, ((group_len - 1, group_len - 1), (0, 0), (0, 0)))
    shifted = [padded[group_len - 1 - offset:group_len - 1 - offset + extent] for offset in range(group_len)]
    return jnp.stack(shifted, axis=2).reshape(extent, blocks.shape[1], group_len * blocks.shape[2])

def hankel_pass(lags_all, stack, shift_by, form, group_len):
    extent = stack.shape[0]
    stack_wide = stack.astype(jnp.float32)
    pieces = []
    for group in range(NB // group_len):
        start_lag = group * group_len + shift_by
        window_lags = lags_all[start_lag:start_lag + extent].astype(jnp.float32)
        product = jnp.einsum(form, window_lags, stack_wide)
        pieces.append(product.reshape(product.shape[0], group_len, P_SIZE).transpose(1, 0, 2))
    return jnp.concatenate(pieces, axis=0)

def finish(mine, gram):
    highest = lax.Precision.HIGHEST
    scale = jnp.trace(gram) + 1e-06
    current = gram / scale
    eye_mat = jnp.eye(P_SIZE, dtype=jnp.float32)
    inverse = eye_mat
    for repeat in range(NSTEPS):
        weight = 1.5 * eye_mat - 0.5 * jnp.dot(inverse, current, precision=highest)
        current = jnp.dot(current, weight, precision=highest)
        inverse = jnp.dot(weight, inverse, precision=highest)
    factor = math.sqrt(NB * M) / jnp.sqrt(scale)
    return factor * jnp.einsum('bcp,pq->bcq', mine, inverse, precision=highest)

def reference(damping, block_seeds):
    group_len = min(16, NB)
    cos_table = lag_table()
    by_freq = jnp.transpose(damping, (1, 2, 0)).reshape(NF, M * M)
    lags_all = jnp.dot(cos_table, by_freq, preferred_element_type=jnp.float32)
    lags_all = lags_all.astype(jnp.bfloat16).reshape(2 * NB, M, M)
    probes = probe_blocks(block_seeds, 0, M)
    forward = hankel_pass(lags_all, hankel_stack(probes, group_len), 0, 'lrc,lcn->rn', group_len)
    forward_b = forward.astype(jnp.bfloat16)
    backward = hankel_pass(lags_all, hankel_stack(forward_b, group_len), 1, 'lrc,lrn->cn', group_len)
    gram = jnp.einsum('bcp,bcq->pq', backward, backward, precision=lax.Precision.HIGHEST)
    return finish(backward, gram)
```

```python
import math

import numpy as np
import jax
import jax.numpy as jnp
from jax import lax
from jax.experimental import pallas as pl
from jax.experimental.pallas import tpu as pltpu
from jax.sharding import PartitionSpec as P

NSTEPS = 12
PRIME = 65521
P_SIZE = 32
BF16 = jnp.bfloat16
F32 = jnp.float32
NT = (((1,), (1,)), ((), ()))


def channel_table(n_freq, freqs, steps, n_blocks):
    angle = math.pi * (np.asarray(freqs)[:, None] + 0.5) / n_freq * np.asarray(steps)[None, :]
    decay = 3.0 ** (-np.asarray(steps) / n_blocks)
    return np.stack([decay * np.cos(angle), decay * np.sin(angle)], axis=1)


def high_low(values):
    high = values.astype(np.float32).astype(jnp.bfloat16)
    low = (values - high.astype(np.float64)).astype(np.float32).astype(jnp.bfloat16)
    return high, low


def cosine_turns(turns):
    u = turns * turns
    out = jnp.full_like(u, COS_COEFS[-1])
    for coef in COS_COEFS[-2::-1]:
        out = out * u + coef
    return out


def _fit_cosine():
    nodes = np.cos(np.pi * (np.arange(64) + 0.5) / 64)
    u = 0.125 * (nodes + 1.0)
    series = np.polynomial.chebyshev.Chebyshev.fit(
        u, np.cos(2 * np.pi * np.sqrt(u)), 8, domain=[0.0, 0.25]
    )
    coefs = series.convert(kind=np.polynomial.Polynomial, domain=[-1, 1], window=[-1, 1]).coef
    return [float(x) for x in coefs]


COS_COEFS = _fit_cosine()


def forward_kernel(n_local, inner_ref, shift_ref, whi_ref, wlo_ref, rep_ref, mask_ref, d_ref, t_ref, probes, acc):
    step = pl.program_id(0)
    n_blocks = inner_ref.shape[0]
    inner = inner_ref[...]
    for p in range(P_SIZE):
        x = inner * float(p + 1) + shift_ref[p]
        turns = (x - jnp.round(x * (1.0 / PRIME)) * float(PRIME)) * (1.0 / PRIME)
        probes[p * n_blocks : (p + 1) * n_blocks, :] = cosine_turns(turns).astype(BF16)
    rows, depth = whi_ref.shape
    parts = []
    for group in range(P_SIZE * n_blocks // depth):
        block = probes[group * depth : (group + 1) * depth, :]
        parts.append(
            jnp.dot(whi_ref[...], block, preferred_element_type=F32)
            + jnp.dot(wlo_ref[...], block, preferred_element_type=F32)
        )
    q = jnp.concatenate(parts, axis=0).astype(BF16)
    spread = jnp.dot(q, rep_ref[...], preferred_element_type=F32).astype(BF16)
    spread = spread * mask_ref[...]
    product = jnp.dot(spread, d_ref[...], preferred_element_type=F32)

    @pl.when(step == 0)
    def _():
        acc[...] = product

    @pl.when(step > 0)
    def _():
        acc[...] += product

    @pl.when(step == pl.num_programs(0) - 1)
    def _():
        t_ref[...] = acc[...].astype(BF16)


def middle_kernel(chi_ref, clo_ref, bhi_ref, blo_ref, x_ref, f_ref):
    x = x_ref[...]
    fwd = jnp.dot(chi_ref[...], x, preferred_element_type=F32) + jnp.dot(
        clo_ref[...], x, preferred_element_type=F32
    )
    high = fwd.astype(BF16)
    low = (fwd - high.astype(F32)).astype(BF16)
    out = (
        jnp.dot(bhi_ref[...], high, preferred_element_type=F32)
        + jnp.dot(bhi_ref[...], low, preferred_element_type=F32)
        + jnp.dot(blo_ref[...], high, preferred_element_type=F32)
    ).astype(BF16)
    n_rows, n_cols, channels, lanes = f_ref.shape
    out = out.reshape(n_rows, channels, lanes)
    for col in range(n_cols):
        f_ref[:, col] = out


def backward_kernel(khi_ref, klo_ref, sel_ref, mask_ref, f_ref, d_ref, keep_ref, send_ref):
    product = lax.dot_general(f_ref[...], d_ref[...], NT, preferred_element_type=F32)
    masked = product.astype(BF16) * mask_ref[...]
    u = jnp.dot(masked, sel_ref[...], preferred_element_type=F32).astype(BF16)
    rows, depth = khi_ref.shape
    half = keep_ref.shape[0]
    p_group = rows // (2 * half)
    for group in range(P_SIZE // p_group):
        block = u[group * depth : (group + 1) * depth, :]
        out = jnp.dot(khi_ref[...], block, preferred_element_type=F32) + jnp.dot(
            klo_ref[...], block, preferred_element_type=F32
        )
        out = out.reshape(2 * half, p_group, out.shape[-1])
        at = slice(group * p_group, (group + 1) * p_group)
        keep_ref[:, at, :] = out[:half]
        send_ref[:, at, :] = out[half:].astype(BF16)


def gram_kernel(x_ref, mine_ref, gram_ref):
    mine = jnp.sum(x_ref[...].astype(F32), axis=0)
    mine_ref[...] = mine
    gram = jnp.zeros((P_SIZE, P_SIZE), F32)
    for j in range(mine.shape[0]):
        gram += lax.dot_general(
            mine[j], mine[j], NT, preferred_element_type=F32, precision=lax.Precision.HIGHEST
        )
    gram_ref[...] = jnp.concatenate([gram[8 * i : 8 * i + 8] for i in range(P_SIZE // 8)], axis=1)


def last_kernel(factor, gram_ref, mine_ref, out_ref):
    total = jnp.sum(gram_ref[...], axis=0)
    gram = jnp.concatenate([total[:, P_SIZE * i : P_SIZE * (i + 1)] for i in range(P_SIZE // 8)], axis=0)
    row = lax.broadcasted_iota(jnp.int32, (P_SIZE, P_SIZE), 0)
    col = lax.broadcasted_iota(jnp.int32, (P_SIZE, P_SIZE), 1)
    eye = jnp.where(row == col, 1.0, 0.0).astype(F32)
    scale = jnp.sum(gram * eye, keepdims=True) + 1e-06

    def dot(a, b):
        return jnp.dot(a, b, preferred_element_type=F32, precision=lax.Precision.HIGHEST)

    current = gram / scale
    inverse = eye
    for _ in range(NSTEPS):
        weight = 1.5 * eye - 0.5 * dot(inverse, current)
        current = dot(current, weight)
        inverse = dot(weight, inverse)
    inverse = inverse * (factor / jnp.sqrt(scale))
    for j in range(mine_ref.shape[0]):
        out_ref[j] = lax.dot_general(
            inverse,
            mine_ref[j],
            (((0,), (0,)), ((), ())),
            preferred_element_type=F32,
            precision=lax.Precision.HIGHEST,
        )


def vmem(n):
    return [pl.BlockSpec(memory_space=pltpu.VMEM)] * n


def shards(damping, block_seeds, n_row, n_col):
    cols, local, m = damping.shape
    n_blocks = block_seeds.shape[0]
    n_freq = local * n_row
    channels = 2 * local
    n_dev = n_row * n_col
    amp = math.sqrt(2.0 / n_freq) / math.sqrt(n_blocks * m)
    row_at, col_at = lax.axis_index("row"), lax.axis_index("col")
    params = pltpu.CompilerParams(vmem_limit_bytes=60 << 20)

    block_c = 128 if cols % 128 == 0 else cols
    wide = block_c * local
    flat = damping.reshape(cols * local, m)

    freqs = np.arange(n_freq)
    steps = np.arange(n_blocks)
    w_all = channel_table(n_freq, freqs, steps, n_blocks)
    sign = np.array([1.0, -1.0])[None, :, None]
    back_all = channel_table(n_freq, freqs, steps + 1, n_blocks) * sign * amp
    per_row = w_all.reshape(n_row, channels, n_blocks)
    back_row = back_all.reshape(n_row, channels, n_blocks).transpose(0, 2, 1)

    def mine_of(table):
        return lax.dynamic_index_in_dim(jnp.asarray(table), row_at, 0, keepdims=False)

    def select(shape, dim, fn):
        r, c = np.indices(shape)
        return jnp.asarray((fn(r) == c) if dim == 0 else (r == fn(c)), BF16)

    pw = max(1, 256 // n_blocks)
    w_rows, w_depth = pw * channels, pw * n_blocks
    r, c = np.indices((w_rows, w_depth))
    w_mask = jnp.asarray(r // channels == c // n_blocks, F32)
    spread_l = select((w_rows, channels), 0, lambda a: a % channels)
    spread_r = select((n_blocks, w_depth), 1, lambda a: a % n_blocks)

    def spread_w(table):
        inner = jnp.dot(mine_of(table), spread_r, preferred_element_type=F32).astype(BF16)
        return (jnp.dot(spread_l, inner, preferred_element_type=F32) * w_mask).astype(BF16)

    w_hi, w_lo = (spread_w(t) for t in high_low(per_row))

    per_owner = n_blocks // n_row
    pk = min(P_SIZE, max(8, 256 // channels))
    k_rows, k_depth = n_blocks * pk, pk * channels
    r, c = np.indices((k_rows, k_depth))
    k_mask = jnp.asarray(r % pk == c // channels, F32)
    k_right = select((channels, k_depth), 1, lambda a: a % channels)
    parity = row_at % 2
    place = np.arange(n_blocks)
    half = n_blocks // 2
    flip = place // half
    chip, within = (place % half) // per_owner, (place % half) % per_owner
    order = (chip * 2) * per_owner + within + ((flip + parity) % 2) * per_owner
    pick = (order[:, None] == jnp.arange(n_blocks)[None, :]).astype(BF16)
    k_left = select((k_rows, n_blocks), 0, lambda a: a // pk)

    def spread_k(table):
        ordered = jnp.dot(pick, mine_of(table), preferred_element_type=F32).astype(BF16)
        inner = jnp.dot(ordered, k_right, preferred_element_type=F32).astype(BF16)
        return (jnp.dot(k_left, inner, preferred_element_type=F32) * k_mask).astype(BF16)

    k_hi, k_lo = (spread_k(t) for t in high_low(back_row))

    n_rows = P_SIZE * channels
    r, c = np.indices((n_rows, wide))
    own = jnp.asarray((r // 2) % local == c % local, BF16)
    repeat = select((block_c, wide), 1, lambda a: a // local)
    gather = select((wide, block_c), 0, lambda a: a // local)

    seeds = block_seeds[:, None]
    column = (col_at * cols + jnp.arange(cols, dtype=jnp.int32))[None, :]
    inner = (seeds * (column + 1) % PRIME * (column + 3) % PRIME).astype(F32)
    pcol = jnp.arange(P_SIZE, dtype=jnp.int32)[:, None]
    shift = (block_seeds[None, :] * (pcol + 1) % PRIME * (pcol + 2) % PRIME).astype(F32)
    shift = jnp.broadcast_to(shift[:, :, None], (P_SIZE, n_blocks, block_c))

    whole = lambda *s: pl.BlockSpec(s, lambda i: (0,) * len(s))
    t = pl.pallas_call(
        lambda *refs: forward_kernel(local, *refs),
        grid=(cols // block_c,),
        out_shape=jax.ShapeDtypeStruct((n_rows, m), BF16),
        in_specs=[
            pl.BlockSpec((n_blocks, block_c), lambda i: (0, i)),
            whole(P_SIZE, n_blocks, block_c),
            whole(w_rows, w_depth),
            whole(w_rows, w_depth),
            whole(block_c, wide),
            whole(n_rows, wide),
            pl.BlockSpec((wide, m), lambda i: (i, 0)),
        ],
        out_specs=whole(n_rows, m),
        scratch_shapes=[
            pltpu.VMEM((P_SIZE * n_blocks, block_c), BF16),
            pltpu.VMEM((n_rows, m), F32),
        ],
        compiler_params=params,
        name="forward",
    )(inner, shift, w_hi, w_lo, repeat, own, flat)

    n_p = math.gcd(P_SIZE, n_dev)
    n_r = n_dev // n_p
    p_own, lanes = P_SIZE // n_p, m // n_r
    t = t.reshape(n_p, p_own * channels, n_r, lanes).transpose(0, 2, 1, 3)
    t = t.reshape(n_dev, p_own * channels, lanes)
    t = lax.all_to_all(t, ("row", "col"), 0, 0, tiled=True)
    t = t.reshape(n_dev, p_own, channels, lanes).transpose(0, 2, 1, 3)
    t = t.reshape(n_dev * channels, p_own * lanes)

    merge = w_all.reshape(n_freq, 2, n_blocks) * sign * amp
    merge = merge.reshape(n_row, 1, channels, n_blocks).repeat(n_col, axis=1)
    merge = merge.reshape(n_dev * channels, n_blocks).T
    c_hi, c_lo = high_low(merge)
    b_hi, b_lo = high_low(w_all.reshape(n_row * channels, n_blocks))
    block_l = 512 if (p_own * lanes) % 512 == 0 else p_own * lanes
    f = pl.pallas_call(
        middle_kernel,
        grid=(p_own * lanes // block_l,),
        out_shape=jax.ShapeDtypeStruct((n_row, n_col, channels, p_own * lanes), BF16),
        in_specs=[
            whole(n_blocks, n_dev * channels),
            whole(n_blocks, n_dev * channels),
            whole(n_row * channels, n_blocks),
            whole(n_row * channels, n_blocks),
            pl.BlockSpec((n_dev * channels, block_l), lambda i: (0, i)),
        ],
        out_specs=pl.BlockSpec((n_row, n_col, channels, block_l), lambda i: (0, 0, 0, i)),
        compiler_params=params,
        name="middle",
    )(*(jnp.asarray(x) for x in (c_hi, c_lo, b_hi, b_lo)), t)
    f = f.reshape(n_dev, channels, p_own, lanes).transpose(0, 2, 1, 3).reshape(n_dev, p_own * channels, lanes)
    f = lax.all_to_all(f, ("row", "col"), 0, 0, tiled=True)
    f = f.reshape(n_p, n_r, p_own * channels, lanes).transpose(0, 2, 1, 3).reshape(n_rows, m)

    keep, send = pl.pallas_call(
        backward_kernel,
        grid=(cols // block_c,),
        out_shape=(
            jax.ShapeDtypeStruct((half, P_SIZE, cols), F32),
            jax.ShapeDtypeStruct((half, P_SIZE, cols), BF16),
        ),
        in_specs=[
            whole(k_rows, k_depth),
            whole(k_rows, k_depth),
            whole(wide, block_c),
            whole(n_rows, wide),
            whole(n_rows, m),
            pl.BlockSpec((wide, m), lambda i: (i, 0)),
        ],
        out_specs=(
            pl.BlockSpec((half, P_SIZE, block_c), lambda i: (0, 0, i)),
            pl.BlockSpec((half, P_SIZE, block_c), lambda i: (0, 0, i)),
        ),
        compiler_params=params,
        name="backward",
    )(k_hi, k_lo, gather, own, f, flat)
    got = lax.ppermute(send, "row", [(i, i ^ 1) for i in range(n_row)])
    summed = (keep + got.astype(F32)).astype(BF16)
    groups = [list(range(core, n_row, 2)) for core in range(2)]
    summed = lax.all_to_all(summed, "row", 0, 0, axis_index_groups=groups, tiled=True)
    summed = summed.reshape(n_row // 2, per_owner, P_SIZE, cols)

    mine, gram = pl.pallas_call(
        gram_kernel,
        out_shape=(
            jax.ShapeDtypeStruct((per_owner, P_SIZE, cols), F32),
            jax.ShapeDtypeStruct((8, 4 * P_SIZE), F32),
        ),
        in_specs=vmem(1),
        out_specs=tuple(vmem(2)),
        compiler_params=params,
        name="gram",
    )(summed)
    gram = jnp.broadcast_to(gram[None], (n_dev, *gram.shape))
    gram = lax.all_to_all(gram, ("row", "col"), 0, 0, tiled=True)
    out = pl.pallas_call(
        lambda *refs: last_kernel(math.sqrt(n_blocks * m), *refs),
        out_shape=jax.ShapeDtypeStruct((per_owner, P_SIZE, cols), F32),
        in_specs=vmem(2),
        out_specs=vmem(1)[0],
        compiler_params=params,
        name="last",
    )(gram, mine)
    return out.transpose(0, 2, 1)


def solution(mesh):
    n_row, n_col = mesh.shape["row"], mesh.shape["col"]
    return jax.shard_map(
        lambda damping, block_seeds: shards(damping, block_seeds, n_row, n_col),
        mesh=mesh,
        in_specs=(P("col", "row", None), P()),
        out_specs=P("row", "col", None),
        check_vma=False,
    )
```

```python
import math

import numpy as np
import jax
import jax.numpy as jnp
from jax import lax
from jax.experimental import pallas as pl
from jax.experimental.pallas import tpu as pltpu
from jax.sharding import PartitionSpec as P

NSTEPS = 12
PRIME = 65521
P_SIZE = 32
BF16 = jnp.bfloat16
F32 = jnp.float32
NT = (((1,), (1,)), ((), ()))


def channel_table(n_freq, freqs, steps, n_blocks):
    angle = math.pi * (np.asarray(freqs)[:, None] + 0.5) / n_freq * np.asarray(steps)[None, :]
    decay = 3.0 ** (-np.asarray(steps) / n_blocks)
    return np.stack([decay * np.cos(angle), decay * np.sin(angle)], axis=1)


def high_low(values):
    high = values.astype(np.float32).astype(jnp.bfloat16)
    low = (values - high.astype(np.float64)).astype(np.float32).astype(jnp.bfloat16)
    return high, low


def cosine_turns(turns):
    u = turns * turns
    out = jnp.full_like(u, COS_COEFS[-1])
    for coef in COS_COEFS[-2::-1]:
        out = out * u + coef
    return out


def _fit_cosine():
    nodes = np.cos(np.pi * (np.arange(64) + 0.5) / 64)
    u = 0.125 * (nodes + 1.0)
    series = np.polynomial.chebyshev.Chebyshev.fit(
        u, np.cos(2 * np.pi * np.sqrt(u)), 8, domain=[0.0, 0.25]
    )
    coefs = series.convert(kind=np.polynomial.Polynomial, domain=[-1, 1], window=[-1, 1]).coef
    return [float(x) for x in coefs]


COS_COEFS = _fit_cosine()


def place(rows, cols, test):
    r = lax.broadcasted_iota(jnp.int32, (rows, cols), 0)
    c = lax.broadcasted_iota(jnp.int32, (rows, cols), 1)
    return test(r, c).astype(F32)


def less_turns(x):
    return x - (x.astype(F32) * (1.0 / PRIME)).astype(jnp.int32) * PRIME


def forward_kernel(local, seeds_ref, table_ref, d_ref, t_ref, held, wide, acc, probes, shift, spread, q_all, sems):
    n_chunks, rows, m = held.shape
    block_c = rows // local
    channels = 2 * local
    n_blocks, lanes = seeds_ref.shape
    group = 8
    tiles = P_SIZE // 8
    lane_w = wide.shape[-1]
    per_pass = wide.shape[1]

    def copy(b):
        return pltpu.make_async_copy(d_ref.at[pl.ds(b * rows, rows)], held.at[b], sems.at[b])

    for b in range(n_chunks):
        copy(b).start()
    start = lax.axis_index("col") * (n_chunks * block_c)
    table = table_ref[lax.axis_index("row")]
    left = place(channels * group, channels, lambda r, c: r // group == c)
    right = place(n_blocks, group * n_blocks, lambda r, c: r == c % n_blocks)
    same = place(channels * group, group * n_blocks, lambda r, c: r % group == c // n_blocks)
    for part in range(2):
        w = jnp.dot(table[part * channels : (part + 1) * channels], right, preferred_element_type=F32)
        spread[part] = (jnp.dot(left, w, preferred_element_type=F32) * same).astype(BF16)
    seeds = seeds_ref[...]
    for p in range(P_SIZE):
        x = (seeds * (p + 1)).astype(F32)
        shift[p] = (x - jnp.round(x * (1.0 / PRIME)) * float(PRIME)) * float(p + 2)
    acc[...] = jnp.zeros_like(acc)

    @pl.loop(0, n_chunks)
    def _(b):
        lane = lax.broadcasted_iota(jnp.int32, (n_blocks, lanes), 1)
        for at in range(0, block_c, lanes):
            column = start + b * block_c + at + lane
            inner = less_turns(less_turns(seeds * (column + 1)) * (column + 3)).astype(F32)
            for p in range(P_SIZE):
                x = inner * float(p + 1) + shift[p]
                turns = (x - jnp.round(x * (1.0 / PRIME)) * float(PRIME)) * (1.0 / PRIME)
                probes[p * n_blocks : (p + 1) * n_blocks, at : at + lanes] = cosine_turns(turns).astype(BF16)
        for g in range(P_SIZE // group):
            block = probes[g * group * n_blocks : (g + 1) * group * n_blocks, :]
            q = jnp.dot(spread[0], block, preferred_element_type=F32) + jnp.dot(
                spread[1], block, preferred_element_type=F32
            )
            q_all[:, g * group : (g + 1) * group, :] = q.reshape(channels, group, block_c)
        copy(b).wait()
        for i in range(m // (per_pass * lane_w)):
            for l in range(per_pass):
                at = (i * per_pass + l) * lane_w
                wide[i % 2, l] = held[b, :, at : at + lane_w].astype(F32)
            for k in range(local):
                s = jnp.concatenate(
                    [wide[i % 2, l, pl.ds(k, block_c, stride=local), :] for l in range(per_pass)], axis=1
                ).astype(BF16)
                q = jnp.concatenate([q_all[k], q_all[local + k]], axis=0).astype(BF16)
                o = jnp.dot(q, s, preferred_element_type=F32)
                for l in range(per_pass):
                    for t in range(2 * tiles):
                        acc[i * per_pass + l, t, k * 8 : k * 8 + 8, :] += o[
                            t * 8 : t * 8 + 8, l * lane_w : (l + 1) * lane_w
                        ]

    for l in range(m // lane_w):
        for p in range(P_SIZE):
            t = jnp.concatenate(
                [acc[l, part * tiles + p // 8, pl.ds(p % 8, local, stride=8), :] for part in range(2)], axis=0
            )
            t_ref[p, :, l * lane_w : (l + 1) * lane_w] = t.astype(BF16)


def separate_kernel(local, d_ref, o_ref, wide):
    rows, m = d_ref.shape
    lane_w = wide.shape[-1]
    for l in range(m // lane_w):
        at = slice(l * lane_w, (l + 1) * lane_w)
        wide[l % 2] = d_ref[:, at].astype(F32)
        for k in range(local):
            o_ref[k, at, :] = wide[l % 2, pl.ds(k, rows // local, stride=local), :].T.astype(BF16)


def middle_kernel(chi_ref, clo_ref, bhi_ref, blo_ref, x_ref, f_ref):
    x = x_ref[...]
    fwd = jnp.dot(chi_ref[...], x, preferred_element_type=F32) + jnp.dot(
        clo_ref[...], x, preferred_element_type=F32
    )
    high = fwd.astype(BF16)
    low = (fwd - high.astype(F32)).astype(BF16)
    out = (
        jnp.dot(bhi_ref[...], high, preferred_element_type=F32)
        + jnp.dot(bhi_ref[...], low, preferred_element_type=F32)
        + jnp.dot(blo_ref[...], high, preferred_element_type=F32)
    ).astype(BF16)
    n_rows, n_cols, channels, lanes = f_ref.shape
    out = out.reshape(n_rows, channels, lanes)
    for col in range(n_cols):
        f_ref[:, col] = out


def backward_kernel(khi_ref, klo_ref, f_ref, d_ref, keep_ref, send_ref, wide, f_by):
    local, m, _ = d_ref.shape
    channels = 2 * local
    tiles = P_SIZE // 8
    lane_w = wide.shape[-1]

    @pl.when(pl.program_id(0) == 0)
    def _():
        for l in range(m // lane_w):
            at = slice(l * lane_w, (l + 1) * lane_w)
            for p in range(P_SIZE):
                x = f_ref[p * channels : (p + 1) * channels, at].astype(F32)
                for part in range(2):
                    wide[l % 2, part * tiles + p // 8, (p % 8) * local : (p % 8 + 1) * local, :] = x[
                        part * local : (part + 1) * local
                    ]
            for k in range(local):
                f_by[k, :, at] = jnp.concatenate(
                    [wide[l % 2, t, pl.ds(k, 8, stride=local), :] for t in range(2 * tiles)], axis=0
                ).astype(BF16)

    u = [jnp.dot(f_by[k], d_ref[k], preferred_element_type=F32).astype(BF16) for k in range(local)]
    half = keep_ref.shape[0]
    group = khi_ref.shape[0] // (2 * half)
    for g in range(P_SIZE // group):
        block = jnp.concatenate(
            [
                u[k][part * P_SIZE + g * group : part * P_SIZE + (g + 1) * group]
                for k in range(local)
                for part in range(2)
            ],
            axis=0,
        )
        out = jnp.dot(khi_ref[...], block, preferred_element_type=F32) + jnp.dot(
            klo_ref[...], block, preferred_element_type=F32
        )
        out = out.reshape(2 * half, group, out.shape[-1])
        at = slice(g * group, (g + 1) * group)
        keep_ref[:, at, :] = out[:half]
        send_ref[:, at, :] = out[half:].astype(BF16)


def gram_kernel(x_ref, mine_ref, gram_ref):
    mine = jnp.sum(x_ref[...].astype(F32), axis=0)
    mine_ref[...] = mine
    gram = jnp.zeros((P_SIZE, P_SIZE), F32)
    for j in range(mine.shape[0]):
        gram += lax.dot_general(
            mine[j], mine[j], NT, preferred_element_type=F32, precision=lax.Precision.HIGHEST
        )
    gram_ref[...] = jnp.concatenate([gram[8 * i : 8 * i + 8] for i in range(P_SIZE // 8)], axis=1)


def last_kernel(factor, gram_ref, mine_ref, out_ref):
    total = jnp.sum(gram_ref[...], axis=0)
    gram = jnp.concatenate([total[:, P_SIZE * i : P_SIZE * (i + 1)] for i in range(P_SIZE // 8)], axis=0)
    row = lax.broadcasted_iota(jnp.int32, (P_SIZE, P_SIZE), 0)
    col = lax.broadcasted_iota(jnp.int32, (P_SIZE, P_SIZE), 1)
    eye = jnp.where(row == col, 1.0, 0.0).astype(F32)
    scale = jnp.sum(gram * eye, keepdims=True) + 1e-06

    def dot(a, b):
        return jnp.dot(a, b, preferred_element_type=F32, precision=lax.Precision.HIGHEST)

    current = gram / scale
    inverse = eye
    for _ in range(NSTEPS):
        weight = 1.5 * eye - 0.5 * dot(inverse, current)
        current = dot(current, weight)
        inverse = dot(weight, inverse)
    inverse = inverse * (factor / jnp.sqrt(scale))
    for j in range(mine_ref.shape[0]):
        out_ref[j] = lax.dot_general(
            inverse,
            mine_ref[j],
            (((0,), (0,)), ((), ())),
            preferred_element_type=F32,
            precision=lax.Precision.HIGHEST,
        )


def vmem(n):
    return [pl.BlockSpec(memory_space=pltpu.VMEM)] * n


def shards(damping, block_seeds, n_row, n_col):
    cols, local, m = damping.shape
    n_blocks = block_seeds.shape[0]
    n_freq = local * n_row
    channels = 2 * local
    n_dev = n_row * n_col
    amp = math.sqrt(2.0 / n_freq) / math.sqrt(n_blocks * m)
    row_at, col_at = lax.axis_index("row"), lax.axis_index("col")
    params = pltpu.CompilerParams(vmem_limit_bytes=60 << 20)

    block_c = 256 if cols % 256 == 0 else cols
    lanes_c = 128 if block_c % 128 == 0 else block_c
    lane_w = 128 if m % 128 == 0 else m
    per_pass = 2 if m % (2 * lane_w) == 0 else 1
    flat = damping.reshape(cols * local, m)

    freqs = np.arange(n_freq)
    steps = np.arange(n_blocks)
    w_all = channel_table(n_freq, freqs, steps, n_blocks)
    sign = np.array([1.0, -1.0])[None, :, None]
    back_all = channel_table(n_freq, freqs, steps + 1, n_blocks) * sign * amp
    back_row = back_all.reshape(n_row, channels, n_blocks).transpose(0, 2, 1)

    def by_channel(table):
        table = table.reshape(n_row, local, 2, n_blocks)
        return table.transpose(0, 2, 1, 3).reshape(n_row, channels, n_blocks)

    w_row = by_channel(w_all)
    w_parts = np.concatenate([x.astype(np.float32) for x in high_low(w_row)], axis=1)

    def mine_of(table):
        return lax.dynamic_index_in_dim(jnp.asarray(table), row_at, 0, keepdims=False)

    def select(shape, dim, fn):
        r, c = np.indices(shape)
        return jnp.asarray((fn(r) == c) if dim == 0 else (r == fn(c)), BF16)

    per_owner = n_blocks // n_row
    pk = 16
    k_rows, k_depth = n_blocks * pk, pk * channels
    r, c = np.indices((k_rows, k_depth))
    k_mask = jnp.asarray(r % pk == c % pk, F32)
    k_right = select((channels, k_depth), 1, lambda a: a // pk)
    parity = row_at % 2
    place = np.arange(n_blocks)
    half = n_blocks // 2
    flip = place // half
    chip, within = (place % half) // per_owner, (place % half) % per_owner
    order = (chip * 2) * per_owner + within + ((flip + parity) % 2) * per_owner
    pick = (order[:, None] == jnp.arange(n_blocks)[None, :]).astype(BF16)
    k_left = select((k_rows, n_blocks), 0, lambda a: a // pk)

    def spread_k(table):
        ordered = jnp.dot(pick, mine_of(table), preferred_element_type=F32).astype(BF16)
        inner = jnp.dot(ordered, k_right, preferred_element_type=F32).astype(BF16)
        return (jnp.dot(k_left, inner, preferred_element_type=F32) * k_mask).astype(BF16)

    k_hi, k_lo = (spread_k(t) for t in high_low(back_row))

    n_rows = P_SIZE * channels
    seeds = jnp.broadcast_to(block_seeds[:, None], (n_blocks, lanes_c))

    whole = lambda *s: pl.BlockSpec(s, lambda i: (0,) * len(s))
    v_one = pl.BlockSpec(memory_space=pltpu.VMEM)
    work = 2 * cols * local * m
    t = pl.pallas_call(
        lambda *refs: forward_kernel(local, *refs),
        out_shape=jax.ShapeDtypeStruct((P_SIZE, channels, m), BF16),
        in_specs=[v_one, v_one, pl.BlockSpec(memory_space=pl.ANY)],
        out_specs=v_one,
        scratch_shapes=[
            pltpu.VMEM((cols // block_c, block_c * local, m), BF16),
            pltpu.VMEM((2, per_pass, block_c * local, lane_w), F32),
            pltpu.VMEM((m // lane_w, P_SIZE // 4, 8 * local, lane_w), F32),
            pltpu.VMEM((P_SIZE * n_blocks, block_c), BF16),
            pltpu.VMEM((P_SIZE, n_blocks, lanes_c), F32),
            pltpu.VMEM((2, channels * 8, 8 * n_blocks), BF16),
            pltpu.VMEM((channels, P_SIZE, block_c), F32),
            pltpu.SemaphoreType.DMA((cols // block_c,)),
        ],
        compiler_params=params,
        cost_estimate=pl.CostEstimate(flops=64 * work, bytes_accessed=work, transcendentals=0),
        name="forward",
    )(seeds, jnp.asarray(w_parts), flat)
    t, flat = lax.optimization_barrier((t, flat))
    block_s = 128 if cols % 128 == 0 else cols
    by_freq = pl.pallas_call(
        lambda *refs: separate_kernel(local, *refs),
        grid=(cols // block_s,),
        out_shape=jax.ShapeDtypeStruct((local, m, cols), BF16),
        in_specs=[pl.BlockSpec((block_s * local, m), lambda i: (i, 0))],
        out_specs=pl.BlockSpec((local, m, block_s), lambda i: (0, 0, i)),
        scratch_shapes=[pltpu.VMEM((2, block_s * local, lane_w), F32)],
        compiler_params=params,
        cost_estimate=pl.CostEstimate(flops=work, bytes_accessed=2 * work, transcendentals=0),
        name="separate",
    )(flat)

    n_p = math.gcd(P_SIZE, n_dev)
    n_r = n_dev // n_p
    p_own, lanes = P_SIZE // n_p, m // n_r
    t = t.reshape(n_p, p_own * channels, n_r, lanes).transpose(0, 2, 1, 3)
    t = t.reshape(n_dev, p_own * channels, lanes)
    t = lax.all_to_all(t, ("row", "col"), 0, 0, tiled=True)
    t = t.reshape(n_dev, p_own, channels, lanes).transpose(0, 2, 1, 3)
    t = t.reshape(n_dev * channels, p_own * lanes)

    merge = by_channel(w_all * sign * amp)
    merge = merge.reshape(n_row, 1, channels, n_blocks).repeat(n_col, axis=1)
    merge = merge.reshape(n_dev * channels, n_blocks).T
    c_hi, c_lo = high_low(merge)
    b_hi, b_lo = high_low(w_row.reshape(n_row * channels, n_blocks))
    block_l = 512 if (p_own * lanes) % 512 == 0 else p_own * lanes
    f = pl.pallas_call(
        middle_kernel,
        grid=(p_own * lanes // block_l,),
        out_shape=jax.ShapeDtypeStruct((n_row, n_col, channels, p_own * lanes), BF16),
        in_specs=[
            whole(n_blocks, n_dev * channels),
            whole(n_blocks, n_dev * channels),
            whole(n_row * channels, n_blocks),
            whole(n_row * channels, n_blocks),
            pl.BlockSpec((n_dev * channels, block_l), lambda i: (0, i)),
        ],
        out_specs=pl.BlockSpec((n_row, n_col, channels, block_l), lambda i: (0, 0, 0, i)),
        compiler_params=params,
        name="middle",
    )(*(jnp.asarray(x) for x in (c_hi, c_lo, b_hi, b_lo)), t)
    f = f.reshape(n_dev, channels, p_own, lanes).transpose(0, 2, 1, 3).reshape(n_dev, p_own * channels, lanes)
    f = lax.all_to_all(f, ("row", "col"), 0, 0, tiled=True)
    f = f.reshape(n_p, n_r, p_own * channels, lanes).transpose(0, 2, 1, 3).reshape(n_rows, m)

    keep, send = pl.pallas_call(
        backward_kernel,
        grid=(cols // block_s,),
        out_shape=(
            jax.ShapeDtypeStruct((half, P_SIZE, cols), F32),
            jax.ShapeDtypeStruct((half, P_SIZE, cols), BF16),
        ),
        in_specs=[
            whole(k_rows, k_depth),
            whole(k_rows, k_depth),
            whole(n_rows, m),
            pl.BlockSpec((local, m, block_s), lambda i: (0, 0, i)),
        ],
        out_specs=(
            pl.BlockSpec((half, P_SIZE, block_s), lambda i: (0, 0, i)),
            pl.BlockSpec((half, P_SIZE, block_s), lambda i: (0, 0, i)),
        ),
        scratch_shapes=[
            pltpu.VMEM((2, P_SIZE // 4, 8 * local, lane_w), F32),
            pltpu.VMEM((local, 2 * P_SIZE, m), BF16),
        ],
        compiler_params=params,
        cost_estimate=pl.CostEstimate(flops=64 * work, bytes_accessed=work, transcendentals=0),
        name="backward",
    )(k_hi, k_lo, f, by_freq)
    got = lax.ppermute(send, "row", [(i, i ^ 1) for i in range(n_row)])
    summed = (keep + got.astype(F32)).astype(BF16)
    groups = [list(range(core, n_row, 2)) for core in range(2)]
    summed = lax.all_to_all(summed, "row", 0, 0, axis_index_groups=groups, tiled=True)
    summed = summed.reshape(n_row // 2, per_owner, P_SIZE, cols)

    mine, gram = pl.pallas_call(
        gram_kernel,
        out_shape=(
            jax.ShapeDtypeStruct((per_owner, P_SIZE, cols), F32),
            jax.ShapeDtypeStruct((8, 4 * P_SIZE), F32),
        ),
        in_specs=vmem(1),
        out_specs=tuple(vmem(2)),
        compiler_params=params,
        name="gram",
    )(summed)
    gram = jnp.broadcast_to(gram[None], (n_dev, *gram.shape))
    gram = lax.all_to_all(gram, ("row", "col"), 0, 0, tiled=True)
    out = pl.pallas_call(
        lambda *refs: last_kernel(math.sqrt(n_blocks * m), *refs),
        out_shape=jax.ShapeDtypeStruct((per_owner, P_SIZE, cols), F32),
        in_specs=vmem(2),
        out_specs=vmem(1)[0],
        compiler_params=params,
        name="last",
    )(gram, mine)
    return out.transpose(0, 2, 1)


def solution(mesh):
    n_row, n_col = mesh.shape["row"], mesh.shape["col"]
    return jax.shard_map(
        lambda damping, block_seeds: shards(damping, block_seeds, n_row, n_col),
        mesh=mesh,
        in_specs=(P("col", "row", None), P()),
        out_specs=P("row", "col", None),
        check_vma=False,
    )
```

```python
import math

import numpy as np
import jax
import jax.numpy as jnp
from jax import lax
from jax.experimental import pallas as pl
from jax.experimental.pallas import tpu as pltpu
from jax.sharding import PartitionSpec as P

NSTEPS = 12
PRIME = 65521
P_SIZE = 32
BF16 = jnp.bfloat16
F32 = jnp.float32
NT = (((1,), (1,)), ((), ()))


def channel_table(n_freq, freqs, steps, n_blocks):
    angle = math.pi * (np.asarray(freqs)[:, None] + 0.5) / n_freq * np.asarray(steps)[None, :]
    decay = 3.0 ** (-np.asarray(steps) / n_blocks)
    return np.stack([decay * np.cos(angle), decay * np.sin(angle)], axis=1)


def high_low(values):
    high = values.astype(np.float32).astype(jnp.bfloat16)
    low = (values - high.astype(np.float64)).astype(np.float32).astype(jnp.bfloat16)
    return high, low


def cosine_turns(turns):
    u = turns * turns
    out = jnp.full_like(u, COS_COEFS[-1])
    for coef in COS_COEFS[-2::-1]:
        out = out * u + coef
    return out


def _fit_cosine():
    nodes = np.cos(np.pi * (np.arange(64) + 0.5) / 64)
    u = 0.125 * (nodes + 1.0)
    series = np.polynomial.chebyshev.Chebyshev.fit(
        u, np.cos(2 * np.pi * np.sqrt(u)), 8, domain=[0.0, 0.25]
    )
    coefs = series.convert(kind=np.polynomial.Polynomial, domain=[-1, 1], window=[-1, 1]).coef
    return [float(x) for x in coefs]


COS_COEFS = _fit_cosine()


def place(rows, cols, test):
    r = lax.broadcasted_iota(jnp.int32, (rows, cols), 0)
    c = lax.broadcasted_iota(jnp.int32, (rows, cols), 1)
    return test(r, c).astype(F32)


def less_turns(x):
    return x - (x.astype(F32) * (1.0 / PRIME)).astype(jnp.int32) * PRIME


def forward_kernel(local, seeds_ref, table_ref, d_ref, t_ref, held, wide, acc, probes, shift, spread, q_all, sems):
    n_chunks, rows, m = held.shape
    block_c = rows // local
    channels = 2 * local
    n_blocks, lanes = seeds_ref.shape
    group = 8
    tiles = P_SIZE // 8
    lane_w = wide.shape[-1]
    per_pass = wide.shape[1]

    def copy(b):
        return pltpu.make_async_copy(d_ref.at[pl.ds(b * rows, rows)], held.at[b], sems.at[b])

    for b in range(n_chunks):
        copy(b).start()
    start = lax.axis_index("col") * (n_chunks * block_c)
    table = table_ref[lax.axis_index("row")]
    left = place(channels * group, channels, lambda r, c: r // group == c)
    right = place(n_blocks, group * n_blocks, lambda r, c: r == c % n_blocks)
    same = place(channels * group, group * n_blocks, lambda r, c: r % group == c // n_blocks)
    for part in range(2):
        w = jnp.dot(table[part * channels : (part + 1) * channels], right, preferred_element_type=F32)
        spread[part] = (jnp.dot(left, w, preferred_element_type=F32) * same).astype(BF16)
    seeds = seeds_ref[...]
    for p in range(P_SIZE):
        x = (seeds * (p + 1)).astype(F32)
        shift[p] = (x - jnp.round(x * (1.0 / PRIME)) * float(PRIME)) * float(p + 2)
    acc[...] = jnp.zeros_like(acc)

    @pl.loop(0, n_chunks)
    def _(b):
        lane = lax.broadcasted_iota(jnp.int32, (n_blocks, lanes), 1)
        for at in range(0, block_c, lanes):
            column = start + b * block_c + at + lane
            inner = less_turns(less_turns(seeds * (column + 1)) * (column + 3)).astype(F32)
            for p in range(P_SIZE):
                x = inner * float(p + 1) + shift[p]
                turns = (x - jnp.round(x * (1.0 / PRIME)) * float(PRIME)) * (1.0 / PRIME)
                probes[p * n_blocks : (p + 1) * n_blocks, at : at + lanes] = cosine_turns(turns).astype(BF16)
        for g in range(P_SIZE // group):
            block = probes[g * group * n_blocks : (g + 1) * group * n_blocks, :]
            q = jnp.dot(spread[0], block, preferred_element_type=F32) + jnp.dot(
                spread[1], block, preferred_element_type=F32
            )
            q_all[:, g * group : (g + 1) * group, :] = q.reshape(channels, group, block_c)
        copy(b).wait()
        for i in range(m // (per_pass * lane_w)):
            for l in range(per_pass):
                at = (i * per_pass + l) * lane_w
                wide[i % 2, l] = held[b, :, at : at + lane_w].astype(F32)
            for k in range(local):
                s = jnp.concatenate(
                    [wide[i % 2, l, pl.ds(k, block_c, stride=local), :] for l in range(per_pass)], axis=1
                ).astype(BF16)
                q = jnp.concatenate([q_all[k], q_all[local + k]], axis=0).astype(BF16)
                o = jnp.dot(q, s, preferred_element_type=F32)
                for l in range(per_pass):
                    for t in range(2 * tiles):
                        acc[i * per_pass + l, t, k * 8 : k * 8 + 8, :] += o[
                            t * 8 : t * 8 + 8, l * lane_w : (l + 1) * lane_w
                        ]

    for l in range(m // lane_w):
        for p in range(P_SIZE):
            t = jnp.concatenate(
                [acc[l, part * tiles + p // 8, pl.ds(p % 8, local, stride=8), :] for part in range(2)], axis=0
            )
            t_ref[p, :, l * lane_w : (l + 1) * lane_w] = t.astype(BF16)


def separate_kernel(local, d_ref, o_ref, wide):
    rows, m = d_ref.shape
    lane_w = wide.shape[-1]
    for l in range(m // lane_w):
        at = slice(l * lane_w, (l + 1) * lane_w)
        wide[l % 2] = d_ref[:, at].astype(F32)
        for k in range(local):
            o_ref[k, at, :] = wide[l % 2, pl.ds(k, rows // local, stride=local), :].T.astype(BF16)


def half_of(n_row):
    return lax.axis_index("row") // (n_row // 2)


def gather_kernel(n_row, c_ref, x_ref, keep_ref, send_ref):
    n_src, p_own, channels, lanes = x_ref.shape
    table = c_ref[half_of(n_row)]
    n = table.shape[0] // 2
    for p in range(p_own):
        x = x_ref[:, p].reshape(n_src * channels, lanes)
        both = jnp.dot(table, x, preferred_element_type=F32)
        out = both[:n] + both[n:]
        keep_ref[p] = out
        send_ref[p] = out.astype(BF16)


def scatter_kernel(n_row, b_ref, keep_ref, got_ref, f_ref):
    n_rows, n_cols, p_own, channels, lanes = f_ref.shape
    table = b_ref[half_of(n_row)]
    for p in range(p_own):
        forward = keep_ref[p] + got_ref[p].astype(F32)
        high = forward.astype(BF16)
        low = (forward - high.astype(F32)).astype(BF16)
        out = jnp.dot(table, jnp.concatenate([high, low, high], axis=0), preferred_element_type=F32)
        out = out.astype(BF16).reshape(n_rows, channels, lanes)
        for col in range(n_cols):
            f_ref[:, col, p] = out


def join_kernel(x_ref, keep_ref, send_ref):
    x = x_ref[...].astype(F32)
    total = jnp.sum(x, axis=0)
    keep_ref[...] = total[0]
    send_ref[...] = total[1].astype(BF16)


def backward_kernel(khi_ref, klo_ref, f_ref, d_ref, keep_ref, send_ref, wide, f_by):
    local, m, _ = d_ref.shape
    channels = 2 * local
    tiles = P_SIZE // 8
    lane_w = wide.shape[-1]

    @pl.when(pl.program_id(0) == 0)
    def _():
        for l in range(m // lane_w):
            at = slice(l * lane_w, (l + 1) * lane_w)
            for p in range(P_SIZE):
                x = f_ref[p * channels : (p + 1) * channels, at].astype(F32)
                for part in range(2):
                    wide[l % 2, part * tiles + p // 8, (p % 8) * local : (p % 8 + 1) * local, :] = x[
                        part * local : (part + 1) * local
                    ]
            for k in range(local):
                f_by[k, :, at] = jnp.concatenate(
                    [wide[l % 2, t, pl.ds(k, 8, stride=local), :] for t in range(2 * tiles)], axis=0
                ).astype(BF16)

    u = [jnp.dot(f_by[k], d_ref[k], preferred_element_type=F32).astype(BF16) for k in range(local)]
    half = keep_ref.shape[0]
    group = khi_ref.shape[0] // (2 * half)
    for g in range(P_SIZE // group):
        block = jnp.concatenate(
            [
                u[k][part * P_SIZE + g * group : part * P_SIZE + (g + 1) * group]
                for k in range(local)
                for part in range(2)
            ],
            axis=0,
        )
        out = jnp.dot(khi_ref[...], block, preferred_element_type=F32) + jnp.dot(
            klo_ref[...], block, preferred_element_type=F32
        )
        out = out.reshape(2 * half, group, out.shape[-1])
        at = slice(g * group, (g + 1) * group)
        keep_ref[:, at, :] = out[:half]
        send_ref[:, at, :] = out[half:].astype(BF16)


def gram_kernel(keep_ref, got_ref, mine_ref, gram_ref):
    mine = keep_ref[...] + got_ref[...].astype(F32)
    mine_ref[...] = mine
    gram = jnp.zeros((P_SIZE, P_SIZE), F32)
    for j in range(mine.shape[0]):
        gram += lax.dot_general(
            mine[j], mine[j], NT, preferred_element_type=F32, precision=lax.Precision.HIGHEST
        )
    gram = jnp.concatenate([gram[8 * i : 8 * i + 8] for i in range(P_SIZE // 8)], axis=1)
    for i in range(gram_ref.shape[0]):
        gram_ref[i] = gram


def last_kernel(factor, gram_ref, mine_ref, out_ref):
    total = jnp.sum(gram_ref[...], axis=0)
    gram = jnp.concatenate([total[:, P_SIZE * i : P_SIZE * (i + 1)] for i in range(P_SIZE // 8)], axis=0)
    row = lax.broadcasted_iota(jnp.int32, (P_SIZE, P_SIZE), 0)
    col = lax.broadcasted_iota(jnp.int32, (P_SIZE, P_SIZE), 1)
    eye = jnp.where(row == col, 1.0, 0.0).astype(F32)
    scale = jnp.sum(gram * eye, keepdims=True) + 1e-06

    def dot(a, b):
        return jnp.dot(a, b, preferred_element_type=F32, precision=lax.Precision.HIGHEST)

    current = gram / scale
    inverse = eye
    for _ in range(NSTEPS):
        weight = 1.5 * eye - 0.5 * dot(inverse, current)
        current = dot(current, weight)
        inverse = dot(weight, inverse)
    inverse = inverse * (factor / jnp.sqrt(scale))
    for j in range(mine_ref.shape[0]):
        out_ref[j] = lax.dot_general(
            inverse,
            mine_ref[j],
            (((0,), (0,)), ((), ())),
            preferred_element_type=F32,
            precision=lax.Precision.HIGHEST,
        )


def vmem(n):
    return [pl.BlockSpec(memory_space=pltpu.VMEM)] * n


def shards(damping, block_seeds, n_row, n_col):
    cols, local, m = damping.shape
    n_blocks = block_seeds.shape[0]
    n_freq = local * n_row
    channels = 2 * local
    n_dev = n_row * n_col
    amp = math.sqrt(2.0 / n_freq) / math.sqrt(n_blocks * m)
    row_at, col_at = lax.axis_index("row"), lax.axis_index("col")
    large, params = (pltpu.CompilerParams(vmem_limit_bytes=x << 20) for x in (40, 20))

    block_c = 256 if cols % 256 == 0 else cols
    lanes_c = 128 if block_c % 128 == 0 else block_c
    lane_w = 128 if m % 128 == 0 else m
    per_pass = 2 if m % (2 * lane_w) == 0 else 1
    flat = damping.reshape(cols * local, m)

    freqs = np.arange(n_freq)
    steps = np.arange(n_blocks)
    w_all = channel_table(n_freq, freqs, steps, n_blocks)
    sign = np.array([1.0, -1.0])[None, :, None]
    back_all = channel_table(n_freq, freqs, steps + 1, n_blocks) * sign * amp
    back_row = back_all.reshape(n_row, channels, n_blocks).transpose(0, 2, 1)

    def by_channel(table):
        table = table.reshape(n_row, local, 2, n_blocks)
        return table.transpose(0, 2, 1, 3).reshape(n_row, channels, n_blocks)

    w_row = by_channel(w_all)
    w_parts = np.concatenate([x.astype(np.float32) for x in high_low(w_row)], axis=1)

    def mine_of(table):
        return lax.dynamic_index_in_dim(jnp.asarray(table), row_at, 0, keepdims=False)

    def select(shape, dim, fn):
        r, c = np.indices(shape)
        return jnp.asarray((fn(r) == c) if dim == 0 else (r == fn(c)), BF16)

    per_owner = n_blocks // n_row
    pk = 16
    k_rows, k_depth = n_blocks * pk, pk * channels
    r, c = np.indices((k_rows, k_depth))
    k_mask = jnp.asarray(r % pk == c % pk, F32)
    k_right = select((channels, k_depth), 1, lambda a: a // pk)
    parity = row_at % 2
    place = np.arange(n_blocks)
    half = n_blocks // 2
    quarter = n_row // 4
    flip, rest = place // half, place % half
    spot, far, within = rest // (2 * per_owner), rest // per_owner % 2, rest % per_owner
    chip = spot + quarter * ((far + half_of(n_row)) % 2)
    order = (2 * chip + (flip + parity) % 2) * per_owner + within
    pick = (order[:, None] == jnp.arange(n_blocks)[None, :]).astype(BF16)
    k_left = select((k_rows, n_blocks), 0, lambda a: a // pk)

    def spread_k(table):
        ordered = jnp.dot(pick, mine_of(table), preferred_element_type=F32).astype(BF16)
        inner = jnp.dot(ordered, k_right, preferred_element_type=F32).astype(BF16)
        return (jnp.dot(k_left, inner, preferred_element_type=F32) * k_mask).astype(BF16)

    k_hi, k_lo = (spread_k(t) for t in high_low(back_row))

    n_rows = P_SIZE * channels
    seeds = jnp.broadcast_to(block_seeds[:, None], (n_blocks, lanes_c))

    whole = lambda *s: pl.BlockSpec(s, lambda i: (0,) * len(s))
    v_one = pl.BlockSpec(memory_space=pltpu.VMEM)
    work = 2 * cols * local * m
    t = pl.pallas_call(
        lambda *refs: forward_kernel(local, *refs),
        out_shape=jax.ShapeDtypeStruct((P_SIZE, channels, m), BF16),
        in_specs=[v_one, v_one, pl.BlockSpec(memory_space=pl.ANY)],
        out_specs=v_one,
        scratch_shapes=[
            pltpu.VMEM((cols // block_c, block_c * local, m), BF16),
            pltpu.VMEM((2, per_pass, block_c * local, lane_w), F32),
            pltpu.VMEM((m // lane_w, P_SIZE // 4, 8 * local, lane_w), F32),
            pltpu.VMEM((P_SIZE * n_blocks, block_c), BF16),
            pltpu.VMEM((P_SIZE, n_blocks, lanes_c), F32),
            pltpu.VMEM((2, channels * 8, 8 * n_blocks), BF16),
            pltpu.VMEM((channels, P_SIZE, block_c), F32),
            pltpu.SemaphoreType.DMA((cols // block_c,)),
        ],
        compiler_params=large,
        cost_estimate=pl.CostEstimate(flops=64 * work, bytes_accessed=work, transcendentals=0),
        name="forward",
    )(seeds, jnp.asarray(w_parts), flat)
    t, flat = lax.optimization_barrier((t, flat))
    block_s = 128 if cols % 128 == 0 else cols
    by_freq = pl.pallas_call(
        lambda *refs: separate_kernel(local, *refs),
        grid=(cols // block_s,),
        out_shape=jax.ShapeDtypeStruct((local, m, cols), BF16),
        in_specs=[pl.BlockSpec((block_s * local, m), lambda i: (i, 0))],
        out_specs=pl.BlockSpec((local, m, block_s), lambda i: (0, 0, i)),
        scratch_shapes=[pltpu.VMEM((2, block_s * local, lane_w), F32)],
        compiler_params=params,
        cost_estimate=pl.CostEstimate(flops=work, bytes_accessed=2 * work, transcendentals=0),
        name="separate",
    )(flat)

    n_grp = n_dev // 2
    n_p = math.gcd(P_SIZE, n_grp)
    n_r = n_grp // n_p
    p_own, lanes = P_SIZE // n_p, m // n_r
    halves = [list(range(n_grp)), list(range(n_grp, n_dev))]
    across = [(i, (i + n_row // 2) % n_row) for i in range(n_row)]
    t = t.reshape(n_p, p_own * channels, n_r, lanes).transpose(0, 2, 1, 3)
    t = t.reshape(n_grp, p_own * channels, lanes)
    t = lax.all_to_all(t, ("row", "col"), 0, 0, axis_index_groups=halves, tiled=True)
    t = t.reshape(n_grp, p_own, channels, lanes)

    merge = by_channel(w_all * sign * amp).reshape(2, n_row // 2, 1, channels, n_blocks).repeat(n_col, axis=2)
    merge = merge.reshape(2, n_grp * channels, n_blocks).transpose(0, 2, 1)
    merge = np.concatenate(high_low(merge), axis=1)
    b_hi, b_lo = high_low(w_row.reshape(2, n_row // 2 * channels, n_blocks))
    fan = np.concatenate([b_hi, b_hi, b_lo], axis=2)
    keep, send = pl.pallas_call(
        lambda *refs: gather_kernel(n_row, *refs),
        out_shape=(
            jax.ShapeDtypeStruct((p_own, n_blocks, lanes), F32),
            jax.ShapeDtypeStruct((p_own, n_blocks, lanes), BF16),
        ),
        in_specs=vmem(2),
        out_specs=tuple(vmem(2)),
        compiler_params=params,
        name="gather",
    )(jnp.asarray(merge), t)
    got = lax.ppermute(send, "row", across)
    f = pl.pallas_call(
        lambda *refs: scatter_kernel(n_row, *refs),
        out_shape=jax.ShapeDtypeStruct((n_row // 2, n_col, p_own, channels, lanes), BF16),
        in_specs=vmem(3),
        out_specs=v_one,
        compiler_params=params,
        name="scatter",
    )(jnp.asarray(fan), keep, got)
    f = f.reshape(n_grp, p_own * channels, lanes)
    f = lax.all_to_all(f, ("row", "col"), 0, 0, axis_index_groups=halves, tiled=True)
    f = f.reshape(n_p, n_r, p_own * channels, lanes).transpose(0, 2, 1, 3).reshape(n_rows, m)

    keep, send = pl.pallas_call(
        backward_kernel,
        grid=(cols // block_s,),
        out_shape=(
            jax.ShapeDtypeStruct((half, P_SIZE, cols), F32),
            jax.ShapeDtypeStruct((half, P_SIZE, cols), BF16),
        ),
        in_specs=[
            whole(k_rows, k_depth),
            whole(k_rows, k_depth),
            whole(n_rows, m),
            pl.BlockSpec((local, m, block_s), lambda i: (0, 0, i)),
        ],
        out_specs=(
            pl.BlockSpec((half, P_SIZE, block_s), lambda i: (0, 0, i)),
            pl.BlockSpec((half, P_SIZE, block_s), lambda i: (0, 0, i)),
        ),
        scratch_shapes=[
            pltpu.VMEM((2, P_SIZE // 4, 8 * local, lane_w), F32),
            pltpu.VMEM((local, 2 * P_SIZE, m), BF16),
        ],
        compiler_params=params,
        cost_estimate=pl.CostEstimate(flops=64 * work, bytes_accessed=work, transcendentals=0),
        name="backward",
    )(k_hi, k_lo, f, by_freq)
    got = lax.ppermute(send, "row", [(i, i ^ 1) for i in range(n_row)])
    summed = (keep + got.astype(F32)).astype(BF16)
    groups = [[core + 2 * (i + quarter * h) for i in range(quarter)] for h in range(2) for core in range(2)]
    summed = lax.all_to_all(summed, "row", 0, 0, axis_index_groups=groups, tiled=True)
    summed = summed.reshape(quarter, 2, per_owner, P_SIZE, cols)
    keep, send = pl.pallas_call(
        join_kernel,
        out_shape=(
            jax.ShapeDtypeStruct((per_owner, P_SIZE, cols), F32),
            jax.ShapeDtypeStruct((per_owner, P_SIZE, cols), BF16),
        ),
        in_specs=vmem(1),
        out_specs=tuple(vmem(2)),
        compiler_params=params,
        name="join",
    )(summed)
    got = lax.ppermute(send, "row", across)

    mine, gram = pl.pallas_call(
        gram_kernel,
        out_shape=(
            jax.ShapeDtypeStruct((per_owner, P_SIZE, cols), F32),
            jax.ShapeDtypeStruct((n_dev, 8, 4 * P_SIZE), F32),
        ),
        in_specs=vmem(2),
        out_specs=tuple(vmem(2)),
        compiler_params=params,
        name="gram",
    )(keep, got)
    gram = lax.all_to_all(gram, ("row", "col"), 0, 0, tiled=True)
    out = pl.pallas_call(
        lambda *refs: last_kernel(math.sqrt(n_blocks * m), *refs),
        out_shape=jax.ShapeDtypeStruct((per_owner, P_SIZE, cols), F32),
        in_specs=vmem(2),
        out_specs=vmem(1)[0],
        compiler_params=params,
        name="last",
    )(gram, mine)
    return out.transpose(0, 2, 1)


def solution(mesh):
    n_row, n_col = mesh.shape["row"], mesh.shape["col"]
    return jax.shard_map(
        lambda damping, block_seeds: shards(damping, block_seeds, n_row, n_col),
        mesh=mesh,
        in_specs=(P("col", "row", None), P()),
        out_specs=P("row", "col", None),
        check_vma=False,
    )
```

```python
import math

import numpy as np
import jax
import jax.numpy as jnp
from jax import lax
from jax.experimental import pallas as pl
from jax.experimental.pallas import tpu as pltpu
from jax.sharding import PartitionSpec as P

NSTEPS = 12
PRIME = 65521
P_SIZE = 32
BF16 = jnp.bfloat16
F32 = jnp.float32
NT = (((1,), (1,)), ((), ()))


def channel_table(n_freq, freqs, steps, n_blocks):
    angle = math.pi * (np.asarray(freqs)[:, None] + 0.5) / n_freq * np.asarray(steps)[None, :]
    decay = 3.0 ** (-np.asarray(steps) / n_blocks)
    return np.stack([decay * np.cos(angle), decay * np.sin(angle)], axis=1)


def high_low(values):
    high = values.astype(np.float32).astype(jnp.bfloat16)
    low = (values - high.astype(np.float64)).astype(np.float32).astype(jnp.bfloat16)
    return high, low


def cosine_turns(turns):
    u = turns * turns
    out = jnp.full_like(u, COS_COEFS[-1])
    for coef in COS_COEFS[-2::-1]:
        out = out * u + coef
    return out


def _fit_cosine():
    nodes = np.cos(np.pi * (np.arange(64) + 0.5) / 64)
    u = 0.125 * (nodes + 1.0)
    series = np.polynomial.chebyshev.Chebyshev.fit(
        u, np.cos(2 * np.pi * np.sqrt(u)), 8, domain=[0.0, 0.25]
    )
    coefs = series.convert(kind=np.polynomial.Polynomial, domain=[-1, 1], window=[-1, 1]).coef
    return [float(x) for x in coefs]


COS_COEFS = _fit_cosine()


def place(rows, cols, test):
    r = lax.broadcasted_iota(jnp.int32, (rows, cols), 0)
    c = lax.broadcasted_iota(jnp.int32, (rows, cols), 1)
    return test(r, c).astype(F32)


def less_turns(x):
    return x - (x.astype(F32) * (1.0 / PRIME)).astype(jnp.int32) * PRIME


def forward_kernel(local, seeds_ref, table_ref, d_ref, t_ref, held, wide, acc, probes, shift, spread, q_all, own, sems, sem):
    n_chunks, rows, m = held.shape
    block_c = rows // local
    channels = 2 * local
    n_blocks, lanes = shift.shape[1:]
    group = 8
    tiles = P_SIZE // 8
    lane_w = wide.shape[-1]
    per_pass = wide.shape[1]

    def copy(b):
        return pltpu.make_async_copy(d_ref.at[pl.ds(b * rows, rows)], held.at[b], sems.at[b])

    fetch = pltpu.make_async_copy(table_ref.at[lax.axis_index("row")], own, sem)
    fetch.start()
    for b in range(n_chunks):
        copy(b).start()
    start = lax.axis_index("col") * (n_chunks * block_c)
    line = lax.broadcasted_iota(jnp.int32, (n_blocks, lanes), 0)
    seeds = jnp.zeros((n_blocks, lanes), jnp.int32)
    for j in range(n_blocks):
        seeds = jnp.where(line == j, seeds_ref[j], seeds)
    for p in range(P_SIZE):
        x = (seeds * (p + 1)).astype(F32)
        shift[p] = (x - jnp.round(x * (1.0 / PRIME)) * float(PRIME)) * float(p + 2)
    acc[...] = jnp.zeros_like(acc)
    fetch.wait()
    table = own[...]
    left = place(channels * group, channels, lambda r, c: r // group == c)
    right = place(n_blocks, group * n_blocks, lambda r, c: r == c % n_blocks)
    same = place(channels * group, group * n_blocks, lambda r, c: r % group == c // n_blocks)
    for part in range(2):
        w = jnp.dot(table[part * channels : (part + 1) * channels], right, preferred_element_type=F32)
        spread[part] = (jnp.dot(left, w, preferred_element_type=F32) * same).astype(BF16)

    @pl.loop(0, n_chunks)
    def _(b):
        lane = lax.broadcasted_iota(jnp.int32, (n_blocks, lanes), 1)
        for at in range(0, block_c, lanes):
            column = start + b * block_c + at + lane
            inner = less_turns(less_turns(seeds * (column + 1)) * (column + 3)).astype(F32)
            for p in range(P_SIZE):
                x = inner * float(p + 1) + shift[p]
                turns = (x - jnp.round(x * (1.0 / PRIME)) * float(PRIME)) * (1.0 / PRIME)
                probes[p * n_blocks : (p + 1) * n_blocks, at : at + lanes] = cosine_turns(turns).astype(BF16)
        for g in range(P_SIZE // group):
            block = probes[g * group * n_blocks : (g + 1) * group * n_blocks, :]
            q = jnp.dot(spread[0], block, preferred_element_type=F32) + jnp.dot(
                spread[1], block, preferred_element_type=F32
            )
            q_all[:, g * group : (g + 1) * group, :] = q.reshape(channels, group, block_c)
        copy(b).wait()
        for i in range(m // (per_pass * lane_w)):
            for l in range(per_pass):
                at = (i * per_pass + l) * lane_w
                wide[i % 2, l] = held[b, :, at : at + lane_w].astype(F32)
            for k in range(local):
                s = jnp.concatenate(
                    [wide[i % 2, l, pl.ds(k, block_c, stride=local), :] for l in range(per_pass)], axis=1
                ).astype(BF16)
                q = jnp.concatenate([q_all[k], q_all[local + k]], axis=0).astype(BF16)
                o = jnp.dot(q, s, preferred_element_type=F32)
                for l in range(per_pass):
                    for t in range(2 * tiles):
                        acc[i * per_pass + l, t, k * 8 : k * 8 + 8, :] += o[
                            t * 8 : t * 8 + 8, l * lane_w : (l + 1) * lane_w
                        ]

    for l in range(m // lane_w):
        for p in range(P_SIZE):
            t = jnp.concatenate(
                [acc[l, part * tiles + p // 8, pl.ds(p % 8, local, stride=8), :] for part in range(2)], axis=0
            )
            t_ref[p, :, l * lane_w : (l + 1) * lane_w] = t.astype(BF16)


def separate_kernel(local, n_row, group, d_ref, table_ref, o_ref, khi_ref, klo_ref, wide):
    rows, m = d_ref.shape
    lane_w = wide.shape[-1]

    @pl.when(pl.program_id(0) == 0)
    def _():
        row_at = lax.axis_index("row")
        table = table_ref[row_at]
        channels = 2 * local
        n_blocks = table.shape[0] // 2
        half, own, quarter = n_blocks // 2, n_blocks // n_row, n_row // 4

        def is_owner(r, c):
            rest = r % half
            chip = rest // (2 * own) + quarter * ((rest // own + half_of(n_row)) % 2)
            return (2 * chip + (r // half + row_at) % 2) * own + rest % own == c

        pick = place(n_blocks, n_blocks, is_owner)
        right = place(channels, channels * group, lambda r, c: r == c // 32 * 2 + c // 8 % 2)
        left = place(n_blocks * group, n_blocks, lambda r, c: r // group == c)
        same = place(n_blocks * group, channels * group, lambda r, c: r % group == c // 16 % 2 * 8 + c % 8)
        for part, out_ref in enumerate((khi_ref, klo_ref)):
            k = jnp.dot(pick, table[part * n_blocks : (part + 1) * n_blocks], preferred_element_type=F32)
            k = jnp.dot(left, jnp.dot(k, right, preferred_element_type=F32), preferred_element_type=F32)
            out_ref[...] = (k * same).astype(BF16)

    for l in range(m // lane_w):
        at = slice(l * lane_w, (l + 1) * lane_w)
        wide[l % 2] = d_ref[:, at].astype(F32)
        for k in range(local):
            o_ref[k, at, :] = wide[l % 2, pl.ds(k, rows // local, stride=local), :].T.astype(BF16)


def half_of(n_row):
    return lax.axis_index("row") // (n_row // 2)


def gather_kernel(n_row, c_ref, x_ref, keep_ref, send_ref):
    n_src, p_own, channels, lanes = x_ref.shape
    table = c_ref[half_of(n_row)]
    n = table.shape[0] // 2
    for p in range(p_own):
        x = x_ref[:, p].reshape(n_src * channels, lanes)
        both = jnp.dot(table, x, preferred_element_type=F32)
        out = both[:n] + both[n:]
        keep_ref[p] = out
        send_ref[p] = out.astype(BF16)


def scatter_kernel(n_row, b_ref, keep_ref, got_ref, f_ref):
    n_rows, n_cols, p_own, channels, lanes = f_ref.shape
    table = b_ref[half_of(n_row)]
    for p in range(p_own):
        forward = keep_ref[p] + got_ref[p].astype(F32)
        high = forward.astype(BF16)
        low = (forward - high.astype(F32)).astype(BF16)
        out = jnp.dot(table, jnp.concatenate([high, low, high], axis=0), preferred_element_type=F32)
        out = out.astype(BF16).reshape(n_rows, channels, lanes)
        for col in range(n_cols):
            f_ref[:, col, p] = out


def join_kernel(x_ref, keep_ref, send_ref):
    x = x_ref[...].astype(F32)
    total = jnp.sum(x, axis=0)
    keep_ref[...] = total[0]
    send_ref[...] = total[1].astype(BF16)


def backward_kernel(local, khi_ref, klo_ref, f_ref, d_ref, keep_ref, send_ref, held, f_by, sems):
    n_chunks, _, m, block_c = held.shape
    rows = f_ref.shape[0] // 4
    channels = 2 * local

    def copy(b):
        at = pl.ds(pl.multiple_of(b * block_c, block_c), block_c) if n_chunks > 1 else slice(None)
        return pltpu.make_async_copy(d_ref.at[:, :, at], held.at[b], sems.at[b])

    for b in range(n_chunks):
        copy(b).start()

    swap = place(rows, rows, lambda r, c: (r % 8 * 2 + r // 8 % 2) * local + r // 16 == c).astype(BF16)
    for g in range(4):
        out = jnp.dot(swap, f_ref[g * rows : (g + 1) * rows, :], preferred_element_type=F32).astype(BF16)
        for k in range(local):
            f_by[k, g * 16 : g * 16 + 16, :] = out[k * 16 : k * 16 + 16]

    half = keep_ref.shape[0]

    @pl.loop(0, n_chunks)
    def _(b):
        copy(b).wait()
        at = pl.ds(pl.multiple_of(b * block_c, block_c), block_c) if n_chunks > 1 else slice(None)
        u = [jnp.dot(f_by[k], held[b, k], preferred_element_type=F32).astype(BF16) for k in range(local)]
        for g in range(2):
            block = jnp.concatenate([x[g * 32 : g * 32 + 32] for x in u], axis=0)
            out = jnp.dot(khi_ref[...], block, preferred_element_type=F32) + jnp.dot(
                klo_ref[...], block, preferred_element_type=F32
            )
            out = out.reshape(2 * half, 16, block_c)
            keep_ref[:, g * 16 : g * 16 + 16, at] = out[:half]
            send_ref[:, g * 16 : g * 16 + 16, at] = out[half:].astype(BF16)


def gram_kernel(keep_ref, got_ref, mine_ref, gram_ref):
    mine = keep_ref[...] + got_ref[...].astype(F32)
    mine_ref[...] = mine
    gram = jnp.zeros((P_SIZE, P_SIZE), F32)
    for j in range(mine.shape[0]):
        gram += lax.dot_general(
            mine[j], mine[j], NT, preferred_element_type=F32, precision=lax.Precision.HIGHEST
        )
    gram = jnp.concatenate([gram[8 * i : 8 * i + 8] for i in range(P_SIZE // 8)], axis=1)
    for i in range(gram_ref.shape[0]):
        gram_ref[i] = gram


def last_kernel(factor, gram_ref, mine_ref, out_ref):
    total = jnp.sum(gram_ref[...], axis=0)
    gram = jnp.concatenate([total[:, P_SIZE * i : P_SIZE * (i + 1)] for i in range(P_SIZE // 8)], axis=0)
    row = lax.broadcasted_iota(jnp.int32, (P_SIZE, P_SIZE), 0)
    col = lax.broadcasted_iota(jnp.int32, (P_SIZE, P_SIZE), 1)
    eye = jnp.where(row == col, 1.0, 0.0).astype(F32)
    scale = jnp.sum(gram * eye, keepdims=True) + 1e-06

    def dot(a, b):
        return jnp.dot(a, b, preferred_element_type=F32, precision=lax.Precision.HIGHEST)

    current = gram / scale
    inverse = eye
    for _ in range(NSTEPS):
        weight = 1.5 * eye - 0.5 * dot(inverse, current)
        current = dot(current, weight)
        inverse = dot(weight, inverse)
    inverse = inverse * (factor / jnp.sqrt(scale))
    for j in range(mine_ref.shape[0]):
        out_ref[j] = lax.dot_general(
            inverse,
            mine_ref[j],
            (((0,), (0,)), ((), ())),
            preferred_element_type=F32,
            precision=lax.Precision.HIGHEST,
        )


def vmem(n):
    return [pl.BlockSpec(memory_space=pltpu.VMEM)] * n


def shards(damping, block_seeds, n_row, n_col):
    cols, local, m = damping.shape
    n_blocks = block_seeds.shape[0]
    n_freq = local * n_row
    channels = 2 * local
    n_dev = n_row * n_col
    amp = math.sqrt(2.0 / n_freq) / math.sqrt(n_blocks * m)
    most, large, params = (pltpu.CompilerParams(vmem_limit_bytes=x << 20) for x in (54, 40, 20))

    block_c = 256 if cols % 256 == 0 else cols
    lanes_c = 128 if block_c % 128 == 0 else block_c
    lane_w = 128 if m % 128 == 0 else m
    per_pass = 2 if m % (2 * lane_w) == 0 else 1
    flat = damping.reshape(cols * local, m)

    freqs = np.arange(n_freq)
    steps = np.arange(n_blocks)
    w_all = channel_table(n_freq, freqs, steps, n_blocks)
    sign = np.array([1.0, -1.0])[None, :, None]
    back_all = channel_table(n_freq, freqs, steps + 1, n_blocks) * sign * amp
    back_row = back_all.reshape(n_row, channels, n_blocks).transpose(0, 2, 1)

    def by_channel(table):
        table = table.reshape(n_row, local, 2, n_blocks)
        return table.transpose(0, 2, 1, 3).reshape(n_row, channels, n_blocks)

    w_row = by_channel(w_all)
    w_parts = np.concatenate([x.astype(np.float32) for x in high_low(w_row)], axis=1)

    k_parts = np.concatenate([x.astype(np.float32) for x in high_low(back_row)], axis=1)
    per_owner, half, quarter = n_blocks // n_row, n_blocks // 2, n_row // 4
    group = 16
    n_rows = P_SIZE * channels
    whole = lambda *s: pl.BlockSpec(s, lambda i: (0,) * len(s))
    v_one = pl.BlockSpec(memory_space=pltpu.VMEM)
    work = 2 * cols * local * m
    t = pl.pallas_call(
        lambda *refs: forward_kernel(local, *refs),
        out_shape=jax.ShapeDtypeStruct((P_SIZE, channels, m), BF16),
        in_specs=[pl.BlockSpec(memory_space=pltpu.SMEM)] + [pl.BlockSpec(memory_space=pltpu.HBM)] * 2,
        out_specs=v_one,
        scratch_shapes=[
            pltpu.VMEM((cols // block_c, block_c * local, m), BF16),
            pltpu.VMEM((2, per_pass, block_c * local, lane_w), F32),
            pltpu.VMEM((m // lane_w, P_SIZE // 4, 8 * local, lane_w), F32),
            pltpu.VMEM((P_SIZE * n_blocks, block_c), BF16),
            pltpu.VMEM((P_SIZE, n_blocks, lanes_c), F32),
            pltpu.VMEM((2, channels * 8, 8 * n_blocks), BF16),
            pltpu.VMEM((channels, P_SIZE, block_c), F32),
            pltpu.VMEM((2 * channels, n_blocks), F32),
            pltpu.SemaphoreType.DMA((cols // block_c,)),
            pltpu.SemaphoreType.DMA,
        ],
        compiler_params=large,
        cost_estimate=pl.CostEstimate(flops=64 * work, bytes_accessed=work, transcendentals=0),
        name="forward",
    )(block_seeds, jnp.asarray(w_parts), flat)
    t, flat = lax.optimization_barrier((t, flat))
    block_s = 128 if cols % 128 == 0 else cols
    k_shape = (n_blocks * group, channels * group)
    by_freq, k_hi, k_lo = pl.pallas_call(
        lambda *refs: separate_kernel(local, n_row, group, *refs),
        grid=(cols // block_s,),
        out_shape=(
            jax.ShapeDtypeStruct((local, m, cols), BF16),
            jax.ShapeDtypeStruct(k_shape, BF16),
            jax.ShapeDtypeStruct(k_shape, BF16),
        ),
        in_specs=[pl.BlockSpec((block_s * local, m), lambda i: (i, 0)), whole(*k_parts.shape)],
        out_specs=(pl.BlockSpec((local, m, block_s), lambda i: (0, 0, i)), whole(*k_shape), whole(*k_shape)),
        scratch_shapes=[pltpu.VMEM((2, block_s * local, lane_w), F32)],
        compiler_params=most,
        cost_estimate=pl.CostEstimate(flops=work, bytes_accessed=2 * work, transcendentals=0),
        name="separate",
    )(flat, jnp.asarray(k_parts))

    n_grp = n_dev // 2
    n_p = math.gcd(P_SIZE, n_grp)
    n_r = n_grp // n_p
    p_own, lanes = P_SIZE // n_p, m // n_r
    halves = [list(range(n_grp)), list(range(n_grp, n_dev))]
    across = [(i, (i + n_row // 2) % n_row) for i in range(n_row)]
    t = t.reshape(n_p, p_own * channels, n_r, lanes).transpose(0, 2, 1, 3)
    t = t.reshape(n_grp, p_own * channels, lanes)
    t = lax.all_to_all(t, ("row", "col"), 0, 0, axis_index_groups=halves, tiled=True)
    t = t.reshape(n_grp, p_own, channels, lanes)

    merge = by_channel(w_all * sign * amp).reshape(2, n_row // 2, 1, channels, n_blocks).repeat(n_col, axis=2)
    merge = merge.reshape(2, n_grp * channels, n_blocks).transpose(0, 2, 1)
    merge = np.concatenate(high_low(merge), axis=1)
    b_hi, b_lo = high_low(w_row.reshape(2, n_row // 2 * channels, n_blocks))
    fan = np.concatenate([b_hi, b_hi, b_lo], axis=2)
    keep, send = pl.pallas_call(
        lambda *refs: gather_kernel(n_row, *refs),
        out_shape=(
            jax.ShapeDtypeStruct((p_own, n_blocks, lanes), F32),
            jax.ShapeDtypeStruct((p_own, n_blocks, lanes), BF16),
        ),
        in_specs=vmem(2),
        out_specs=tuple(vmem(2)),
        compiler_params=params,
        name="gather",
    )(jnp.asarray(merge), t)
    got = lax.ppermute(send, "row", across)
    f = pl.pallas_call(
        lambda *refs: scatter_kernel(n_row, *refs),
        out_shape=jax.ShapeDtypeStruct((n_row // 2, n_col, p_own, channels, lanes), BF16),
        in_specs=vmem(3),
        out_specs=v_one,
        compiler_params=params,
        name="scatter",
    )(jnp.asarray(fan), keep, got)
    f = f.reshape(n_grp, p_own * channels, lanes)
    f = lax.all_to_all(f, ("row", "col"), 0, 0, axis_index_groups=halves, tiled=True)
    f = f.reshape(n_p, n_r, p_own * channels, lanes).transpose(0, 2, 1, 3).reshape(n_rows, m)

    keep, send = pl.pallas_call(
        lambda *refs: backward_kernel(local, *refs),
        out_shape=(
            jax.ShapeDtypeStruct((half, P_SIZE, cols), F32),
            jax.ShapeDtypeStruct((half, P_SIZE, cols), BF16),
        ),
        in_specs=vmem(3) + [pl.BlockSpec(memory_space=pl.ANY)],
        out_specs=tuple(vmem(2)),
        scratch_shapes=[
            pltpu.VMEM((cols // block_s, local, m, block_s), BF16),
            pltpu.VMEM((local, 2 * P_SIZE, m), BF16),
            pltpu.SemaphoreType.DMA((cols // block_s,)),
        ],
        compiler_params=large,
        cost_estimate=pl.CostEstimate(flops=64 * work, bytes_accessed=work, transcendentals=0),
        name="backward",
    )(k_hi, k_lo, f, by_freq)
    got = lax.ppermute(send, "row", [(i, i ^ 1) for i in range(n_row)])
    summed = (keep + got.astype(F32)).astype(BF16)
    groups = [[core + 2 * (i + quarter * h) for i in range(quarter)] for h in range(2) for core in range(2)]
    summed = lax.all_to_all(summed, "row", 0, 0, axis_index_groups=groups, tiled=True)
    summed = summed.reshape(quarter, 2, per_owner, P_SIZE, cols)
    keep, send = pl.pallas_call(
        join_kernel,
        out_shape=(
            jax.ShapeDtypeStruct((per_owner, P_SIZE, cols), F32),
            jax.ShapeDtypeStruct((per_owner, P_SIZE, cols), BF16),
        ),
        in_specs=vmem(1),
        out_specs=tuple(vmem(2)),
        compiler_params=params,
        name="join",
    )(summed)
    got = lax.ppermute(send, "row", across)

    mine, gram = pl.pallas_call(
        gram_kernel,
        out_shape=(
            jax.ShapeDtypeStruct((per_owner, P_SIZE, cols), F32),
            jax.ShapeDtypeStruct((n_dev, 8, 4 * P_SIZE), F32),
        ),
        in_specs=vmem(2),
        out_specs=tuple(vmem(2)),
        compiler_params=params,
        name="gram",
    )(keep, got)
    gram = lax.all_to_all(gram, ("row", "col"), 0, 0, tiled=True)
    out = pl.pallas_call(
        lambda *refs: last_kernel(math.sqrt(n_blocks * m), *refs),
        out_shape=jax.ShapeDtypeStruct((per_owner, P_SIZE, cols), F32),
        in_specs=vmem(2),
        out_specs=vmem(1)[0],
        compiler_params=params,
        name="last",
    )(gram, mine)
    return out.transpose(0, 2, 1)


def solution(mesh):
    n_row, n_col = mesh.shape["row"], mesh.shape["col"]
    return jax.shard_map(
        lambda damping, block_seeds: shards(damping, block_seeds, n_row, n_col),
        mesh=mesh,
        in_specs=(P("col", "row", None), P()),
        out_specs=P("row", "col", None),
        check_vma=False,
    )
```

```python
import math

import numpy as np
import jax
import jax.numpy as jnp
from jax import lax
from jax.experimental import pallas as pl
from jax.experimental.pallas import tpu as pltpu
from jax.sharding import PartitionSpec as P

NSTEPS = 12
PRIME = 65521
P_SIZE = 32
BF16 = jnp.bfloat16
F32 = jnp.float32
NT = (((1,), (1,)), ((), ()))


def channel_table(n_freq, freqs, steps, n_blocks):
    angle = math.pi * (np.asarray(freqs)[:, None] + 0.5) / n_freq * np.asarray(steps)[None, :]
    decay = 3.0 ** (-np.asarray(steps) / n_blocks)
    return np.stack([decay * np.cos(angle), decay * np.sin(angle)], axis=1)


def high_low(values):
    high = values.astype(np.float32).astype(jnp.bfloat16)
    low = (values - high.astype(np.float64)).astype(np.float32).astype(jnp.bfloat16)
    return high, low


def _fit(fn, degree):
    nodes = np.cos(np.pi * (np.arange(64) + 0.5) / 64)
    u = (nodes + 1.0) / 128
    series = np.polynomial.chebyshev.Chebyshev.fit(u, fn(np.sqrt(u)), degree, domain=[0.0, 1 / 64])
    return [float(x) for x in series.convert(kind=np.polynomial.Polynomial, domain=[-1, 1], window=[-1, 1]).coef]


COS_COEFS = _fit(lambda t: np.cos(2 * np.pi * t), 5)
SIN_COEFS = _fit(lambda t: np.sin(2 * np.pi * t) / t, 5)


def polynomial(coefs, u):
    out = jnp.full_like(u, coefs[-1])
    for coef in coefs[-2::-1]:
        out = out * u + coef
    return out


def cos_sin(turns):
    quarter = jnp.round(turns * 4.0)
    rest = turns - quarter * 0.25
    u = rest * rest
    cos, sin = polynomial(COS_COEFS, u), polynomial(SIN_COEFS, u) * rest
    odd = jnp.abs(quarter) == 1.0
    far = jnp.abs(quarter) == 2.0
    flip_cos = jnp.logical_or(quarter == 1.0, far)
    flip_sin = jnp.logical_or(quarter == -1.0, far)
    out_cos, out_sin = jnp.where(odd, sin, cos), jnp.where(odd, cos, sin)
    return jnp.where(flip_cos, -out_cos, out_cos), jnp.where(flip_sin, -out_sin, out_sin)


def mod_turns(x):
    return (x - jnp.round(x * (1.0 / PRIME)) * float(PRIME)) * (1.0 / PRIME)


def channel_values(n_freq, n_blocks, freq, step, sine):
    turns = ((2 * freq + 1) * step % (4 * n_freq)).astype(F32) * (0.25 / n_freq)
    cos, sin = cos_sin(turns - jnp.round(turns))
    values = jnp.where(sine, sin, cos) * jnp.exp(step.astype(F32) * (-math.log(3.0) / n_blocks))
    return values


def split(values):
    high = values.astype(BF16).astype(F32)
    return high, values - high


def iotas(rows, cols):
    return (lax.broadcasted_iota(jnp.int32, (rows, cols), d) for d in range(2))


def place(rows, cols, test):
    r = lax.broadcasted_iota(jnp.int32, (rows, cols), 0)
    c = lax.broadcasted_iota(jnp.int32, (rows, cols), 1)
    return test(r, c).astype(F32)


def less_turns(x):
    return x - (x.astype(F32) * (1.0 / PRIME)).astype(jnp.int32) * PRIME


def forward_kernel(local, n_freq, seeds_ref, d_ref, t_ref, held, wide, acc, probes, cos_shift, sin_shift, state, spread, q_all, own, sems, sem):
    n_chunks, rows, m = held.shape
    block_c = rows // local
    channels = 2 * local
    n_blocks, lanes = cos_shift.shape[1:]
    group = 8
    tiles = P_SIZE // 8
    per_pass, lane_w = wide.shape[1], wide.shape[3]
    passes = m // (per_pass * lane_w)

    width = per_pass * lane_w

    def copy(b, i):
        part = (slice(b * rows, (b + 1) * rows), slice(i * width, (i + 1) * width))
        return pltpu.make_async_copy(d_ref.at[part], held.at[b, :, part[1]], sems.at[b, i])

    fetch = pltpu.make_async_copy(seeds_ref, own, sem)
    fetch.start()
    for b in range(n_chunks):
        for i in range(passes):
            copy(b, i).start()

    row, col = iotas(channels, n_blocks)
    table = channel_values(n_freq, n_blocks, lax.axis_index("row") * local + row % local, col, row >= local)
    left = place(channels * group, channels, lambda r, c: r // group == c)
    right = place(n_blocks, group * n_blocks, lambda r, c: r == c % n_blocks)
    same = place(channels * group, group * n_blocks, lambda r, c: r % group == c // n_blocks)
    for part, w in enumerate(split(table)):
        w = jnp.dot(w, right, preferred_element_type=F32)
        spread[part] = (jnp.dot(left, w, preferred_element_type=F32) * same).astype(BF16)

    fetch.wait()
    line, lane = iotas(n_blocks, lanes)
    seeds = jnp.zeros((n_blocks, lanes), jnp.int32)
    for j in range(n_blocks):
        seeds = jnp.where(line == j, own[j], seeds)
    steps = (lane + 1).astype(F32)
    shift = mod_turns(seeds.astype(F32) * steps) * float(PRIME)
    shift_parts = cos_sin(mod_turns(jnp.round(shift) * (steps + 1.0)))
    for p in range(P_SIZE):
        for part, out in zip(shift_parts, (cos_shift, sin_shift)):
            out[p] = jnp.broadcast_to(part[:, p : p + 1], (n_blocks, lanes))

    start = lax.axis_index("col") * (n_chunks * block_c)
    spans = [(at, p) for at in range(0, block_c, lanes) for p in range(0, P_SIZE, 8)]

    def make_probes(b, span):
        at, first = span
        if first == 0:
            column = start + b * block_c + at + lane
            inner = less_turns(less_turns(seeds * (column + 1)) * (column + 3)).astype(F32)
            turn_cos, turn_sin = cos_sin(mod_turns(inner))
            cos, sin = turn_cos, turn_sin
        else:
            cos, sin, turn_cos, turn_sin = (state[i] for i in range(4))
        for p in range(first, first + 8):
            value = cos * cos_shift[p] - sin * sin_shift[p]
            probes[p * n_blocks : (p + 1) * n_blocks, at : at + lanes] = value.astype(BF16)
            cos, sin = cos * turn_cos - sin * turn_sin, sin * turn_cos + cos * turn_sin
        for i, x in enumerate((cos, sin, turn_cos, turn_sin)):
            state[i] = x

    def make_channels(b):
        for g in range(P_SIZE // group):
            block = probes[g * group * n_blocks : (g + 1) * group * n_blocks, :]
            q = jnp.dot(spread[0], block, preferred_element_type=F32) + jnp.dot(
                spread[1], block, preferred_element_type=F32
            )
            q = q.astype(BF16)
            for part in range(2):
                for k in range(local):
                    at = (part * local + k) * group
                    to = part * P_SIZE + g * group
                    q_all[b % 2, k, to : to + group, :] = q[at : at + group]

    for span in spans:
        make_probes(0, span)
    make_channels(0)
    for b in range(n_chunks):
        for i in range(passes):
            copy(b, i).wait()
            if b + 1 < n_chunks:
                for span in spans[len(spans) * i // passes : len(spans) * (i + 1) // passes]:
                    make_probes(b + 1, span)
            for l in range(per_pass):
                at = (i * per_pass + l) * lane_w
                wide[i % 2, l] = held[b, :, at : at + lane_w].astype(F32)
            for k in range(local):
                s = jnp.concatenate(
                    [wide[i % 2, l, pl.ds(k, block_c, stride=local), :] for l in range(per_pass)], axis=1
                ).astype(BF16)
                o = jnp.dot(q_all[b % 2, k], s, preferred_element_type=F32)
                for l in range(per_pass):
                    for t in range(2 * tiles):
                        piece = o[t * 8 : t * 8 + 8, l * lane_w : (l + 1) * lane_w]
                        if b > 0:
                            piece += acc[i * per_pass + l, t, k * 8 : k * 8 + 8, :]
                        acc[i * per_pass + l, t, k * 8 : k * 8 + 8, :] = piece
            if b + 1 == n_chunks:
                for l in range(i * per_pass, (i + 1) * per_pass):
                    for p in range(P_SIZE):
                        t = jnp.concatenate(
                            [acc[l, part * tiles + p // 8, pl.ds(p % 8, local, stride=8), :] for part in range(2)],
                            axis=0,
                        )
                        t_ref[p, :, l * lane_w : (l + 1) * lane_w] = t.astype(BF16)
        if b + 1 < n_chunks:
            make_channels(b + 1)


def separate_kernel(local, d_ref, o_ref, wide):
    rows, m = d_ref.shape
    lane_w = wide.shape[-1]
    for l in range(m // lane_w):
        at = slice(l * lane_w, (l + 1) * lane_w)
        wide[l % 2] = d_ref[:, at].astype(F32)
        for k in range(local):
            o_ref[k, at, :] = wide[l % 2, pl.ds(k, rows // local, stride=local), :].T.astype(BF16)


def half_of(n_row):
    return lax.axis_index("row") // (n_row // 2)


def gather_kernel(n_row, c_ref, x_ref, keep_ref, send_ref):
    n_src, p_own, channels, lanes = x_ref.shape
    table = c_ref[half_of(n_row)]
    n = table.shape[0] // 2
    for p in range(p_own):
        x = x_ref[:, p].reshape(n_src * channels, lanes)
        both = jnp.dot(table, x, preferred_element_type=F32)
        out = both[:n] + both[n:]
        keep_ref[p] = out
        send_ref[p] = out.astype(BF16)


def scatter_kernel(n_row, b_ref, keep_ref, got_ref, f_ref):
    n_rows, n_cols, p_own, channels, lanes = f_ref.shape
    table = b_ref[half_of(n_row)]
    for p in range(p_own):
        forward = keep_ref[p] + got_ref[p].astype(F32)
        high = forward.astype(BF16)
        low = (forward - high.astype(F32)).astype(BF16)
        out = jnp.dot(table, jnp.concatenate([high, low, high], axis=0), preferred_element_type=F32)
        out = out.astype(BF16).reshape(n_rows, channels, lanes)
        for col in range(n_cols):
            f_ref[:, col, p] = out


def join_kernel(x_ref, keep_ref, send_ref):
    x = x_ref[...].astype(F32)
    total = jnp.sum(x, axis=0)
    keep_ref[...] = total[0]
    send_ref[...] = total[1].astype(BF16)


def backward_kernel(local, n_row, n_blocks, amp, f_ref, d_ref, keep_ref, send_ref, held, f_by, k_parts, sems):
    n_chunks, _, m, block_c = held.shape
    rows = f_ref.shape[0] // 4
    channels = 2 * local

    def copy(b):
        at = pl.ds(pl.multiple_of(b * block_c, block_c), block_c) if n_chunks > 1 else slice(None)
        return pltpu.make_async_copy(d_ref.at[:, :, at], held.at[b], sems.at[b])

    for b in range(n_chunks):
        copy(b).start()

    row_at = lax.axis_index("row")
    half, per_owner, quarter = n_blocks // 2, n_blocks // n_row, n_row // 4
    r, c = iotas(n_blocks, channels)
    rest = r % half
    chip = rest // (2 * per_owner) + quarter * ((rest // per_owner + half_of(n_row)) % 2)
    block_at = (2 * chip + (r // half + row_at) % 2) * per_owner + rest % per_owner
    sine = c % 2 == 1
    table = channel_values(local * n_row, n_blocks, row_at * local + c // 2, block_at + 1, sine)
    table = table * jnp.where(sine, -amp, amp)
    left = place(n_blocks * 16, n_blocks, lambda r, c: r // 16 == c)
    right = place(channels, channels * 16, lambda r, c: r == c // 32 * 2 + c // 8 % 2)
    same = place(n_blocks * 16, channels * 16, lambda r, c: r % 16 == c // 16 % 2 * 8 + c % 8)
    for part, k in enumerate(split(table)):
        k = jnp.dot(left, jnp.dot(k, right, preferred_element_type=F32), preferred_element_type=F32)
        k_parts[part] = (k * same).astype(BF16)

    swap = place(rows, rows, lambda r, c: (r % 8 * 2 + r // 8 % 2) * local + r // 16 == c).astype(BF16)
    for g in range(4):
        out = jnp.dot(swap, f_ref[g * rows : (g + 1) * rows, :], preferred_element_type=F32).astype(BF16)
        for k in range(local):
            f_by[k, g * 16 : g * 16 + 16, :] = out[k * 16 : k * 16 + 16]

    @pl.loop(0, n_chunks)
    def _(b):
        copy(b).wait()
        at = pl.ds(pl.multiple_of(b * block_c, block_c), block_c) if n_chunks > 1 else slice(None)
        u = [jnp.dot(f_by[k], held[b, k], preferred_element_type=F32).astype(BF16) for k in range(local)]
        for g in range(2):
            block = jnp.concatenate([x[g * 32 : g * 32 + 32] for x in u], axis=0)
            out = jnp.dot(k_parts[0], block, preferred_element_type=F32) + jnp.dot(
                k_parts[1], block, preferred_element_type=F32
            )
            out = out.reshape(2 * half, 16, block_c)
            keep_ref[:, g * 16 : g * 16 + 16, at] = out[:half]
            send_ref[:, g * 16 : g * 16 + 16, at] = out[half:].astype(BF16)


def gram_kernel(keep_ref, got_ref, mine_ref, gram_ref):
    mine = keep_ref[...] + got_ref[...].astype(F32)
    mine_ref[...] = mine
    gram = jnp.zeros((P_SIZE, P_SIZE), F32)
    for j in range(mine.shape[0]):
        gram += lax.dot_general(
            mine[j], mine[j], NT, preferred_element_type=F32, precision=lax.Precision.HIGHEST
        )
    gram = jnp.concatenate([gram[8 * i : 8 * i + 8] for i in range(P_SIZE // 8)], axis=1)
    for i in range(gram_ref.shape[0]):
        gram_ref[i] = gram


def last_kernel(factor, gram_ref, mine_ref, out_ref):
    total = jnp.sum(gram_ref[...], axis=0)
    gram = jnp.concatenate([total[:, P_SIZE * i : P_SIZE * (i + 1)] for i in range(P_SIZE // 8)], axis=0)
    row = lax.broadcasted_iota(jnp.int32, (P_SIZE, P_SIZE), 0)
    col = lax.broadcasted_iota(jnp.int32, (P_SIZE, P_SIZE), 1)
    eye = jnp.where(row == col, 1.0, 0.0).astype(F32)
    scale = jnp.sum(gram * eye, keepdims=True) + 1e-06

    def dot(a, b):
        return jnp.dot(a, b, preferred_element_type=F32, precision=lax.Precision.HIGH)

    current = gram / scale
    inverse = eye
    for _ in range(NSTEPS):
        weight = 1.5 * eye - 0.5 * dot(inverse, current)
        current = dot(current, weight)
        inverse = dot(weight, inverse)
    inverse = inverse * (factor / jnp.sqrt(scale))
    for j in range(mine_ref.shape[0]):
        out_ref[j] = lax.dot_general(
            inverse,
            mine_ref[j],
            (((0,), (0,)), ((), ())),
            preferred_element_type=F32,
            precision=lax.Precision.HIGHEST,
        )


def vmem(n):
    return [pl.BlockSpec(memory_space=pltpu.VMEM)] * n


def shards(damping, block_seeds, n_row, n_col):
    cols, local, m = damping.shape
    n_blocks = block_seeds.shape[0]
    n_freq = local * n_row
    channels = 2 * local
    n_dev = n_row * n_col
    amp = math.sqrt(2.0 / n_freq) / math.sqrt(n_blocks * m)
    most, large, params = (pltpu.CompilerParams(vmem_limit_bytes=x << 20) for x in (54, 40, 20))

    block_c = 256 if cols % 256 == 0 else cols
    lanes_c = 128 if block_c % 128 == 0 else block_c
    lane_w = 128 if m % 128 == 0 else m
    per_pass = 2 if m % (2 * lane_w) == 0 else 1
    flat = damping.reshape(cols * local, m)

    w_row = channel_table(n_freq, np.arange(n_freq), np.arange(n_blocks), n_blocks)
    w_row = w_row.reshape(n_row, local, 2, n_blocks).transpose(0, 2, 1, 3)
    sign = np.array([1.0, -1.0])[None, :, None, None] * amp
    per_owner, half, quarter = n_blocks // n_row, n_blocks // 2, n_row // 4

    n_rows = P_SIZE * channels
    whole = lambda *s: pl.BlockSpec(s, lambda i: (0,) * len(s))
    v_one = pl.BlockSpec(memory_space=pltpu.VMEM)
    work = 2 * cols * local * m
    t = pl.pallas_call(
        lambda *refs: forward_kernel(local, n_freq, *refs),
        out_shape=jax.ShapeDtypeStruct((P_SIZE, channels, m), BF16),
        in_specs=[pl.BlockSpec(memory_space=pl.ANY)] * 2,
        out_specs=v_one,
        scratch_shapes=[
            pltpu.VMEM((cols // block_c, block_c * local, m), BF16),
            pltpu.VMEM((2, per_pass, block_c * local, lane_w), F32),
            pltpu.VMEM((m // lane_w, P_SIZE // 4, 8 * local, lane_w), F32),
            pltpu.VMEM((P_SIZE * n_blocks, block_c), BF16),
            pltpu.VMEM((P_SIZE, n_blocks, lanes_c), F32),
            pltpu.VMEM((P_SIZE, n_blocks, lanes_c), F32),
            pltpu.VMEM((4, n_blocks, lanes_c), F32),
            pltpu.VMEM((2, channels * 8, 8 * n_blocks), BF16),
            pltpu.VMEM((2, local, 2 * P_SIZE, block_c), BF16),
            pltpu.SMEM((n_blocks,), jnp.int32),
            pltpu.SemaphoreType.DMA((cols // block_c, m // (per_pass * lane_w))),
            pltpu.SemaphoreType.DMA,
        ],
        compiler_params=large,
        cost_estimate=pl.CostEstimate(flops=64 * work, bytes_accessed=work, transcendentals=0),
        name="forward",
    )(block_seeds, flat)
    t, flat = lax.optimization_barrier((t, flat))
    block_s = 128 if cols % 128 == 0 else cols
    by_freq = pl.pallas_call(
        lambda *refs: separate_kernel(local, *refs),
        grid=(cols // block_s,),
        out_shape=jax.ShapeDtypeStruct((local, m, cols), BF16),
        in_specs=[pl.BlockSpec((block_s * local, m), lambda i: (i, 0))],
        out_specs=pl.BlockSpec((local, m, block_s), lambda i: (0, 0, i)),
        scratch_shapes=[pltpu.VMEM((2, block_s * local, lane_w), F32)],
        compiler_params=most,
        cost_estimate=pl.CostEstimate(flops=work, bytes_accessed=2 * work, transcendentals=0),
        name="separate",
    )(flat)

    n_grp = n_dev // 2
    n_p = math.gcd(P_SIZE, n_grp)
    n_r = n_grp // n_p
    p_own, lanes = P_SIZE // n_p, m // n_r
    halves = [list(range(n_grp)), list(range(n_grp, n_dev))]
    across = [(i, (i + n_row // 2) % n_row) for i in range(n_row)]
    t = t.reshape(n_p, p_own * channels, n_r, lanes).transpose(0, 2, 1, 3)
    t = t.reshape(n_grp, p_own * channels, lanes)
    t = lax.all_to_all(t, ("row", "col"), 0, 0, axis_index_groups=halves, tiled=True)
    t, by_freq = lax.optimization_barrier((t, by_freq))
    t = t.reshape(n_grp, p_own, channels, lanes)

    merge = (w_row * sign).reshape(2, n_row // 2, 1, channels, n_blocks).repeat(n_col, axis=2)
    merge = merge.reshape(2, n_grp * channels, n_blocks).transpose(0, 2, 1)
    merge = np.concatenate(high_low(merge), axis=1)
    b_hi, b_lo = high_low(w_row.reshape(2, n_row // 2 * channels, n_blocks))
    fan = np.concatenate([b_hi, b_hi, b_lo], axis=2)
    keep, send = pl.pallas_call(
        lambda *refs: gather_kernel(n_row, *refs),
        out_shape=(
            jax.ShapeDtypeStruct((p_own, n_blocks, lanes), F32),
            jax.ShapeDtypeStruct((p_own, n_blocks, lanes), BF16),
        ),
        in_specs=vmem(2),
        out_specs=tuple(vmem(2)),
        compiler_params=params,
        name="gather",
    )(jnp.asarray(merge), t)
    got = lax.ppermute(send, "row", across)
    f = pl.pallas_call(
        lambda *refs: scatter_kernel(n_row, *refs),
        out_shape=jax.ShapeDtypeStruct((n_row // 2, n_col, p_own, channels, lanes), BF16),
        in_specs=vmem(3),
        out_specs=v_one,
        compiler_params=params,
        name="scatter",
    )(jnp.asarray(fan), keep, got)
    f = f.reshape(n_grp, p_own * channels, lanes)
    f = lax.all_to_all(f, ("row", "col"), 0, 0, axis_index_groups=halves, tiled=True)
    f = f.reshape(n_p, n_r, p_own * channels, lanes).transpose(0, 2, 1, 3).reshape(n_rows, m)

    keep, send = pl.pallas_call(
        lambda *refs: backward_kernel(local, n_row, n_blocks, amp, *refs),
        out_shape=(
            jax.ShapeDtypeStruct((half, P_SIZE, cols), F32),
            jax.ShapeDtypeStruct((half, P_SIZE, cols), BF16),
        ),
        in_specs=vmem(1) + [pl.BlockSpec(memory_space=pl.ANY)],
        out_specs=tuple(vmem(2)),
        scratch_shapes=[
            pltpu.VMEM((cols // block_s, local, m, block_s), BF16),
            pltpu.VMEM((local, 2 * P_SIZE, m), BF16),
            pltpu.VMEM((2, n_blocks * 16, channels * 16), BF16),
            pltpu.SemaphoreType.DMA((cols // block_s,)),
        ],
        compiler_params=large,
        cost_estimate=pl.CostEstimate(flops=64 * work, bytes_accessed=work, transcendentals=0),
        name="backward",
    )(f, by_freq)
    got = lax.ppermute(send, "row", [(i, i ^ 1) for i in range(n_row)])
    summed = (keep + got.astype(F32)).astype(BF16)
    groups = [[core + 2 * (i + quarter * h) for i in range(quarter)] for h in range(2) for core in range(2)]
    summed = lax.all_to_all(summed, "row", 0, 0, axis_index_groups=groups, tiled=True)
    summed = summed.reshape(quarter, 2, per_owner, P_SIZE, cols)
    keep, send = pl.pallas_call(
        join_kernel,
        out_shape=(
            jax.ShapeDtypeStruct((per_owner, P_SIZE, cols), F32),
            jax.ShapeDtypeStruct((per_owner, P_SIZE, cols), BF16),
        ),
        in_specs=vmem(1),
        out_specs=tuple(vmem(2)),
        compiler_params=params,
        name="join",
    )(summed)
    got = lax.ppermute(send, "row", across)

    mine, gram = pl.pallas_call(
        gram_kernel,
        out_shape=(
            jax.ShapeDtypeStruct((per_owner, P_SIZE, cols), F32),
            jax.ShapeDtypeStruct((n_dev, 8, 4 * P_SIZE), F32),
        ),
        in_specs=vmem(2),
        out_specs=tuple(vmem(2)),
        compiler_params=params,
        name="gram",
    )(keep, got)
    gram = lax.all_to_all(gram, ("row", "col"), 0, 0, tiled=True)
    out = pl.pallas_call(
        lambda *refs: last_kernel(math.sqrt(n_blocks * m), *refs),
        out_shape=jax.ShapeDtypeStruct((per_owner, P_SIZE, cols), F32),
        in_specs=vmem(2),
        out_specs=vmem(1)[0],
        compiler_params=params,
        name="last",
    )(gram, mine)
    return out.transpose(0, 2, 1)


def solution(mesh):
    n_row, n_col = mesh.shape["row"], mesh.shape["col"]
    return jax.shard_map(
        lambda damping, block_seeds: shards(damping, block_seeds, n_row, n_col),
        mesh=mesh,
        in_specs=(P("col", "row", None), P()),
        out_specs=P("row", "col", None),
        check_vma=False,
    )
```

```python
import math

import numpy as np
import jax
import jax.numpy as jnp
from jax import lax
from jax.experimental import pallas as pl
from jax.experimental.pallas import tpu as pltpu
from jax.sharding import PartitionSpec as P

NSTEPS = 12
PRIME = 65521
P_SIZE = 32
BF16 = jnp.bfloat16
F32 = jnp.float32
NT = (((1,), (1,)), ((), ()))


def channel_table(n_freq, freqs, steps, n_blocks):
    angle = math.pi * (np.asarray(freqs)[:, None] + 0.5) / n_freq * np.asarray(steps)[None, :]
    decay = 3.0 ** (-np.asarray(steps) / n_blocks)
    return np.stack([decay * np.cos(angle), decay * np.sin(angle)], axis=1)


def high_low(values):
    high = values.astype(np.float32).astype(jnp.bfloat16)
    low = (values - high.astype(np.float64)).astype(np.float32).astype(jnp.bfloat16)
    return high, low


def _fit(fn, degree):
    nodes = np.cos(np.pi * (np.arange(64) + 0.5) / 64)
    u = (nodes + 1.0) / 128
    series = np.polynomial.chebyshev.Chebyshev.fit(u, fn(np.sqrt(u)), degree, domain=[0.0, 1 / 64])
    return [float(x) for x in series.convert(kind=np.polynomial.Polynomial, domain=[-1, 1], window=[-1, 1]).coef]


COS_COEFS = _fit(lambda t: np.cos(2 * np.pi * t), 5)
SIN_COEFS = _fit(lambda t: np.sin(2 * np.pi * t) / t, 5)


def polynomial(coefs, u):
    out = jnp.full_like(u, coefs[-1])
    for coef in coefs[-2::-1]:
        out = out * u + coef
    return out


def cos_sin(turns):
    quarter = jnp.round(turns * 4.0)
    rest = turns - quarter * 0.25
    u = rest * rest
    cos, sin = polynomial(COS_COEFS, u), polynomial(SIN_COEFS, u) * rest
    odd = jnp.abs(quarter) == 1.0
    far = jnp.abs(quarter) == 2.0
    flip_cos = jnp.logical_or(quarter == 1.0, far)
    flip_sin = jnp.logical_or(quarter == -1.0, far)
    out_cos, out_sin = jnp.where(odd, sin, cos), jnp.where(odd, cos, sin)
    return jnp.where(flip_cos, -out_cos, out_cos), jnp.where(flip_sin, -out_sin, out_sin)


def mod_turns(x):
    return (x - jnp.round(x * (1.0 / PRIME)) * float(PRIME)) * (1.0 / PRIME)


def channel_values(n_freq, n_blocks, freq, step, sine):
    turns = ((2 * freq + 1) * step % (4 * n_freq)).astype(F32) * (0.25 / n_freq)
    cos, sin = cos_sin(turns - jnp.round(turns))
    values = jnp.where(sine, sin, cos) * jnp.exp(step.astype(F32) * (-math.log(3.0) / n_blocks))
    return values


def split(values):
    high = values.astype(BF16).astype(F32)
    return high, values - high


def separate(x, local):
    return jnp.swapaxes(x.reshape(x.shape[0] // local, local, x.shape[1]), 0, 1)


def iotas(rows, cols):
    return (lax.broadcasted_iota(jnp.int32, (rows, cols), d) for d in range(2))


def place(rows, cols, test):
    r = lax.broadcasted_iota(jnp.int32, (rows, cols), 0)
    c = lax.broadcasted_iota(jnp.int32, (rows, cols), 1)
    return test(r, c).astype(F32)


def less_turns(x):
    return x - (x.astype(F32) * (1.0 / PRIME)).astype(jnp.int32) * PRIME


def forward_kernel(local, n_freq, seeds_ref, d_ref, t_ref, held, by_freq, acc, probes, cos_shift, sin_shift, state, spread, q_all, own, sems, sem):
    n_chunks, rows, m = held.shape
    block_c = rows // local
    channels = 2 * local
    n_blocks, lanes = cos_shift.shape[1:]
    group = 8
    tiles = P_SIZE // 8
    width, lane_w = by_freq.shape[3], acc.shape[3]
    passes, per_pass = m // width, width // lane_w

    def copy(b, i):
        part = (slice(b * rows, (b + 1) * rows), slice(i * width, (i + 1) * width))
        return pltpu.make_async_copy(d_ref.at[part], held.at[b, :, part[1]], sems.at[b, i])

    fetch = pltpu.make_async_copy(seeds_ref, own, sem)
    fetch.start()
    for b in range(n_chunks):
        for i in range(passes):
            copy(b, i).start()

    row, col = iotas(channels, n_blocks)
    table = channel_values(n_freq, n_blocks, lax.axis_index("row") * local + row % local, col, row >= local)
    left = place(channels * group, channels, lambda r, c: r // group == c)
    right = place(n_blocks, group * n_blocks, lambda r, c: r == c % n_blocks)
    same = place(channels * group, group * n_blocks, lambda r, c: r % group == c // n_blocks)
    for part, w in enumerate(split(table)):
        w = jnp.dot(w, right, preferred_element_type=F32)
        spread[part] = (jnp.dot(left, w, preferred_element_type=F32) * same).astype(BF16)

    fetch.wait()
    line, lane = iotas(n_blocks, lanes)
    seeds = jnp.zeros((n_blocks, lanes), jnp.int32)
    for j in range(n_blocks):
        seeds = jnp.where(line == j, own[j], seeds)
    steps = (lane + 1).astype(F32)
    shift = mod_turns(seeds.astype(F32) * steps) * float(PRIME)
    shift_parts = cos_sin(mod_turns(jnp.round(shift) * (steps + 1.0)))
    for p in range(P_SIZE):
        for part, out in zip(shift_parts, (cos_shift, sin_shift)):
            out[p] = jnp.broadcast_to(part[:, p : p + 1], (n_blocks, lanes))

    start = lax.axis_index("col") * (n_chunks * block_c)
    spans = [(at, p) for at in range(0, block_c, lanes) for p in range(0, P_SIZE, 8)]

    def make_probes(b, span):
        at, first = span
        if first == 0:
            column = start + b * block_c + at + lane
            inner = less_turns(less_turns(seeds * (column + 1)) * (column + 3)).astype(F32)
            turn_cos, turn_sin = cos_sin(mod_turns(inner))
            cos, sin = turn_cos, turn_sin
        else:
            cos, sin, turn_cos, turn_sin = (state[i] for i in range(4))
        for p in range(first, first + 8):
            value = cos * cos_shift[p] - sin * sin_shift[p]
            probes[p * n_blocks : (p + 1) * n_blocks, at : at + lanes] = value.astype(BF16)
            cos, sin = cos * turn_cos - sin * turn_sin, sin * turn_cos + cos * turn_sin
        for i, x in enumerate((cos, sin, turn_cos, turn_sin)):
            state[i] = x

    def make_channels(b):
        for g in range(P_SIZE // group):
            block = probes[g * group * n_blocks : (g + 1) * group * n_blocks, :]
            q = jnp.dot(spread[0], block, preferred_element_type=F32) + jnp.dot(
                spread[1], block, preferred_element_type=F32
            )
            q = q.astype(BF16)
            for part in range(2):
                for k in range(local):
                    at = (part * local + k) * group
                    to = part * P_SIZE + g * group
                    q_all[b % 2, k, to : to + group, :] = q[at : at + group]

    for span in spans:
        make_probes(0, span)
    make_channels(0)
    for b in range(n_chunks):
        for i in range(passes):
            copy(b, i).wait()
            if b + 1 < n_chunks:
                for span in spans[len(spans) * i // passes : len(spans) * (i + 1) // passes]:
                    make_probes(b + 1, span)
            at = slice(i * width, (i + 1) * width)
            for c in range(0, block_c, 16):
                by_freq[i % 2, :, c : c + 16, :] = separate(held[b, c * local : (c + 16) * local, at], local)
            for k in range(local):
                o = jnp.dot(q_all[b % 2, k], by_freq[i % 2, k], preferred_element_type=F32)
                for l in range(per_pass):
                    for t in range(2 * tiles):
                        piece = o[t * 8 : t * 8 + 8, l * lane_w : (l + 1) * lane_w]
                        if b > 0:
                            piece += acc[i * per_pass + l, t, k * 8 : k * 8 + 8, :]
                        acc[i * per_pass + l, t, k * 8 : k * 8 + 8, :] = piece
            if b + 1 == n_chunks:
                for l in range(i * per_pass, (i + 1) * per_pass):
                    for p in range(P_SIZE):
                        t = jnp.concatenate(
                            [acc[l, part * tiles + p // 8, pl.ds(p % 8, local, stride=8), :] for part in range(2)],
                            axis=0,
                        )
                        t_ref[p, :, l * lane_w : (l + 1) * lane_w] = t.astype(BF16)
        if b + 1 < n_chunks:
            make_channels(b + 1)


def separate_kernel(local, d_ref, o_ref):
    rows, m = d_ref.shape
    width = 256 if m % 256 == 0 else m
    for i in range(0, m, width):
        parts = [
            separate(d_ref[c : c + 16 * local, i : i + width], local) for c in range(0, rows, 16 * local)
        ]
        for k in range(local):
            o_ref[k, i : i + width, :] = jnp.concatenate([x[k] for x in parts], axis=0).T


def half_of(n_row):
    return lax.axis_index("row") // (n_row // 2)


def gather_kernel(n_row, c_ref, x_ref, keep_ref, send_ref):
    n_src, p_own, channels, lanes = x_ref.shape
    table = c_ref[half_of(n_row)]
    n = table.shape[0] // 2
    for p in range(p_own):
        x = x_ref[:, p].reshape(n_src * channels, lanes)
        both = jnp.dot(table, x, preferred_element_type=F32)
        out = both[:n] + both[n:]
        keep_ref[p] = out
        send_ref[p] = out.astype(BF16)


def scatter_kernel(n_row, b_ref, keep_ref, got_ref, f_ref):
    n_rows, n_cols, p_own, channels, lanes = f_ref.shape
    table = b_ref[half_of(n_row)]
    for p in range(p_own):
        forward = keep_ref[p] + got_ref[p].astype(F32)
        high = forward.astype(BF16)
        low = (forward - high.astype(F32)).astype(BF16)
        out = jnp.dot(table, jnp.concatenate([high, low, high], axis=0), preferred_element_type=F32)
        out = out.astype(BF16).reshape(n_rows, channels, lanes)
        for col in range(n_cols):
            f_ref[:, col, p] = out


def join_kernel(x_ref, keep_ref, send_ref):
    x = x_ref[...].astype(F32)
    total = jnp.sum(x, axis=0)
    keep_ref[...] = total[0]
    send_ref[...] = total[1].astype(BF16)


def backward_kernel(local, n_row, n_blocks, amp, f_ref, d_ref, keep_ref, send_ref, held, f_by, k_parts, sems):
    n_chunks, _, m, block_c = held.shape
    rows = f_ref.shape[0] // 4
    channels = 2 * local

    def copy(b):
        at = pl.ds(pl.multiple_of(b * block_c, block_c), block_c) if n_chunks > 1 else slice(None)
        return pltpu.make_async_copy(d_ref.at[:, :, at], held.at[b], sems.at[b])

    for b in range(n_chunks):
        copy(b).start()

    row_at = lax.axis_index("row")
    half, per_owner, quarter = n_blocks // 2, n_blocks // n_row, n_row // 4
    r, c = iotas(n_blocks, channels)
    rest = r % half
    chip = rest // (2 * per_owner) + quarter * ((rest // per_owner + half_of(n_row)) % 2)
    block_at = (2 * chip + (r // half + row_at) % 2) * per_owner + rest % per_owner
    sine = c % 2 == 1
    table = channel_values(local * n_row, n_blocks, row_at * local + c // 2, block_at + 1, sine)
    table = table * jnp.where(sine, -amp, amp)
    left = place(n_blocks * 16, n_blocks, lambda r, c: r // 16 == c)
    right = place(channels, channels * 16, lambda r, c: r == c // 32 * 2 + c // 8 % 2)
    same = place(n_blocks * 16, channels * 16, lambda r, c: r % 16 == c // 16 % 2 * 8 + c % 8)
    for part, k in enumerate(split(table)):
        k = jnp.dot(left, jnp.dot(k, right, preferred_element_type=F32), preferred_element_type=F32)
        k_parts[part] = (k * same).astype(BF16)

    swap = place(rows, rows, lambda r, c: (r % 8 * 2 + r // 8 % 2) * local + r // 16 == c).astype(BF16)
    for g in range(4):
        out = jnp.dot(swap, f_ref[g * rows : (g + 1) * rows, :], preferred_element_type=F32).astype(BF16)
        for k in range(local):
            f_by[k, g * 16 : g * 16 + 16, :] = out[k * 16 : k * 16 + 16]

    @pl.loop(0, n_chunks)
    def _(b):
        copy(b).wait()
        at = pl.ds(pl.multiple_of(b * block_c, block_c), block_c) if n_chunks > 1 else slice(None)
        u = [jnp.dot(f_by[k], held[b, k], preferred_element_type=F32).astype(BF16) for k in range(local)]
        for g in range(2):
            block = jnp.concatenate([x[g * 32 : g * 32 + 32] for x in u], axis=0)
            out = jnp.dot(k_parts[0], block, preferred_element_type=F32) + jnp.dot(
                k_parts[1], block, preferred_element_type=F32
            )
            out = out.reshape(2 * half, 16, block_c)
            keep_ref[:, g * 16 : g * 16 + 16, at] = out[:half]
            send_ref[:, g * 16 : g * 16 + 16, at] = out[half:].astype(BF16)


def gram_kernel(keep_ref, got_ref, mine_ref, gram_ref):
    mine = keep_ref[...] + got_ref[...].astype(F32)
    mine_ref[...] = mine
    gram = jnp.zeros((P_SIZE, P_SIZE), F32)
    for j in range(mine.shape[0]):
        gram += lax.dot_general(
            mine[j], mine[j], NT, preferred_element_type=F32, precision=lax.Precision.HIGHEST
        )
    gram = jnp.concatenate([gram[8 * i : 8 * i + 8] for i in range(P_SIZE // 8)], axis=1)
    for i in range(gram_ref.shape[0]):
        gram_ref[i] = gram


def last_kernel(factor, gram_ref, mine_ref, out_ref):
    total = jnp.sum(gram_ref[...], axis=0)
    gram = jnp.concatenate([total[:, P_SIZE * i : P_SIZE * (i + 1)] for i in range(P_SIZE // 8)], axis=0)
    row = lax.broadcasted_iota(jnp.int32, (P_SIZE, P_SIZE), 0)
    col = lax.broadcasted_iota(jnp.int32, (P_SIZE, P_SIZE), 1)
    eye = jnp.where(row == col, 1.0, 0.0).astype(F32)
    scale = jnp.sum(gram * eye, keepdims=True) + 1e-06

    def dot(a, b):
        return jnp.dot(a, b, preferred_element_type=F32, precision=lax.Precision.HIGH)

    current = gram / scale
    inverse = eye
    for _ in range(NSTEPS):
        weight = 1.5 * eye - 0.5 * dot(inverse, current)
        current = dot(current, weight)
        inverse = dot(weight, inverse)
    inverse = inverse * (factor / jnp.sqrt(scale))
    for j in range(mine_ref.shape[0]):
        out_ref[j] = lax.dot_general(
            inverse,
            mine_ref[j],
            (((0,), (0,)), ((), ())),
            preferred_element_type=F32,
            precision=lax.Precision.HIGHEST,
        )


def vmem(n):
    return [pl.BlockSpec(memory_space=pltpu.VMEM)] * n


def shards(damping, block_seeds, n_row, n_col):
    cols, local, m = damping.shape
    n_blocks = block_seeds.shape[0]
    n_freq = local * n_row
    channels = 2 * local
    n_dev = n_row * n_col
    amp = math.sqrt(2.0 / n_freq) / math.sqrt(n_blocks * m)
    most, large, params = (pltpu.CompilerParams(vmem_limit_bytes=x << 20) for x in (54, 40, 20))

    block_c = 256 if cols % 256 == 0 else cols
    lanes_c = 128 if block_c % 128 == 0 else block_c
    lane_w = 128 if m % 128 == 0 else m
    per_pass = 2 if m % (2 * lane_w) == 0 else 1
    flat = damping.reshape(cols * local, m)

    w_row = channel_table(n_freq, np.arange(n_freq), np.arange(n_blocks), n_blocks)
    w_row = w_row.reshape(n_row, local, 2, n_blocks).transpose(0, 2, 1, 3)
    sign = np.array([1.0, -1.0])[None, :, None, None] * amp
    per_owner, half, quarter = n_blocks // n_row, n_blocks // 2, n_row // 4

    n_rows = P_SIZE * channels
    whole = lambda *s: pl.BlockSpec(s, lambda i: (0,) * len(s))
    v_one = pl.BlockSpec(memory_space=pltpu.VMEM)
    work = 2 * cols * local * m
    t = pl.pallas_call(
        lambda *refs: forward_kernel(local, n_freq, *refs),
        out_shape=jax.ShapeDtypeStruct((P_SIZE, channels, m), BF16),
        in_specs=[pl.BlockSpec(memory_space=pl.ANY)] * 2,
        out_specs=v_one,
        scratch_shapes=[
            pltpu.VMEM((cols // block_c, block_c * local, m), BF16),
            pltpu.VMEM((2, local, block_c, per_pass * lane_w), BF16),
            pltpu.VMEM((m // lane_w, P_SIZE // 4, 8 * local, lane_w), F32),
            pltpu.VMEM((P_SIZE * n_blocks, block_c), BF16),
            pltpu.VMEM((P_SIZE, n_blocks, lanes_c), F32),
            pltpu.VMEM((P_SIZE, n_blocks, lanes_c), F32),
            pltpu.VMEM((4, n_blocks, lanes_c), F32),
            pltpu.VMEM((2, channels * 8, 8 * n_blocks), BF16),
            pltpu.VMEM((2, local, 2 * P_SIZE, block_c), BF16),
            pltpu.SMEM((n_blocks,), jnp.int32),
            pltpu.SemaphoreType.DMA((cols // block_c, m // (per_pass * lane_w))),
            pltpu.SemaphoreType.DMA,
        ],
        compiler_params=large,
        cost_estimate=pl.CostEstimate(flops=64 * work, bytes_accessed=work, transcendentals=0),
        name="forward",
    )(block_seeds, flat)
    t, flat = lax.optimization_barrier((t, flat))
    block_s = 128 if cols % 128 == 0 else cols
    by_freq = pl.pallas_call(
        lambda *refs: separate_kernel(local, *refs),
        grid=(cols // block_s,),
        out_shape=jax.ShapeDtypeStruct((local, m, cols), BF16),
        in_specs=[pl.BlockSpec((block_s * local, m), lambda i: (i, 0))],
        out_specs=pl.BlockSpec((local, m, block_s), lambda i: (0, 0, i)),
        compiler_params=most,
        cost_estimate=pl.CostEstimate(flops=work, bytes_accessed=2 * work, transcendentals=0),
        name="separate",
    )(flat)

    n_grp = n_dev // 2
    n_p = math.gcd(P_SIZE, n_grp)
    n_r = n_grp // n_p
    p_own, lanes = P_SIZE // n_p, m // n_r
    halves = [list(range(n_grp)), list(range(n_grp, n_dev))]
    across = [(i, (i + n_row // 2) % n_row) for i in range(n_row)]
    t = t.reshape(n_p, p_own * channels, n_r, lanes).transpose(0, 2, 1, 3)
    t = t.reshape(n_grp, p_own * channels, lanes)
    t = lax.all_to_all(t, ("row", "col"), 0, 0, axis_index_groups=halves, tiled=True)
    t, by_freq = lax.optimization_barrier((t, by_freq))
    t = t.reshape(n_grp, p_own, channels, lanes)

    merge = (w_row * sign).reshape(2, n_row // 2, 1, channels, n_blocks).repeat(n_col, axis=2)
    merge = merge.reshape(2, n_grp * channels, n_blocks).transpose(0, 2, 1)
    merge = np.concatenate(high_low(merge), axis=1)
    b_hi, b_lo = high_low(w_row.reshape(2, n_row // 2 * channels, n_blocks))
    fan = np.concatenate([b_hi, b_hi, b_lo], axis=2)
    keep, send = pl.pallas_call(
        lambda *refs: gather_kernel(n_row, *refs),
        out_shape=(
            jax.ShapeDtypeStruct((p_own, n_blocks, lanes), F32),
            jax.ShapeDtypeStruct((p_own, n_blocks, lanes), BF16),
        ),
        in_specs=vmem(2),
        out_specs=tuple(vmem(2)),
        compiler_params=params,
        name="gather",
    )(jnp.asarray(merge), t)
    got = lax.ppermute(send, "row", across)
    f = pl.pallas_call(
        lambda *refs: scatter_kernel(n_row, *refs),
        out_shape=jax.ShapeDtypeStruct((n_row // 2, n_col, p_own, channels, lanes), BF16),
        in_specs=vmem(3),
        out_specs=v_one,
        compiler_params=params,
        name="scatter",
    )(jnp.asarray(fan), keep, got)
    f = f.reshape(n_grp, p_own * channels, lanes)
    f = lax.all_to_all(f, ("row", "col"), 0, 0, axis_index_groups=halves, tiled=True)
    f = f.reshape(n_p, n_r, p_own * channels, lanes).transpose(0, 2, 1, 3).reshape(n_rows, m)

    keep, send = pl.pallas_call(
        lambda *refs: backward_kernel(local, n_row, n_blocks, amp, *refs),
        out_shape=(
            jax.ShapeDtypeStruct((half, P_SIZE, cols), F32),
            jax.ShapeDtypeStruct((half, P_SIZE, cols), BF16),
        ),
        in_specs=vmem(1) + [pl.BlockSpec(memory_space=pl.ANY)],
        out_specs=tuple(vmem(2)),
        scratch_shapes=[
            pltpu.VMEM((cols // block_s, local, m, block_s), BF16),
            pltpu.VMEM((local, 2 * P_SIZE, m), BF16),
            pltpu.VMEM((2, n_blocks * 16, channels * 16), BF16),
            pltpu.SemaphoreType.DMA((cols // block_s,)),
        ],
        compiler_params=large,
        cost_estimate=pl.CostEstimate(flops=64 * work, bytes_accessed=work, transcendentals=0),
        name="backward",
    )(f, by_freq)
    got = lax.ppermute(send, "row", [(i, i ^ 1) for i in range(n_row)])
    summed = (keep + got.astype(F32)).astype(BF16)
    groups = [[core + 2 * (i + quarter * h) for i in range(quarter)] for h in range(2) for core in range(2)]
    summed = lax.all_to_all(summed, "row", 0, 0, axis_index_groups=groups, tiled=True)
    summed = summed.reshape(quarter, 2, per_owner, P_SIZE, cols)
    keep, send = pl.pallas_call(
        join_kernel,
        out_shape=(
            jax.ShapeDtypeStruct((per_owner, P_SIZE, cols), F32),
            jax.ShapeDtypeStruct((per_owner, P_SIZE, cols), BF16),
        ),
        in_specs=vmem(1),
        out_specs=tuple(vmem(2)),
        compiler_params=params,
        name="join",
    )(summed)
    got = lax.ppermute(send, "row", across)

    mine, gram = pl.pallas_call(
        gram_kernel,
        out_shape=(
            jax.ShapeDtypeStruct((per_owner, P_SIZE, cols), F32),
            jax.ShapeDtypeStruct((n_dev, 8, 4 * P_SIZE), F32),
        ),
        in_specs=vmem(2),
        out_specs=tuple(vmem(2)),
        compiler_params=params,
        name="gram",
    )(keep, got)
    gram = lax.all_to_all(gram, ("row", "col"), 0, 0, tiled=True)
    out = pl.pallas_call(
        lambda *refs: last_kernel(math.sqrt(n_blocks * m), *refs),
        out_shape=jax.ShapeDtypeStruct((per_owner, P_SIZE, cols), F32),
        in_specs=vmem(2),
        out_specs=vmem(1)[0],
        compiler_params=params,
        name="last",
    )(gram, mine)
    return out.transpose(0, 2, 1)


def solution(mesh):
    n_row, n_col = mesh.shape["row"], mesh.shape["col"]
    return jax.shard_map(
        lambda damping, block_seeds: shards(damping, block_seeds, n_row, n_col),
        mesh=mesh,
        in_specs=(P("col", "row", None), P()),
        out_specs=P("row", "col", None),
        check_vma=False,
    )
```

```python
import math

import numpy as np
import jax
import jax.numpy as jnp
from jax import lax
from jax.experimental import pallas as pl
from jax.experimental.pallas import tpu as pltpu
from jax.sharding import PartitionSpec as P

NSTEPS = 12
PRIME = 65521
P_SIZE = 32
BF16 = jnp.bfloat16
F32 = jnp.float32
NT = (((1,), (1,)), ((), ()))


def channel_table(n_freq, freqs, steps, n_blocks):
    angle = math.pi * (np.asarray(freqs)[:, None] + 0.5) / n_freq * np.asarray(steps)[None, :]
    decay = 3.0 ** (-np.asarray(steps) / n_blocks)
    return np.stack([decay * np.cos(angle), decay * np.sin(angle)], axis=1)


def high_low(values):
    high = values.astype(np.float32).astype(jnp.bfloat16)
    low = (values - high.astype(np.float64)).astype(np.float32).astype(jnp.bfloat16)
    return high, low


def _fit(fn, degree):
    nodes = np.cos(np.pi * (np.arange(64) + 0.5) / 64)
    u = (nodes + 1.0) / 128
    series = np.polynomial.chebyshev.Chebyshev.fit(u, fn(np.sqrt(u)), degree, domain=[0.0, 1 / 64])
    return [float(x) for x in series.convert(kind=np.polynomial.Polynomial, domain=[-1, 1], window=[-1, 1]).coef]


COS_COEFS = _fit(lambda t: np.cos(2 * np.pi * t), 5)
SIN_COEFS = _fit(lambda t: np.sin(2 * np.pi * t) / t, 5)


def polynomial(coefs, u):
    out = jnp.full_like(u, coefs[-1])
    for coef in coefs[-2::-1]:
        out = out * u + coef
    return out


def cos_sin(turns):
    quarter = jnp.round(turns * 4.0)
    rest = turns - quarter * 0.25
    u = rest * rest
    cos, sin = polynomial(COS_COEFS, u), polynomial(SIN_COEFS, u) * rest
    odd = jnp.abs(quarter) == 1.0
    far = jnp.abs(quarter) == 2.0
    flip_cos = jnp.logical_or(quarter == 1.0, far)
    flip_sin = jnp.logical_or(quarter == -1.0, far)
    out_cos, out_sin = jnp.where(odd, sin, cos), jnp.where(odd, cos, sin)
    return jnp.where(flip_cos, -out_cos, out_cos), jnp.where(flip_sin, -out_sin, out_sin)


def mod_turns(x):
    return (x - jnp.round(x * (1.0 / PRIME)) * float(PRIME)) * (1.0 / PRIME)


def channel_values(n_freq, n_blocks, freq, step, sine):
    turns = ((2 * freq + 1) * step % (4 * n_freq)).astype(F32) * (0.25 / n_freq)
    cos, sin = cos_sin(turns - jnp.round(turns))
    values = jnp.where(sine, sin, cos) * jnp.exp(step.astype(F32) * (-math.log(3.0) / n_blocks))
    return values


def split(values):
    high = values.astype(BF16).astype(F32)
    return high, values - high


def separate(x, local):
    return jnp.swapaxes(x.reshape(x.shape[0] // local, local, x.shape[1]), 0, 1)


def iotas(rows, cols):
    return (lax.broadcasted_iota(jnp.int32, (rows, cols), d) for d in range(2))


def place(rows, cols, test):
    r = lax.broadcasted_iota(jnp.int32, (rows, cols), 0)
    c = lax.broadcasted_iota(jnp.int32, (rows, cols), 1)
    return test(r, c).astype(F32)


def less_turns(x):
    return x - (x.astype(F32) * (1.0 / PRIME)).astype(jnp.int32) * PRIME


def forward_kernel(local, n_freq, seeds_ref, d_ref, t_ref, held, by_freq, acc, probes, cos_shift, sin_shift, state, spread, q_all, own, sems, sem):
    n_chunks, rows, m = held.shape
    block_c = rows // local
    channels = 2 * local
    n_blocks, lanes = cos_shift.shape[1:]
    group = 8
    tiles = P_SIZE // 8
    width, lane_w = by_freq.shape[3], acc.shape[3]
    passes, per_pass = m // width, width // lane_w

    n_parts = sems.shape[1]

    def copy(b, i):
        part = (slice(b * rows, (b + 1) * rows), slice(i * m // n_parts, (i + 1) * m // n_parts))
        return pltpu.make_async_copy(d_ref.at[part], held.at[b, :, part[1]], sems.at[b, i])

    fetch = pltpu.make_async_copy(seeds_ref, own, sem)
    fetch.start()
    for b in range(n_chunks):
        for i in range(n_parts):
            copy(b, i).start()

    row, col = iotas(channels, n_blocks)
    table = channel_values(n_freq, n_blocks, lax.axis_index("row") * local + row % local, col, row >= local)
    left = place(channels * group, channels, lambda r, c: r // group == c)
    right = place(n_blocks, group * n_blocks, lambda r, c: r == c % n_blocks)
    same = place(channels * group, group * n_blocks, lambda r, c: r % group == c // n_blocks)
    for part, w in enumerate(split(table)):
        w = jnp.dot(w, right, preferred_element_type=F32)
        spread[part] = (jnp.dot(left, w, preferred_element_type=F32) * same).astype(BF16)

    fetch.wait()
    line, lane = iotas(n_blocks, lanes)
    seeds = jnp.zeros((n_blocks, lanes), jnp.int32)
    for j in range(n_blocks):
        seeds = jnp.where(line == j, own[j], seeds)
    steps = (lane + 1).astype(F32)
    shift = mod_turns(seeds.astype(F32) * steps) * float(PRIME)
    shift_parts = cos_sin(mod_turns(jnp.round(shift) * (steps + 1.0)))
    for p in range(P_SIZE):
        for part, out in zip(shift_parts, (cos_shift, sin_shift)):
            out[p] = jnp.broadcast_to(part[:, p : p + 1], (n_blocks, lanes))

    start = lax.axis_index("col") * (n_chunks * block_c)
    spans = [(at, p) for at in range(0, block_c, lanes) for p in range(0, P_SIZE, 8)]

    def make_probes(b, span):
        at, first = span
        if first == 0:
            column = start + b * block_c + at + lane
            inner = less_turns(less_turns(seeds * (column + 1)) * (column + 3)).astype(F32)
            turn_cos, turn_sin = cos_sin(mod_turns(inner))
            cos, sin = turn_cos, turn_sin
        else:
            cos, sin, turn_cos, turn_sin = (state[i] for i in range(4))
        for p in range(first, first + 8):
            value = cos * cos_shift[p] - sin * sin_shift[p]
            probes[p * n_blocks : (p + 1) * n_blocks, at : at + lanes] = value.astype(BF16)
            cos, sin = cos * turn_cos - sin * turn_sin, sin * turn_cos + cos * turn_sin
        for i, x in enumerate((cos, sin, turn_cos, turn_sin)):
            state[i] = x

    def make_channels(b):
        for g in range(P_SIZE // group):
            block = probes[g * group * n_blocks : (g + 1) * group * n_blocks, :]
            q = jnp.dot(spread[0], block, preferred_element_type=F32) + jnp.dot(
                spread[1], block, preferred_element_type=F32
            )
            q = q.astype(BF16)
            for part in range(2):
                for k in range(local):
                    at = (part * local + k) * group
                    to = part * P_SIZE + g * group
                    q_all[b % 2, k, to : to + group, :] = q[at : at + group]

    for span in spans:
        make_probes(0, span)
    make_channels(0)
    for b in range(n_chunks):
        for i in range(passes):
            if i * n_parts % passes == 0:
                copy(b, i * n_parts // passes).wait()
            if b + 1 < n_chunks:
                for span in spans[len(spans) * i // passes : len(spans) * (i + 1) // passes]:
                    make_probes(b + 1, span)
            at = slice(i * width, (i + 1) * width)
            for c in range(0, block_c, 16):
                by_freq[i % 2, :, c : c + 16, :] = separate(held[b, c * local : (c + 16) * local, at], local)
            for k in range(local):
                o = jnp.dot(q_all[b % 2, k], by_freq[i % 2, k], preferred_element_type=F32)
                for l in range(per_pass):
                    for t in range(2 * tiles):
                        piece = o[t * 8 : t * 8 + 8, l * lane_w : (l + 1) * lane_w]
                        if b > 0:
                            piece += acc[i * per_pass + l, t, k * 8 : k * 8 + 8, :]
                        acc[i * per_pass + l, t, k * 8 : k * 8 + 8, :] = piece
            if b + 1 == n_chunks:
                for l in range(i * per_pass, (i + 1) * per_pass):
                    for p in range(P_SIZE):
                        t = jnp.concatenate(
                            [acc[l, part * tiles + p // 8, pl.ds(p % 8, local, stride=8), :] for part in range(2)],
                            axis=0,
                        )
                        t_ref[p, :, l * lane_w : (l + 1) * lane_w] = t.astype(BF16)
        if b + 1 < n_chunks:
            make_channels(b + 1)


def half_of(n_row):
    return lax.axis_index("row") // (n_row // 2)


def gather_kernel(n_row, c_ref, x_ref, keep_ref, send_ref):
    n_src, p_own, channels, lanes = x_ref.shape
    table = c_ref[half_of(n_row)]
    n = table.shape[0] // 2
    for p in range(p_own):
        x = x_ref[:, p].reshape(n_src * channels, lanes)
        both = jnp.dot(table, x, preferred_element_type=F32)
        out = both[:n] + both[n:]
        keep_ref[p] = out
        send_ref[p] = out.astype(BF16)


def scatter_kernel(n_row, b_ref, keep_ref, got_ref, f_ref):
    n_rows, n_cols, p_own, channels, lanes = f_ref.shape
    table = b_ref[half_of(n_row)]
    for p in range(p_own):
        forward = keep_ref[p] + got_ref[p].astype(F32)
        high = forward.astype(BF16)
        low = (forward - high.astype(F32)).astype(BF16)
        out = jnp.dot(table, jnp.concatenate([high, low, high], axis=0), preferred_element_type=F32)
        out = out.astype(BF16).reshape(n_rows, channels, lanes)
        for col in range(n_cols):
            f_ref[:, col, p] = out


def join_kernel(x_ref, keep_ref, send_ref):
    x = x_ref[...].astype(F32)
    total = jnp.sum(x, axis=0)
    keep_ref[...] = total[0]
    send_ref[...] = total[1].astype(BF16)


def backward_kernel(local, n_row, n_blocks, amp, f_ref, d_ref, keep_ref, send_ref, held, by_freq, sums, f_by, k_parts, sems):
    n_chunks, tall, m = held.shape
    block_c = tall // local
    width = 256 if m % 256 == 0 else m
    rows = f_ref.shape[0] // 4
    channels = 2 * local

    n_parts = sems.shape[1]

    def copy(b, i):
        at = pl.ds(i * m // n_parts, m // n_parts)
        return pltpu.make_async_copy(d_ref.at[pl.ds(b * tall, tall), at], held.at[b, :, at], sems.at[b, i])

    for b in range(n_chunks):
        for i in range(n_parts):
            copy(b, i).start()

    row_at = lax.axis_index("row")
    half, per_owner, quarter = n_blocks // 2, n_blocks // n_row, n_row // 4
    r, c = iotas(n_blocks, channels)
    rest = r % half
    chip = rest // (2 * per_owner) + quarter * ((rest // per_owner + half_of(n_row)) % 2)
    block_at = (2 * chip + (r // half + row_at) % 2) * per_owner + rest % per_owner
    sine = c % 2 == 1
    table = channel_values(local * n_row, n_blocks, row_at * local + c // 2, block_at + 1, sine)
    table = table * jnp.where(sine, -amp, amp)
    left = place(n_blocks * 16, n_blocks, lambda r, c: r // 16 == c)
    right = place(channels, channels * 16, lambda r, c: r == c // 32 * 2 + c // 8 % 2)
    same = place(n_blocks * 16, channels * 16, lambda r, c: r % 16 == c // 16 % 2 * 8 + c % 8)
    for part, k in enumerate(split(table)):
        k = jnp.dot(left, jnp.dot(k, right, preferred_element_type=F32), preferred_element_type=F32)
        k_parts[part] = (k * same).astype(BF16)

    swap = place(rows, rows, lambda r, c: (r % 8 * 2 + r // 8 % 2) * local + r // 16 == c).astype(BF16)
    for g in range(4):
        out = jnp.dot(swap, f_ref[g * rows : (g + 1) * rows, :], preferred_element_type=F32).astype(BF16)
        for k in range(local):
            f_by[k, g * 16 : g * 16 + 16, :] = out[k * 16 : k * 16 + 16]

    @pl.loop(0, n_chunks)
    def _(b):
        at = pl.ds(pl.multiple_of(b * block_c, block_c), block_c) if n_chunks > 1 else slice(None)
        for i in range(0, m, width):
            if i * n_parts % m == 0:
                copy(b, i * n_parts // m).wait()
            for c in range(0, block_c, 16):
                piece = held[b, c * local : (c + 16) * local, i : i + width]
                by_freq[:, c : c + 16, i : i + width] = separate(piece, local)
            for k in range(local):
                part = lax.dot_general(
                    f_by[k, :, i : i + width], by_freq[k, :, i : i + width], NT, preferred_element_type=F32
                )
                sums[k] = part if i == 0 else sums[k] + part
        u = [sums[k].astype(BF16) for k in range(local)]
        for g in range(2):
            block = jnp.concatenate([x[g * 32 : g * 32 + 32] for x in u], axis=0)
            out = jnp.dot(k_parts[0], block, preferred_element_type=F32) + jnp.dot(
                k_parts[1], block, preferred_element_type=F32
            )
            out = out.reshape(2 * half, 16, block_c)
            keep_ref[:, g * 16 : g * 16 + 16, at] = out[:half]
            send_ref[:, g * 16 : g * 16 + 16, at] = out[half:].astype(BF16)


def gram_kernel(keep_ref, got_ref, mine_ref, gram_ref):
    mine = keep_ref[...] + got_ref[...].astype(F32)
    mine_ref[...] = mine
    gram = jnp.zeros((P_SIZE, P_SIZE), F32)
    for j in range(mine.shape[0]):
        gram += lax.dot_general(
            mine[j], mine[j], NT, preferred_element_type=F32, precision=lax.Precision.HIGHEST
        )
    gram = jnp.concatenate([gram[8 * i : 8 * i + 8] for i in range(P_SIZE // 8)], axis=1)
    for i in range(gram_ref.shape[0]):
        gram_ref[i] = gram


def last_kernel(factor, gram_ref, mine_ref, out_ref):
    total = jnp.sum(gram_ref[...], axis=0)
    gram = jnp.concatenate([total[:, P_SIZE * i : P_SIZE * (i + 1)] for i in range(P_SIZE // 8)], axis=0)
    row = lax.broadcasted_iota(jnp.int32, (P_SIZE, P_SIZE), 0)
    col = lax.broadcasted_iota(jnp.int32, (P_SIZE, P_SIZE), 1)
    eye = jnp.where(row == col, 1.0, 0.0).astype(F32)
    scale = jnp.sum(gram * eye, keepdims=True) + 1e-06

    def dot(a, b):
        return jnp.dot(a, b, preferred_element_type=F32, precision=lax.Precision.HIGH)

    current = gram / scale
    inverse = eye
    for _ in range(NSTEPS):
        weight = 1.5 * eye - 0.5 * dot(inverse, current)
        current = dot(current, weight)
        inverse = dot(weight, inverse)
    inverse = inverse * (factor / jnp.sqrt(scale))
    for j in range(mine_ref.shape[0]):
        out_ref[j] = lax.dot_general(
            inverse,
            mine_ref[j],
            (((0,), (0,)), ((), ())),
            preferred_element_type=F32,
            precision=lax.Precision.HIGHEST,
        )


def vmem(n):
    return [pl.BlockSpec(memory_space=pltpu.VMEM)] * n


def shards(damping, block_seeds, n_row, n_col):
    cols, local, m = damping.shape
    n_blocks = block_seeds.shape[0]
    n_freq = local * n_row
    channels = 2 * local
    n_dev = n_row * n_col
    amp = math.sqrt(2.0 / n_freq) / math.sqrt(n_blocks * m)
    large, params = (pltpu.CompilerParams(vmem_limit_bytes=x << 20) for x in (40, 20))

    block_c = 256 if cols % 256 == 0 else cols
    lanes_c = 128 if block_c % 128 == 0 else block_c
    lane_w = 128 if m % 128 == 0 else m
    per_pass = 2 if m % (2 * lane_w) == 0 else 1
    halves_m = 2 if m % (4 * lane_w) == 0 else 1
    flat = damping.reshape(cols * local, m)

    w_row = channel_table(n_freq, np.arange(n_freq), np.arange(n_blocks), n_blocks)
    w_row = w_row.reshape(n_row, local, 2, n_blocks).transpose(0, 2, 1, 3)
    sign = np.array([1.0, -1.0])[None, :, None, None] * amp
    per_owner, half, quarter = n_blocks // n_row, n_blocks // 2, n_row // 4

    n_rows = P_SIZE * channels
    whole = lambda *s: pl.BlockSpec(s, lambda i: (0,) * len(s))
    v_one = pl.BlockSpec(memory_space=pltpu.VMEM)
    work = 2 * cols * local * m
    t = pl.pallas_call(
        lambda *refs: forward_kernel(local, n_freq, *refs),
        out_shape=jax.ShapeDtypeStruct((P_SIZE, channels, m), BF16),
        in_specs=[pl.BlockSpec(memory_space=pl.ANY)] * 2,
        out_specs=v_one,
        scratch_shapes=[
            pltpu.VMEM((cols // block_c, block_c * local, m), BF16),
            pltpu.VMEM((2, local, block_c, per_pass * lane_w), BF16),
            pltpu.VMEM((m // lane_w, P_SIZE // 4, 8 * local, lane_w), F32),
            pltpu.VMEM((P_SIZE * n_blocks, block_c), BF16),
            pltpu.VMEM((P_SIZE, n_blocks, lanes_c), F32),
            pltpu.VMEM((P_SIZE, n_blocks, lanes_c), F32),
            pltpu.VMEM((4, n_blocks, lanes_c), F32),
            pltpu.VMEM((2, channels * 8, 8 * n_blocks), BF16),
            pltpu.VMEM((2, local, 2 * P_SIZE, block_c), BF16),
            pltpu.SMEM((n_blocks,), jnp.int32),
            pltpu.SemaphoreType.DMA((cols // block_c, halves_m)),
            pltpu.SemaphoreType.DMA,
        ],
        compiler_params=large,
        cost_estimate=pl.CostEstimate(flops=64 * work, bytes_accessed=work, transcendentals=0),
        name="forward",
    )(block_seeds, flat)
    block_s = 256 if cols % 256 == 0 else cols

    n_grp = n_dev // 2
    n_p = math.gcd(P_SIZE, n_grp)
    n_r = n_grp // n_p
    p_own, lanes = P_SIZE // n_p, m // n_r
    halves = [list(range(n_grp)), list(range(n_grp, n_dev))]
    across = [(i, (i + n_row // 2) % n_row) for i in range(n_row)]
    t = t.reshape(n_p, p_own * channels, n_r, lanes).transpose(0, 2, 1, 3)
    t = t.reshape(n_grp, p_own * channels, lanes)
    t = lax.all_to_all(t, ("row", "col"), 0, 0, axis_index_groups=halves, tiled=True)
    t = t.reshape(n_grp, p_own, channels, lanes)

    merge = (w_row * sign).reshape(2, n_row // 2, 1, channels, n_blocks).repeat(n_col, axis=2)
    merge = merge.reshape(2, n_grp * channels, n_blocks).transpose(0, 2, 1)
    merge = np.concatenate(high_low(merge), axis=1)
    b_hi, b_lo = high_low(w_row.reshape(2, n_row // 2 * channels, n_blocks))
    fan = np.concatenate([b_hi, b_hi, b_lo], axis=2)
    keep, send = pl.pallas_call(
        lambda *refs: gather_kernel(n_row, *refs),
        out_shape=(
            jax.ShapeDtypeStruct((p_own, n_blocks, lanes), F32),
            jax.ShapeDtypeStruct((p_own, n_blocks, lanes), BF16),
        ),
        in_specs=vmem(2),
        out_specs=tuple(vmem(2)),
        compiler_params=params,
        name="gather",
    )(jnp.asarray(merge), t)
    got = lax.ppermute(send, "row", across)
    f = pl.pallas_call(
        lambda *refs: scatter_kernel(n_row, *refs),
        out_shape=jax.ShapeDtypeStruct((n_row // 2, n_col, p_own, channels, lanes), BF16),
        in_specs=vmem(3),
        out_specs=v_one,
        compiler_params=params,
        name="scatter",
    )(jnp.asarray(fan), keep, got)
    f = f.reshape(n_grp, p_own * channels, lanes)
    f = lax.all_to_all(f, ("row", "col"), 0, 0, axis_index_groups=halves, tiled=True)
    f = f.reshape(n_p, n_r, p_own * channels, lanes).transpose(0, 2, 1, 3).reshape(n_rows, m)

    keep, send = pl.pallas_call(
        lambda *refs: backward_kernel(local, n_row, n_blocks, amp, *refs),
        out_shape=(
            jax.ShapeDtypeStruct((half, P_SIZE, cols), F32),
            jax.ShapeDtypeStruct((half, P_SIZE, cols), BF16),
        ),
        in_specs=vmem(1) + [pl.BlockSpec(memory_space=pl.ANY)],
        out_specs=tuple(vmem(2)),
        scratch_shapes=[
            pltpu.VMEM((cols // block_s, block_s * local, m), BF16),
            pltpu.VMEM((local, block_s, m), BF16),
            pltpu.VMEM((local, 2 * P_SIZE, block_s), F32),
            pltpu.VMEM((local, 2 * P_SIZE, m), BF16),
            pltpu.VMEM((2, n_blocks * 16, channels * 16), BF16),
            pltpu.SemaphoreType.DMA((cols // block_s, halves_m)),
        ],
        compiler_params=large,
        cost_estimate=pl.CostEstimate(flops=64 * work, bytes_accessed=work, transcendentals=0),
        name="backward",
    )(f, flat)
    got = lax.ppermute(send, "row", [(i, i ^ 1) for i in range(n_row)])
    summed = (keep + got.astype(F32)).astype(BF16)
    groups = [[core + 2 * (i + quarter * h) for i in range(quarter)] for h in range(2) for core in range(2)]
    summed = lax.all_to_all(summed, "row", 0, 0, axis_index_groups=groups, tiled=True)
    summed = summed.reshape(quarter, 2, per_owner, P_SIZE, cols)
    keep, send = pl.pallas_call(
        join_kernel,
        out_shape=(
            jax.ShapeDtypeStruct((per_owner, P_SIZE, cols), F32),
            jax.ShapeDtypeStruct((per_owner, P_SIZE, cols), BF16),
        ),
        in_specs=vmem(1),
        out_specs=tuple(vmem(2)),
        compiler_params=params,
        name="join",
    )(summed)
    got = lax.ppermute(send, "row", across)

    mine, gram = pl.pallas_call(
        gram_kernel,
        out_shape=(
            jax.ShapeDtypeStruct((per_owner, P_SIZE, cols), F32),
            jax.ShapeDtypeStruct((n_dev, 8, 4 * P_SIZE), F32),
        ),
        in_specs=vmem(2),
        out_specs=tuple(vmem(2)),
        compiler_params=params,
        name="gram",
    )(keep, got)
    gram = lax.all_to_all(gram, ("row", "col"), 0, 0, tiled=True)
    out = pl.pallas_call(
        lambda *refs: last_kernel(math.sqrt(n_blocks * m), *refs),
        out_shape=jax.ShapeDtypeStruct((per_owner, P_SIZE, cols), F32),
        in_specs=vmem(2),
        out_specs=vmem(1)[0],
        compiler_params=params,
        name="last",
    )(gram, mine)
    return out.transpose(0, 2, 1)


def solution(mesh):
    n_row, n_col = mesh.shape["row"], mesh.shape["col"]
    return jax.shard_map(
        lambda damping, block_seeds: shards(damping, block_seeds, n_row, n_col),
        mesh=mesh,
        in_specs=(P("col", "row", None), P()),
        out_specs=P("row", "col", None),
        check_vma=False,
    )
```

```python
import math

import numpy as np
import jax
import jax.numpy as jnp
from jax import lax
from jax.experimental import pallas as pl
from jax.experimental.pallas import tpu as pltpu
from jax.sharding import PartitionSpec as P

NSTEPS = 12
PRIME = 65521
P_SIZE = 32
BF16 = jnp.bfloat16
F32 = jnp.float32
NT = (((1,), (1,)), ((), ()))


def channel_table(n_freq, freqs, steps, n_blocks):
    angle = math.pi * (np.asarray(freqs)[:, None] + 0.5) / n_freq * np.asarray(steps)[None, :]
    decay = 3.0 ** (-np.asarray(steps) / n_blocks)
    return np.stack([decay * np.cos(angle), decay * np.sin(angle)], axis=1)


def high_low(values):
    high = values.astype(np.float32).astype(jnp.bfloat16)
    low = (values - high.astype(np.float64)).astype(np.float32).astype(jnp.bfloat16)
    return high, low


def _fit(fn, degree):
    nodes = np.cos(np.pi * (np.arange(64) + 0.5) / 64)
    u = (nodes + 1.0) / 128
    series = np.polynomial.chebyshev.Chebyshev.fit(u, fn(np.sqrt(u)), degree, domain=[0.0, 1 / 64])
    return [float(x) for x in series.convert(kind=np.polynomial.Polynomial, domain=[-1, 1], window=[-1, 1]).coef]


COS_COEFS = _fit(lambda t: np.cos(2 * np.pi * t), 5)
SIN_COEFS = _fit(lambda t: np.sin(2 * np.pi * t) / t, 5)


def polynomial(coefs, u):
    out = jnp.full_like(u, coefs[-1])
    for coef in coefs[-2::-1]:
        out = out * u + coef
    return out


def cos_sin(turns):
    quarter = jnp.round(turns * 4.0)
    rest = turns - quarter * 0.25
    u = rest * rest
    cos, sin = polynomial(COS_COEFS, u), polynomial(SIN_COEFS, u) * rest
    odd = jnp.abs(quarter) == 1.0
    far = jnp.abs(quarter) == 2.0
    flip_cos = jnp.logical_or(quarter == 1.0, far)
    flip_sin = jnp.logical_or(quarter == -1.0, far)
    out_cos, out_sin = jnp.where(odd, sin, cos), jnp.where(odd, cos, sin)
    return jnp.where(flip_cos, -out_cos, out_cos), jnp.where(flip_sin, -out_sin, out_sin)


def mod_turns(x):
    return (x - jnp.round(x * (1.0 / PRIME)) * float(PRIME)) * (1.0 / PRIME)


def channel_values(n_freq, n_blocks, freq, step, sine):
    turns = ((2 * freq + 1) * step % (4 * n_freq)).astype(F32) * (0.25 / n_freq)
    cos, sin = cos_sin(turns - jnp.round(turns))
    values = jnp.where(sine, sin, cos) * jnp.exp(step.astype(F32) * (-math.log(3.0) / n_blocks))
    return values


def split(values):
    high = values.astype(BF16).astype(F32)
    return high, values - high


def separate(x, local):
    return jnp.swapaxes(x.reshape(x.shape[0] // local, local, x.shape[1]), 0, 1)


def iotas(rows, cols):
    return (lax.broadcasted_iota(jnp.int32, (rows, cols), d) for d in range(2))


def place(rows, cols, test):
    r = lax.broadcasted_iota(jnp.int32, (rows, cols), 0)
    c = lax.broadcasted_iota(jnp.int32, (rows, cols), 1)
    return test(r, c).astype(F32)


def less_turns(x):
    return x - (x.astype(F32) * (1.0 / PRIME)).astype(jnp.int32) * PRIME


def forward_kernel(local, n_freq, seeds_ref, d_ref, t_ref, held, by_freq, acc, probes, cos_shift, sin_shift, state, spread, q_all, own, sems, sem):
    n_chunks, rows, m = held.shape
    block_c = rows // local
    channels = 2 * local
    n_blocks, lanes = cos_shift.shape[1:]
    group = 8
    tiles = P_SIZE // 8
    width, lane_w = by_freq.shape[3], acc.shape[3]
    passes, per_pass = m // width, width // lane_w

    n_parts = sems.shape[1]

    def copy(b, i):
        part = (slice(b * rows, (b + 1) * rows), slice(i * m // n_parts, (i + 1) * m // n_parts))
        return pltpu.make_async_copy(d_ref.at[part], held.at[b, :, part[1]], sems.at[b, i])

    fetch = pltpu.make_async_copy(seeds_ref, own, sem)
    fetch.start()
    for b in range(n_chunks):
        for i in range(n_parts):
            copy(b, i).start()

    row, col = iotas(channels, n_blocks)
    table = channel_values(n_freq, n_blocks, lax.axis_index("row") * local + row % local, col, row >= local)
    left = place(channels * group, channels, lambda r, c: r // group == c)
    right = place(n_blocks, group * n_blocks, lambda r, c: r == c % n_blocks)
    same = place(channels * group, group * n_blocks, lambda r, c: r % group == c // n_blocks)
    for part, w in enumerate(split(table)):
        w = jnp.dot(w, right, preferred_element_type=F32)
        spread[part] = (jnp.dot(left, w, preferred_element_type=F32) * same).astype(BF16)

    fetch.wait()
    line, lane = iotas(n_blocks, lanes)
    seeds = jnp.zeros((n_blocks, lanes), jnp.int32)
    for j in range(n_blocks):
        seeds = jnp.where(line == j, own[j], seeds)
    steps = (lane + 1).astype(F32)
    shift = mod_turns(seeds.astype(F32) * steps) * float(PRIME)
    shift_parts = cos_sin(mod_turns(jnp.round(shift) * (steps + 1.0)))
    for p in range(P_SIZE):
        for part, out in zip(shift_parts, (cos_shift, sin_shift)):
            out[p] = jnp.broadcast_to(part[:, p : p + 1], (n_blocks, lanes))

    start = lax.axis_index("col") * (n_chunks * block_c)
    spans = [(at, p) for at in range(0, block_c, lanes) for p in range(0, P_SIZE, 8)]

    def make_probes(b, span):
        at, first = span
        if first == 0:
            column = start + b * block_c + at + lane
            inner = less_turns(less_turns(seeds * (column + 1)) * (column + 3)).astype(F32)
            turn_cos, turn_sin = cos_sin(mod_turns(inner))
            cos, sin = turn_cos, turn_sin
        else:
            cos, sin, turn_cos, turn_sin = (state[i] for i in range(4))
        for p in range(first, first + 8):
            value = cos * cos_shift[p] - sin * sin_shift[p]
            probes[p * n_blocks : (p + 1) * n_blocks, at : at + lanes] = value.astype(BF16)
            cos, sin = cos * turn_cos - sin * turn_sin, sin * turn_cos + cos * turn_sin
        for i, x in enumerate((cos, sin, turn_cos, turn_sin)):
            state[i] = x

    def make_channels(b):
        for g in range(P_SIZE // group):
            block = probes[g * group * n_blocks : (g + 1) * group * n_blocks, :]
            q = jnp.dot(spread[0], block, preferred_element_type=F32) + jnp.dot(
                spread[1], block, preferred_element_type=F32
            )
            q = q.astype(BF16)
            for part in range(2):
                for k in range(local):
                    at = (part * local + k) * group
                    to = part * P_SIZE + g * group
                    q_all[b % 2, k, to : to + group, :] = q[at : at + group]

    for span in spans:
        make_probes(0, span)
    make_channels(0)
    for b in range(n_chunks):
        for i in range(passes):
            if i * n_parts % passes == 0:
                copy(b, i * n_parts // passes).wait()
            if b + 1 < n_chunks:
                for span in spans[len(spans) * i // passes : len(spans) * (i + 1) // passes]:
                    make_probes(b + 1, span)
            at = slice(i * width, (i + 1) * width)
            for c in range(0, block_c, 16):
                by_freq[i % 2, :, c : c + 16, :] = separate(held[b, c * local : (c + 16) * local, at], local)
            for k in range(local):
                o = jnp.dot(q_all[b % 2, k], by_freq[i % 2, k], preferred_element_type=F32)
                for l in range(per_pass):
                    for t in range(2 * tiles):
                        piece = o[t * 8 : t * 8 + 8, l * lane_w : (l + 1) * lane_w]
                        if b > 0:
                            piece += acc[i * per_pass + l, t, k * 8 : k * 8 + 8, :]
                        acc[i * per_pass + l, t, k * 8 : k * 8 + 8, :] = piece
            if b + 1 == n_chunks:
                for l in range(i * per_pass, (i + 1) * per_pass):
                    for p in range(P_SIZE):
                        t = jnp.concatenate(
                            [acc[l, part * tiles + p // 8, pl.ds(p % 8, local, stride=8), :] for part in range(2)],
                            axis=0,
                        )
                        t_ref[p, :, l * lane_w : (l + 1) * lane_w] = t.astype(BF16)
        if b + 1 < n_chunks:
            make_channels(b + 1)


def half_of(n_row):
    return lax.axis_index("row") // (n_row // 2)


def gather_kernel(n_row, c_ref, x_ref, keep_ref, send_ref):
    n_src, p_own, channels, lanes = x_ref.shape
    table = c_ref[half_of(n_row)]
    n = table.shape[0] // 2
    for p in range(p_own):
        x = x_ref[:, p].reshape(n_src * channels, lanes)
        both = jnp.dot(table, x, preferred_element_type=F32)
        out = both[:n] + both[n:]
        keep_ref[p] = out
        send_ref[p] = out.astype(BF16)


def scatter_kernel(n_row, b_ref, keep_ref, got_ref, f_ref):
    n_rows, n_cols, p_own, channels, lanes = f_ref.shape
    table = b_ref[half_of(n_row)]
    for p in range(p_own):
        forward = keep_ref[p] + got_ref[p].astype(F32)
        high = forward.astype(BF16)
        low = (forward - high.astype(F32)).astype(BF16)
        out = jnp.dot(table, jnp.concatenate([high, low, high], axis=0), preferred_element_type=F32)
        out = out.astype(BF16).reshape(n_rows, channels, lanes)
        for col in range(n_cols):
            f_ref[:, col, p] = out


def join_kernel(x_ref, keep_ref, send_ref):
    x = x_ref[...].astype(F32)
    total = jnp.sum(x, axis=0)
    keep_ref[...] = total[0]
    send_ref[...] = total[1].astype(BF16)


def blocks_kernel(local, n_row, n_blocks, amp, k_ref):
    channels = 2 * local
    row_at = lax.axis_index("row")
    half, per_owner, quarter = n_blocks // 2, n_blocks // n_row, n_row // 4
    r, c = iotas(n_blocks, channels)
    rest = r % half
    chip = rest // (2 * per_owner) + quarter * ((rest // per_owner + half_of(n_row)) % 2)
    block_at = (2 * chip + (r // half + row_at) % 2) * per_owner + rest % per_owner
    sine = c % 2 == 1
    table = channel_values(local * n_row, n_blocks, row_at * local + c // 2, block_at + 1, sine)
    table = table * jnp.where(sine, -amp, amp)
    left = place(n_blocks * 16, n_blocks, lambda r, c: r // 16 == c)
    right = place(channels, channels * 16, lambda r, c: r == c // 32 * 2 + c // 8 % 2)
    same = place(n_blocks * 16, channels * 16, lambda r, c: r % 16 == c // 16 % 2 * 8 + c % 8)
    for part, k in enumerate(split(table)):
        k = jnp.dot(left, jnp.dot(k, right, preferred_element_type=F32), preferred_element_type=F32)
        k_ref[part] = (k * same).astype(BF16)


def separate_kernel(local, d_ref, o_ref):
    rows, m = d_ref.shape
    for i in range(0, m, 256):
        for c in range(0, rows // local, 16):
            piece = d_ref[c * local : (c + 16) * local, i : i + 256]
            o_ref[:, c : c + 16, i : i + 256] = separate(piece, local)


def backward_kernel(local, n_blocks, n_ready, f_ref, k_ref, d_ref, *refs):
    ready_ref = refs[0] if n_ready else None
    keep_ref, send_ref, raw, held, sums, f_by, k_parts, sems, sem = refs[bool(n_ready) :]
    n_chunks, _, block_c, m = held.shape
    n_parts = sems.shape[1]
    width = m // n_parts
    tall = block_c * local
    rows = f_ref.shape[0] // 4
    half = n_blocks // 2

    def copy(b, i):
        at = slice(i * width, (i + 1) * width)
        if b == 0:
            return pltpu.make_async_copy(d_ref.at[pl.ds(0, tall), at], raw.at[:, at], sems.at[b, i])
        source = ready_ref.at[:, pl.ds((b - 1) * block_c, block_c), at]
        return pltpu.make_async_copy(source, held.at[b, :, :, at], sems.at[b, i])

    tables = pltpu.make_async_copy(k_ref, k_parts, sem)
    for i in range(n_parts):
        for b in range(n_chunks):
            copy(b, i).start()
    tables.start()

    swap = place(rows, rows, lambda r, c: (r % 8 * 2 + r // 8 % 2) * local + r // 16 == c).astype(BF16)
    for g in range(4):
        out = jnp.dot(swap, f_ref[g * rows : (g + 1) * rows, :], preferred_element_type=F32).astype(BF16)
        for k in range(local):
            f_by[k, g * 16 : g * 16 + 16, :] = out[k * 16 : k * 16 + 16]

    for i in range(n_parts):
        at = slice(i * width, (i + 1) * width)
        for b in range(n_chunks):
            copy(b, i).wait()
        for c in range(0, block_c, 16):
            held[0, :, c : c + 16, at] = separate(raw[c * local : (c + 16) * local, at], local)
        for b in (*range(1, n_chunks), 0):
            for k in range(local):
                part = lax.dot_general(f_by[k, :, at], held[b, k, :, at], NT, preferred_element_type=F32)
                sums[b, k] = part if i == 0 else sums[b, k] + part

    tables.wait()
    for b in range(n_chunks):
        at = slice(b * block_c, (b + 1) * block_c)
        u = [sums[b, k].astype(BF16) for k in range(local)]
        for g in range(2):
            block = jnp.concatenate([x[g * 32 : g * 32 + 32] for x in u], axis=0)
            out = jnp.dot(k_parts[0], block, preferred_element_type=F32) + jnp.dot(
                k_parts[1], block, preferred_element_type=F32
            )
            out = out.reshape(2 * half, 16, block_c)
            keep_ref[:, g * 16 : g * 16 + 16, at] = out[:half]
            send_ref[:, g * 16 : g * 16 + 16, at] = out[half:].astype(BF16)


def gram_kernel(keep_ref, got_ref, mine_ref, gram_ref):
    mine = keep_ref[...] + got_ref[...].astype(F32)
    mine_ref[...] = mine
    gram = jnp.zeros((P_SIZE, P_SIZE), F32)
    for j in range(mine.shape[0]):
        gram += lax.dot_general(
            mine[j], mine[j], NT, preferred_element_type=F32, precision=lax.Precision.HIGHEST
        )
    gram = jnp.concatenate([gram[8 * i : 8 * i + 8] for i in range(P_SIZE // 8)], axis=1)
    for i in range(gram_ref.shape[0]):
        gram_ref[i] = gram


def last_kernel(factor, gram_ref, mine_ref, out_ref):
    total = jnp.sum(gram_ref[...], axis=0)
    gram = jnp.concatenate([total[:, P_SIZE * i : P_SIZE * (i + 1)] for i in range(P_SIZE // 8)], axis=0)
    row = lax.broadcasted_iota(jnp.int32, (P_SIZE, P_SIZE), 0)
    col = lax.broadcasted_iota(jnp.int32, (P_SIZE, P_SIZE), 1)
    eye = jnp.where(row == col, 1.0, 0.0).astype(F32)
    scale = jnp.sum(gram * eye, keepdims=True) + 1e-06

    def dot(a, b):
        return jnp.dot(a, b, preferred_element_type=F32, precision=lax.Precision.HIGH)

    current = gram / scale
    inverse = eye
    for _ in range(NSTEPS):
        weight = 1.5 * eye - 0.5 * dot(inverse, current)
        current = dot(current, weight)
        inverse = dot(weight, inverse)
    inverse = inverse * (factor / jnp.sqrt(scale))
    for j in range(mine_ref.shape[0]):
        out_ref[j] = lax.dot_general(
            inverse,
            mine_ref[j],
            (((0,), (0,)), ((), ())),
            preferred_element_type=F32,
            precision=lax.Precision.HIGHEST,
        )


def vmem(n):
    return [pl.BlockSpec(memory_space=pltpu.VMEM)] * n


def shards(damping, block_seeds, n_row, n_col):
    cols, local, m = damping.shape
    n_blocks = block_seeds.shape[0]
    n_freq = local * n_row
    channels = 2 * local
    n_dev = n_row * n_col
    amp = math.sqrt(2.0 / n_freq) / math.sqrt(n_blocks * m)
    most, large, params = (pltpu.CompilerParams(vmem_limit_bytes=x << 20) for x in (54, 44, 20))

    block_c = 256 if cols % 256 == 0 else cols
    lanes_c = 128 if block_c % 128 == 0 else block_c
    lane_w = 128 if m % 128 == 0 else m
    per_pass = 2 if m % (2 * lane_w) == 0 else 1
    halves_m = 2 if m % (4 * lane_w) == 0 else 1
    flat = damping.reshape(cols * local, m)

    w_row = channel_table(n_freq, np.arange(n_freq), np.arange(n_blocks), n_blocks)
    w_row = w_row.reshape(n_row, local, 2, n_blocks).transpose(0, 2, 1, 3)
    sign = np.array([1.0, -1.0])[None, :, None, None] * amp
    per_owner, half, quarter = n_blocks // n_row, n_blocks // 2, n_row // 4

    n_rows = P_SIZE * channels
    whole = lambda *s: pl.BlockSpec(s, lambda i: (0,) * len(s))
    v_one = pl.BlockSpec(memory_space=pltpu.VMEM)
    work = 2 * cols * local * m
    t = pl.pallas_call(
        lambda *refs: forward_kernel(local, n_freq, *refs),
        out_shape=jax.ShapeDtypeStruct((P_SIZE, channels, m), BF16),
        in_specs=[pl.BlockSpec(memory_space=pl.ANY)] * 2,
        out_specs=v_one,
        scratch_shapes=[
            pltpu.VMEM((cols // block_c, block_c * local, m), BF16),
            pltpu.VMEM((2, local, block_c, per_pass * lane_w), BF16),
            pltpu.VMEM((m // lane_w, P_SIZE // 4, 8 * local, lane_w), F32),
            pltpu.VMEM((P_SIZE * n_blocks, block_c), BF16),
            pltpu.VMEM((P_SIZE, n_blocks, lanes_c), F32),
            pltpu.VMEM((P_SIZE, n_blocks, lanes_c), F32),
            pltpu.VMEM((4, n_blocks, lanes_c), F32),
            pltpu.VMEM((2, channels * 8, 8 * n_blocks), BF16),
            pltpu.VMEM((2, local, 2 * P_SIZE, block_c), BF16),
            pltpu.SMEM((n_blocks,), jnp.int32),
            pltpu.SemaphoreType.DMA((cols // block_c, halves_m)),
            pltpu.SemaphoreType.DMA,
        ],
        compiler_params=large,
        cost_estimate=pl.CostEstimate(flops=64 * work, bytes_accessed=work, transcendentals=0),
        name="forward",
    )(block_seeds, flat)
    n_grp = n_dev // 2
    n_p = math.gcd(P_SIZE, n_grp)
    n_r = n_grp // n_p
    p_own, lanes = P_SIZE // n_p, m // n_r
    halves = [list(range(n_grp)), list(range(n_grp, n_dev))]
    across = [(i, (i + n_row // 2) % n_row) for i in range(n_row)]
    t = t.reshape(n_p, p_own * channels, n_r, lanes).transpose(0, 2, 1, 3)
    t = t.reshape(n_grp, p_own * channels, lanes)
    t = lax.all_to_all(t, ("row", "col"), 0, 0, axis_index_groups=halves, tiled=True)
    t = t.reshape(n_grp, p_own, channels, lanes)

    merge = (w_row * sign).reshape(2, n_row // 2, 1, channels, n_blocks).repeat(n_col, axis=2)
    merge = merge.reshape(2, n_grp * channels, n_blocks).transpose(0, 2, 1)
    merge = np.concatenate(high_low(merge), axis=1)
    b_hi, b_lo = high_low(w_row.reshape(2, n_row // 2 * channels, n_blocks))
    fan = np.concatenate([b_hi, b_hi, b_lo], axis=2)
    keep, send = pl.pallas_call(
        lambda *refs: gather_kernel(n_row, *refs),
        out_shape=(
            jax.ShapeDtypeStruct((p_own, n_blocks, lanes), F32),
            jax.ShapeDtypeStruct((p_own, n_blocks, lanes), BF16),
        ),
        in_specs=vmem(2),
        out_specs=tuple(vmem(2)),
        compiler_params=params,
        name="gather",
    )(jnp.asarray(merge), t)
    send, flat = lax.optimization_barrier((send, flat))
    got = lax.ppermute(send, "row", across)
    n_ready = cols // block_c - 1 if m % 256 == 0 else 0
    k_tables = pl.pallas_call(
        lambda *refs: blocks_kernel(local, n_row, n_blocks, amp, *refs),
        out_shape=jax.ShapeDtypeStruct((2, n_blocks * 16, channels * 16), BF16),
        in_specs=[],
        out_specs=v_one,
        compiler_params=params,
        cost_estimate=pl.CostEstimate(flops=10**9, bytes_accessed=10**6, transcendentals=0),
        name="blocks",
    )()
    ready = []
    if n_ready:
        ready.append(
            pl.pallas_call(
                lambda *refs: separate_kernel(local, *refs),
                grid=(2 * n_ready,),
                out_shape=jax.ShapeDtypeStruct((local, n_ready * block_c, m), BF16),
                in_specs=[pl.BlockSpec((block_c // 2 * local, m), lambda i: (i + 2, 0))],
                out_specs=pl.BlockSpec((local, block_c // 2, m), lambda i: (0, i, 0)),
                compiler_params=most,
                cost_estimate=pl.CostEstimate(flops=work, bytes_accessed=2 * work, transcendentals=0),
                name="separate",
            )(flat)
        )
    got, k_tables, *ready = lax.optimization_barrier((got, k_tables, *ready))
    f = pl.pallas_call(
        lambda *refs: scatter_kernel(n_row, *refs),
        out_shape=jax.ShapeDtypeStruct((n_row // 2, n_col, p_own, channels, lanes), BF16),
        in_specs=vmem(3),
        out_specs=v_one,
        compiler_params=params,
        name="scatter",
    )(jnp.asarray(fan), keep, got)
    f = f.reshape(n_grp, p_own * channels, lanes)
    f = lax.all_to_all(f, ("row", "col"), 0, 0, axis_index_groups=halves, tiled=True)
    f = f.reshape(n_p, n_r, p_own * channels, lanes).transpose(0, 2, 1, 3).reshape(n_rows, m)

    n_parts = m // 256 if m % 256 == 0 else 1
    n_chunks = n_ready + 1
    deep = cols // n_chunks
    keep, send = pl.pallas_call(
        lambda *refs: backward_kernel(local, n_blocks, n_ready, *refs),
        out_shape=(
            jax.ShapeDtypeStruct((half, P_SIZE, cols), F32),
            jax.ShapeDtypeStruct((half, P_SIZE, cols), BF16),
        ),
        in_specs=vmem(1) + [pl.BlockSpec(memory_space=pl.ANY)] * (2 + len(ready)),
        out_specs=tuple(vmem(2)),
        scratch_shapes=[
            pltpu.VMEM((deep * local, m), BF16),
            pltpu.VMEM((n_chunks, local, deep, m), BF16),
            pltpu.VMEM((n_chunks, local, 2 * P_SIZE, deep), F32),
            pltpu.VMEM((local, 2 * P_SIZE, m), BF16),
            pltpu.VMEM((2, n_blocks * 16, channels * 16), BF16),
            pltpu.SemaphoreType.DMA((n_chunks, n_parts)),
            pltpu.SemaphoreType.DMA,
        ],
        compiler_params=large,
        cost_estimate=pl.CostEstimate(flops=64 * work, bytes_accessed=work, transcendentals=0),
        name="backward",
    )(f, k_tables, flat, *ready)
    got = lax.ppermute(send, "row", [(i, i ^ 1) for i in range(n_row)])
    summed = (keep + got.astype(F32)).astype(BF16)
    groups = [[core + 2 * (i + quarter * h) for i in range(quarter)] for h in range(2) for core in range(2)]
    summed = lax.all_to_all(summed, "row", 0, 0, axis_index_groups=groups, tiled=True)
    summed = summed.reshape(quarter, 2, per_owner, P_SIZE, cols)
    keep, send = pl.pallas_call(
        join_kernel,
        out_shape=(
            jax.ShapeDtypeStruct((per_owner, P_SIZE, cols), F32),
            jax.ShapeDtypeStruct((per_owner, P_SIZE, cols), BF16),
        ),
        in_specs=vmem(1),
        out_specs=tuple(vmem(2)),
        compiler_params=params,
        name="join",
    )(summed)
    got = lax.ppermute(send, "row", across)

    mine, gram = pl.pallas_call(
        gram_kernel,
        out_shape=(
            jax.ShapeDtypeStruct((per_owner, P_SIZE, cols), F32),
            jax.ShapeDtypeStruct((n_dev, 8, 4 * P_SIZE), F32),
        ),
        in_specs=vmem(2),
        out_specs=tuple(vmem(2)),
        compiler_params=params,
        name="gram",
    )(keep, got)
    gram = lax.all_to_all(gram, ("row", "col"), 0, 0, tiled=True)
    out = pl.pallas_call(
        lambda *refs: last_kernel(math.sqrt(n_blocks * m), *refs),
        out_shape=jax.ShapeDtypeStruct((per_owner, P_SIZE, cols), F32),
        in_specs=vmem(2),
        out_specs=vmem(1)[0],
        compiler_params=params,
        name="last",
    )(gram, mine)
    return out.transpose(0, 2, 1)


def solution(mesh):
    n_row, n_col = mesh.shape["row"], mesh.shape["col"]
    return jax.shard_map(
        lambda damping, block_seeds: shards(damping, block_seeds, n_row, n_col),
        mesh=mesh,
        in_specs=(P("col", "row", None), P()),
        out_specs=P("row", "col", None),
        check_vma=False,
    )
```

```python
import math

import numpy as np
import jax
import jax.numpy as jnp
from jax import lax
from jax.experimental import pallas as pl
from jax.experimental.pallas import tpu as pltpu
from jax.sharding import PartitionSpec as P

NSTEPS = 12
PRIME = 65521
P_SIZE = 32
BF16 = jnp.bfloat16
F32 = jnp.float32
NT = (((1,), (1,)), ((), ()))


def channel_table(n_freq, freqs, steps, n_blocks):
    angle = math.pi * (np.asarray(freqs)[:, None] + 0.5) / n_freq * np.asarray(steps)[None, :]
    decay = 3.0 ** (-np.asarray(steps) / n_blocks)
    return np.stack([decay * np.cos(angle), decay * np.sin(angle)], axis=1)


def high_low(values):
    high = values.astype(np.float32).astype(jnp.bfloat16)
    low = (values - high.astype(np.float64)).astype(np.float32).astype(jnp.bfloat16)
    return high, low


def _fit(fn, degree):
    nodes = np.cos(np.pi * (np.arange(64) + 0.5) / 64)
    u = (nodes + 1.0) / 128
    series = np.polynomial.chebyshev.Chebyshev.fit(u, fn(np.sqrt(u)), degree, domain=[0.0, 1 / 64])
    return [float(x) for x in series.convert(kind=np.polynomial.Polynomial, domain=[-1, 1], window=[-1, 1]).coef]


COS_COEFS = _fit(lambda t: np.cos(2 * np.pi * t), 5)
SIN_COEFS = _fit(lambda t: np.sin(2 * np.pi * t) / t, 5)


def polynomial(coefs, u):
    out = jnp.full_like(u, coefs[-1])
    for coef in coefs[-2::-1]:
        out = out * u + coef
    return out


def cos_sin(turns):
    quarter = jnp.round(turns * 4.0)
    rest = turns - quarter * 0.25
    u = rest * rest
    cos, sin = polynomial(COS_COEFS, u), polynomial(SIN_COEFS, u) * rest
    odd = jnp.abs(quarter) == 1.0
    far = jnp.abs(quarter) == 2.0
    flip_cos = jnp.logical_or(quarter == 1.0, far)
    flip_sin = jnp.logical_or(quarter == -1.0, far)
    out_cos, out_sin = jnp.where(odd, sin, cos), jnp.where(odd, cos, sin)
    return jnp.where(flip_cos, -out_cos, out_cos), jnp.where(flip_sin, -out_sin, out_sin)


def mod_turns(x):
    return (x - jnp.round(x * (1.0 / PRIME)) * float(PRIME)) * (1.0 / PRIME)


def channel_values(n_freq, n_blocks, freq, step, sine):
    turns = ((2 * freq + 1) * step % (4 * n_freq)).astype(F32) * (0.25 / n_freq)
    cos, sin = cos_sin(turns - jnp.round(turns))
    values = jnp.where(sine, sin, cos) * jnp.exp(step.astype(F32) * (-math.log(3.0) / n_blocks))
    return values


def split(values):
    high = values.astype(BF16).astype(F32)
    return high, values - high


def separate(x, local):
    return jnp.swapaxes(x.reshape(x.shape[0] // local, local, x.shape[1]), 0, 1)


def iotas(rows, cols):
    return (lax.broadcasted_iota(jnp.int32, (rows, cols), d) for d in range(2))


def place(rows, cols, test):
    r = lax.broadcasted_iota(jnp.int32, (rows, cols), 0)
    c = lax.broadcasted_iota(jnp.int32, (rows, cols), 1)
    return test(r, c).astype(F32)


def less_turns(x):
    return x - (x.astype(F32) * (1.0 / PRIME)).astype(jnp.int32) * PRIME


def forward_kernel(local, n_freq, seeds_ref, d_ref, t_ref, held, by_freq, acc, probes, cos_shift, sin_shift, state, spread, q_all, own, sems, sem):
    n_chunks, rows, m = held.shape
    block_c = rows // local
    channels = 2 * local
    n_blocks, lanes = cos_shift.shape[1:]
    group = 8
    tiles = P_SIZE // 8
    width, lane_w = by_freq.shape[3], acc.shape[3]
    passes, per_pass = m // width, width // lane_w

    n_parts = sems.shape[1]

    def copy(b, i):
        part = (slice(b * rows, (b + 1) * rows), slice(i * m // n_parts, (i + 1) * m // n_parts))
        return pltpu.make_async_copy(d_ref.at[part], held.at[b, :, part[1]], sems.at[b, i])

    fetch = pltpu.make_async_copy(seeds_ref, own, sem)
    fetch.start()
    for b in range(n_chunks):
        for i in range(n_parts):
            copy(b, i).start()

    row, col = iotas(channels, n_blocks)
    table = channel_values(n_freq, n_blocks, lax.axis_index("row") * local + row % local, col, row >= local)
    left = place(channels * group, channels, lambda r, c: r // group == c)
    right = place(n_blocks, group * n_blocks, lambda r, c: r == c % n_blocks)
    same = place(channels * group, group * n_blocks, lambda r, c: r % group == c // n_blocks)
    for part, w in enumerate(split(table)):
        w = jnp.dot(w, right, preferred_element_type=F32)
        spread[part] = (jnp.dot(left, w, preferred_element_type=F32) * same).astype(BF16)

    fetch.wait()
    line, lane = iotas(n_blocks, lanes)
    seeds = jnp.zeros((n_blocks, lanes), jnp.int32)
    for j in range(n_blocks):
        seeds = jnp.where(line == j, own[j], seeds)
    steps = (lane + 1).astype(F32)
    shift = mod_turns(seeds.astype(F32) * steps) * float(PRIME)
    shift_parts = cos_sin(mod_turns(jnp.round(shift) * (steps + 1.0)))
    for p in range(P_SIZE):
        for part, out in zip(shift_parts, (cos_shift, sin_shift)):
            out[p] = jnp.broadcast_to(part[:, p : p + 1], (n_blocks, lanes))

    start = lax.axis_index("col") * (n_chunks * block_c)
    spans = [(at, p) for at in range(0, block_c, lanes) for p in range(0, P_SIZE, 8)]

    def make_probes(b, span):
        at, first = span
        if first == 0:
            column = start + b * block_c + at + lane
            inner = less_turns(less_turns(seeds * (column + 1)) * (column + 3)).astype(F32)
            turn_cos, turn_sin = cos_sin(mod_turns(inner))
            cos, sin = turn_cos, turn_sin
        else:
            cos, sin, turn_cos, turn_sin = (state[i] for i in range(4))
        for p in range(first, first + 8):
            value = cos * cos_shift[p] - sin * sin_shift[p]
            probes[p * n_blocks : (p + 1) * n_blocks, at : at + lanes] = value.astype(BF16)
            cos, sin = cos * turn_cos - sin * turn_sin, sin * turn_cos + cos * turn_sin
        for i, x in enumerate((cos, sin, turn_cos, turn_sin)):
            state[i] = x

    def make_channels(b):
        for g in range(P_SIZE // group):
            block = probes[g * group * n_blocks : (g + 1) * group * n_blocks, :]
            q = jnp.dot(spread[0], block, preferred_element_type=F32) + jnp.dot(
                spread[1], block, preferred_element_type=F32
            )
            q = q.astype(BF16)
            for part in range(2):
                for k in range(local):
                    at = (part * local + k) * group
                    to = part * P_SIZE + g * group
                    q_all[b % 2, k, to : to + group, :] = q[at : at + group]

    for span in spans:
        make_probes(0, span)
    make_channels(0)
    for b in range(n_chunks):
        for i in range(passes):
            if i * n_parts % passes == 0:
                copy(b, i * n_parts // passes).wait()
            if b + 1 < n_chunks:
                for span in spans[len(spans) * i // passes : len(spans) * (i + 1) // passes]:
                    make_probes(b + 1, span)
            at = slice(i * width, (i + 1) * width)
            for c in range(0, block_c, 16):
                by_freq[i % 2, :, c : c + 16, :] = separate(held[b, c * local : (c + 16) * local, at], local)
            for k in range(local):
                o = jnp.dot(q_all[b % 2, k], by_freq[i % 2, k], preferred_element_type=F32)
                for l in range(per_pass):
                    for t in range(2 * tiles):
                        piece = o[t * 8 : t * 8 + 8, l * lane_w : (l + 1) * lane_w]
                        if b > 0:
                            piece += acc[i * per_pass + l, t, k * 8 : k * 8 + 8, :]
                        acc[i * per_pass + l, t, k * 8 : k * 8 + 8, :] = piece
            if b + 1 == n_chunks:
                for l in range(i * per_pass, (i + 1) * per_pass):
                    for p in range(P_SIZE):
                        t = jnp.concatenate(
                            [acc[l, part * tiles + p // 8, pl.ds(p % 8, local, stride=8), :] for part in range(2)],
                            axis=0,
                        )
                        t_ref[p, :, l * lane_w : (l + 1) * lane_w] = t.astype(BF16)
        if b + 1 < n_chunks:
            make_channels(b + 1)


def half_of(n_row):
    return lax.axis_index("row") // (n_row // 2)


def gather_kernel(n_row, c_ref, x_ref, keep_ref, send_ref):
    n_src, p_own, channels, lanes = x_ref.shape
    table = c_ref[half_of(n_row)]
    n = table.shape[0] // 2
    for p in range(p_own):
        x = x_ref[:, p].reshape(n_src * channels, lanes)
        both = jnp.dot(table, x, preferred_element_type=F32)
        out = both[:n] + both[n:]
        keep_ref[p] = out
        send_ref[p] = out.astype(BF16)


def scatter_kernel(n_row, b_ref, keep_ref, got_ref, f_ref):
    n_rows, n_cols, p_own, channels, lanes = f_ref.shape
    table = b_ref[half_of(n_row)]
    for p in range(p_own):
        forward = keep_ref[p] + got_ref[p].astype(F32)
        high = forward.astype(BF16)
        low = (forward - high.astype(F32)).astype(BF16)
        out = jnp.dot(table, jnp.concatenate([high, low, high], axis=0), preferred_element_type=F32)
        out = out.astype(BF16).reshape(n_rows, channels, lanes)
        for col in range(n_cols):
            f_ref[:, col, p] = out


def join_kernel(x_ref, keep_ref, send_ref):
    x = x_ref[...].astype(F32)
    total = jnp.sum(x, axis=0)
    keep_ref[...] = total[0]
    send_ref[...] = total[1].astype(BF16)


def blocks_kernel(local, n_row, n_blocks, amp, k_ref):
    channels = 2 * local
    row_at = lax.axis_index("row")
    half, per_owner, quarter = n_blocks // 2, n_blocks // n_row, n_row // 4
    r, c = iotas(n_blocks, channels)
    rest = r % half
    chip = rest // (2 * per_owner) + quarter * ((rest // per_owner + half_of(n_row)) % 2)
    block_at = (2 * chip + (r // half + row_at) % 2) * per_owner + rest % per_owner
    sine = c % 2 == 1
    table = channel_values(local * n_row, n_blocks, row_at * local + c // 2, block_at + 1, sine)
    table = table * jnp.where(sine, -amp, amp)
    left = place(n_blocks * 16, n_blocks, lambda r, c: r // 16 == c)
    right = place(channels, channels * 16, lambda r, c: r == c // 32 * 2 + c // 8 % 2)
    same = place(n_blocks * 16, channels * 16, lambda r, c: r % 16 == c // 16 % 2 * 8 + c % 8)
    for part, k in enumerate(split(table)):
        k = jnp.dot(left, jnp.dot(k, right, preferred_element_type=F32), preferred_element_type=F32)
        k_ref[part] = (k * same).astype(BF16)


def separate_kernel(local, d_ref, o_ref):
    rows, m = d_ref.shape
    for i in range(0, m, 256):
        for c in range(0, rows // local, 16):
            piece = d_ref[c * local : (c + 16) * local, i : i + 256]
            o_ref[:, c : c + 16, i : i + 256] = separate(piece, local)


def backward_kernel(local, n_blocks, n_ready, f_ref, k_ref, d_ref, *refs):
    ready_ref = refs[0] if n_ready else None
    keep_ref, send_ref, raw, held, sums, f_by, k_parts, sems, sem = refs[bool(n_ready) :]
    n_chunks, _, block_c, m = held.shape
    n_raw, n_parts = n_chunks - n_ready, sems.shape[1]
    width = m // n_parts
    step = 256 if width % 256 == 0 else width
    tall = block_c * local
    rows = f_ref.shape[0] // 4
    half = n_blocks // 2

    def copy(b, i):
        at = slice(i * width, (i + 1) * width)
        if b < n_raw:
            return pltpu.make_async_copy(d_ref.at[pl.ds(b * tall, tall), at], raw.at[b, :, at], sems.at[b, i])
        source = ready_ref.at[:, pl.ds((b - n_raw) * block_c, block_c), at]
        return pltpu.make_async_copy(source, held.at[b, :, :, at], sems.at[b, i])

    tables = pltpu.make_async_copy(k_ref, k_parts, sem)
    order = (*range(n_raw, n_chunks), *range(n_raw))
    for i in range(n_parts):
        for b in order:
            copy(b, i).start()
    tables.start()

    swap = place(rows, rows, lambda r, c: (r % 8 * 2 + r // 8 % 2) * local + r // 16 == c).astype(BF16)
    for g in range(4):
        out = jnp.dot(swap, f_ref[g * rows : (g + 1) * rows, :], preferred_element_type=F32).astype(BF16)
        for k in range(local):
            f_by[k, g * 16 : g * 16 + 16, :] = out[k * 16 : k * 16 + 16]

    for i in range(n_parts):
        at = slice(i * width, (i + 1) * width)
        for b in order:
            copy(b, i).wait()
            for p in range(i * width, (i + 1) * width, step) if b < n_raw else ():
                for c in range(0, block_c, 16):
                    piece = raw[b, c * local : (c + 16) * local, p : p + step]
                    held[b, :, c : c + 16, p : p + step] = separate(piece, local)
            for k in range(local):
                part = lax.dot_general(f_by[k, :, at], held[b, k, :, at], NT, preferred_element_type=F32)
                sums[b, k] = part if i == 0 else sums[b, k] + part

    tables.wait()
    for b in range(n_chunks):
        at = slice(b * block_c, (b + 1) * block_c)
        u = [sums[b, k].astype(BF16) for k in range(local)]
        for g in range(2):
            block = jnp.concatenate([x[g * 32 : g * 32 + 32] for x in u], axis=0)
            out = jnp.dot(k_parts[0], block, preferred_element_type=F32) + jnp.dot(
                k_parts[1], block, preferred_element_type=F32
            )
            out = out.reshape(2 * half, 16, block_c)
            keep_ref[:, g * 16 : g * 16 + 16, at] = out[:half]
            send_ref[:, g * 16 : g * 16 + 16, at] = out[half:].astype(BF16)


def gram_kernel(keep_ref, got_ref, mine_ref, gram_ref):
    mine = keep_ref[...] + got_ref[...].astype(F32)
    mine_ref[...] = mine
    gram = jnp.zeros((P_SIZE, P_SIZE), F32)
    for j in range(mine.shape[0]):
        gram += lax.dot_general(
            mine[j], mine[j], NT, preferred_element_type=F32, precision=lax.Precision.HIGHEST
        )
    gram = jnp.concatenate([gram[8 * i : 8 * i + 8] for i in range(P_SIZE // 8)], axis=1)
    for i in range(gram_ref.shape[0]):
        gram_ref[i] = gram


def last_kernel(factor, gram_ref, mine_ref, out_ref):
    total = jnp.sum(gram_ref[...], axis=0)
    gram = jnp.concatenate([total[:, P_SIZE * i : P_SIZE * (i + 1)] for i in range(P_SIZE // 8)], axis=0)
    row = lax.broadcasted_iota(jnp.int32, (P_SIZE, P_SIZE), 0)
    col = lax.broadcasted_iota(jnp.int32, (P_SIZE, P_SIZE), 1)
    eye = jnp.where(row == col, 1.0, 0.0).astype(F32)
    scale = jnp.sum(gram * eye, keepdims=True) + 1e-06

    def dot(a, b):
        return jnp.dot(a, b, preferred_element_type=F32, precision=lax.Precision.HIGH)

    current = gram / scale
    inverse = eye
    for _ in range(NSTEPS):
        weight = 1.5 * eye - 0.5 * dot(inverse, current)
        current = dot(current, weight)
        inverse = dot(weight, inverse)
    inverse = inverse * (factor / jnp.sqrt(scale))
    for j in range(mine_ref.shape[0]):
        out_ref[j] = lax.dot_general(
            inverse,
            mine_ref[j],
            (((0,), (0,)), ((), ())),
            preferred_element_type=F32,
            precision=lax.Precision.HIGHEST,
        )


def vmem(n):
    return [pl.BlockSpec(memory_space=pltpu.VMEM)] * n


def shards(damping, block_seeds, n_row, n_col):
    cols, local, m = damping.shape
    n_blocks = block_seeds.shape[0]
    n_freq = local * n_row
    channels = 2 * local
    n_dev = n_row * n_col
    amp = math.sqrt(2.0 / n_freq) / math.sqrt(n_blocks * m)
    most, large, params = (pltpu.CompilerParams(vmem_limit_bytes=x << 20) for x in (54, 46, 20))

    block_c = 256 if cols % 256 == 0 else cols
    lanes_c = 128 if block_c % 128 == 0 else block_c
    lane_w = 128 if m % 128 == 0 else m
    per_pass = 2 if m % (2 * lane_w) == 0 else 1
    halves_m = 2 if m % (4 * lane_w) == 0 else 1
    flat = damping.reshape(cols * local, m)

    w_row = channel_table(n_freq, np.arange(n_freq), np.arange(n_blocks), n_blocks)
    w_row = w_row.reshape(n_row, local, 2, n_blocks).transpose(0, 2, 1, 3)
    sign = np.array([1.0, -1.0])[None, :, None, None] * amp
    per_owner, half, quarter = n_blocks // n_row, n_blocks // 2, n_row // 4

    n_rows = P_SIZE * channels
    whole = lambda *s: pl.BlockSpec(s, lambda i: (0,) * len(s))
    v_one = pl.BlockSpec(memory_space=pltpu.VMEM)
    work = 2 * cols * local * m
    t = pl.pallas_call(
        lambda *refs: forward_kernel(local, n_freq, *refs),
        out_shape=jax.ShapeDtypeStruct((P_SIZE, channels, m), BF16),
        in_specs=[pl.BlockSpec(memory_space=pl.ANY)] * 2,
        out_specs=v_one,
        scratch_shapes=[
            pltpu.VMEM((cols // block_c, block_c * local, m), BF16),
            pltpu.VMEM((2, local, block_c, per_pass * lane_w), BF16),
            pltpu.VMEM((m // lane_w, P_SIZE // 4, 8 * local, lane_w), F32),
            pltpu.VMEM((P_SIZE * n_blocks, block_c), BF16),
            pltpu.VMEM((P_SIZE, n_blocks, lanes_c), F32),
            pltpu.VMEM((P_SIZE, n_blocks, lanes_c), F32),
            pltpu.VMEM((4, n_blocks, lanes_c), F32),
            pltpu.VMEM((2, channels * 8, 8 * n_blocks), BF16),
            pltpu.VMEM((2, local, 2 * P_SIZE, block_c), BF16),
            pltpu.SMEM((n_blocks,), jnp.int32),
            pltpu.SemaphoreType.DMA((cols // block_c, halves_m)),
            pltpu.SemaphoreType.DMA,
        ],
        compiler_params=large,
        cost_estimate=pl.CostEstimate(flops=64 * work, bytes_accessed=work, transcendentals=0),
        name="forward",
    )(block_seeds, flat)
    n_grp = n_dev // 2
    n_p = math.gcd(P_SIZE, n_grp)
    n_r = n_grp // n_p
    p_own, lanes = P_SIZE // n_p, m // n_r
    halves = [list(range(n_grp)), list(range(n_grp, n_dev))]
    across = [(i, (i + n_row // 2) % n_row) for i in range(n_row)]
    t = t.reshape(n_p, p_own * channels, n_r, lanes).transpose(0, 2, 1, 3)
    t = t.reshape(n_grp, p_own * channels, lanes)
    t = lax.all_to_all(t, ("row", "col"), 0, 0, axis_index_groups=halves, tiled=True)
    t = t.reshape(n_grp, p_own, channels, lanes)

    merge = (w_row * sign).reshape(2, n_row // 2, 1, channels, n_blocks).repeat(n_col, axis=2)
    merge = merge.reshape(2, n_grp * channels, n_blocks).transpose(0, 2, 1)
    merge = np.concatenate(high_low(merge), axis=1)
    b_hi, b_lo = high_low(w_row.reshape(2, n_row // 2 * channels, n_blocks))
    fan = np.concatenate([b_hi, b_hi, b_lo], axis=2)
    keep, send = pl.pallas_call(
        lambda *refs: gather_kernel(n_row, *refs),
        out_shape=(
            jax.ShapeDtypeStruct((p_own, n_blocks, lanes), F32),
            jax.ShapeDtypeStruct((p_own, n_blocks, lanes), BF16),
        ),
        in_specs=vmem(2),
        out_specs=tuple(vmem(2)),
        compiler_params=params,
        name="gather",
    )(jnp.asarray(merge), t)
    send, flat = lax.optimization_barrier((send, flat))
    got = lax.ppermute(send, "row", across)
    n_ready = (cols // block_c) // 2 if m % 256 == 0 else 0
    n_raw = cols // block_c - n_ready
    k_tables = pl.pallas_call(
        lambda *refs: blocks_kernel(local, n_row, n_blocks, amp, *refs),
        out_shape=jax.ShapeDtypeStruct((2, n_blocks * 16, channels * 16), BF16),
        in_specs=[],
        out_specs=v_one,
        compiler_params=params,
        cost_estimate=pl.CostEstimate(flops=10**9, bytes_accessed=10**6, transcendentals=0),
        name="blocks",
    )()
    ready = []
    if n_ready:
        ready.append(
            pl.pallas_call(
                lambda *refs: separate_kernel(local, *refs),
                grid=(2 * n_ready,),
                out_shape=jax.ShapeDtypeStruct((local, n_ready * block_c, m), BF16),
                in_specs=[pl.BlockSpec((block_c // 2 * local, m), lambda i: (i + 2 * n_raw, 0))],
                out_specs=pl.BlockSpec((local, block_c // 2, m), lambda i: (0, i, 0)),
                compiler_params=most,
                cost_estimate=pl.CostEstimate(flops=work, bytes_accessed=2 * work, transcendentals=0),
                name="separate",
            )(flat)
        )
    got, k_tables, *ready = lax.optimization_barrier((got, k_tables, *ready))
    f = pl.pallas_call(
        lambda *refs: scatter_kernel(n_row, *refs),
        out_shape=jax.ShapeDtypeStruct((n_row // 2, n_col, p_own, channels, lanes), BF16),
        in_specs=vmem(3),
        out_specs=v_one,
        compiler_params=params,
        name="scatter",
    )(jnp.asarray(fan), keep, got)
    f = f.reshape(n_grp, p_own * channels, lanes)
    f = lax.all_to_all(f, ("row", "col"), 0, 0, axis_index_groups=halves, tiled=True)
    f = f.reshape(n_p, n_r, p_own * channels, lanes).transpose(0, 2, 1, 3).reshape(n_rows, m)

    n_parts = 3 if m % 768 == 0 else 1
    n_chunks = n_raw + n_ready
    deep = cols // n_chunks
    keep, send = pl.pallas_call(
        lambda *refs: backward_kernel(local, n_blocks, n_ready, *refs),
        out_shape=(
            jax.ShapeDtypeStruct((half, P_SIZE, cols), F32),
            jax.ShapeDtypeStruct((half, P_SIZE, cols), BF16),
        ),
        in_specs=vmem(1) + [pl.BlockSpec(memory_space=pl.ANY)] * (2 + len(ready)),
        out_specs=tuple(vmem(2)),
        scratch_shapes=[
            pltpu.VMEM((n_raw, deep * local, m), BF16),
            pltpu.VMEM((n_chunks, local, deep, m), BF16),
            pltpu.VMEM((n_chunks, local, 2 * P_SIZE, deep), F32),
            pltpu.VMEM((local, 2 * P_SIZE, m), BF16),
            pltpu.VMEM((2, n_blocks * 16, channels * 16), BF16),
            pltpu.SemaphoreType.DMA((n_chunks, n_parts)),
            pltpu.SemaphoreType.DMA,
        ],
        compiler_params=large,
        cost_estimate=pl.CostEstimate(flops=64 * work, bytes_accessed=work, transcendentals=0),
        name="backward",
    )(f, k_tables, flat, *ready)
    got = lax.ppermute(send, "row", [(i, i ^ 1) for i in range(n_row)])
    summed = (keep + got.astype(F32)).astype(BF16)
    groups = [[core + 2 * (i + quarter * h) for i in range(quarter)] for h in range(2) for core in range(2)]
    summed = lax.all_to_all(summed, "row", 0, 0, axis_index_groups=groups, tiled=True)
    summed = summed.reshape(quarter, 2, per_owner, P_SIZE, cols)
    keep, send = pl.pallas_call(
        join_kernel,
        out_shape=(
            jax.ShapeDtypeStruct((per_owner, P_SIZE, cols), F32),
            jax.ShapeDtypeStruct((per_owner, P_SIZE, cols), BF16),
        ),
        in_specs=vmem(1),
        out_specs=tuple(vmem(2)),
        compiler_params=params,
        name="join",
    )(summed)
    got = lax.ppermute(send, "row", across)

    mine, gram = pl.pallas_call(
        gram_kernel,
        out_shape=(
            jax.ShapeDtypeStruct((per_owner, P_SIZE, cols), F32),
            jax.ShapeDtypeStruct((n_dev, 8, 4 * P_SIZE), F32),
        ),
        in_specs=vmem(2),
        out_specs=tuple(vmem(2)),
        compiler_params=params,
        name="gram",
    )(keep, got)
    gram = lax.all_to_all(gram, ("row", "col"), 0, 0, tiled=True)
    out = pl.pallas_call(
        lambda *refs: last_kernel(math.sqrt(n_blocks * m), *refs),
        out_shape=jax.ShapeDtypeStruct((per_owner, P_SIZE, cols), F32),
        in_specs=vmem(2),
        out_specs=vmem(1)[0],
        compiler_params=params,
        name="last",
    )(gram, mine)
    return out.transpose(0, 2, 1)


def solution(mesh):
    n_row, n_col = mesh.shape["row"], mesh.shape["col"]
    return jax.shard_map(
        lambda damping, block_seeds: shards(damping, block_seeds, n_row, n_col),
        mesh=mesh,
        in_specs=(P("col", "row", None), P()),
        out_specs=P("row", "col", None),
        check_vma=False,
    )
```

```python
import math

import numpy as np
import jax
import jax.numpy as jnp
from jax import lax
from jax.experimental import pallas as pl
from jax.experimental.pallas import tpu as pltpu
from jax.sharding import PartitionSpec as P

NSTEPS = 12
PRIME = 65521
P_SIZE = 32
BF16 = jnp.bfloat16
F32 = jnp.float32
NT = (((1,), (1,)), ((), ()))


def channel_table(n_freq, freqs, steps, n_blocks):
    angle = math.pi * (np.asarray(freqs)[:, None] + 0.5) / n_freq * np.asarray(steps)[None, :]
    decay = 3.0 ** (-np.asarray(steps) / n_blocks)
    return np.stack([decay * np.cos(angle), decay * np.sin(angle)], axis=1)


def high_low(values):
    high = values.astype(np.float32).astype(jnp.bfloat16)
    low = (values - high.astype(np.float64)).astype(np.float32).astype(jnp.bfloat16)
    return high, low


def _fit(fn, degree):
    nodes = np.cos(np.pi * (np.arange(64) + 0.5) / 64)
    u = (nodes + 1.0) / 128
    series = np.polynomial.chebyshev.Chebyshev.fit(u, fn(np.sqrt(u)), degree, domain=[0.0, 1 / 64])
    return [float(x) for x in series.convert(kind=np.polynomial.Polynomial, domain=[-1, 1], window=[-1, 1]).coef]


COS_COEFS = _fit(lambda t: np.cos(2 * np.pi * t), 5)
SIN_COEFS = _fit(lambda t: np.sin(2 * np.pi * t) / t, 5)


def polynomial(coefs, u):
    out = jnp.full_like(u, coefs[-1])
    for coef in coefs[-2::-1]:
        out = out * u + coef
    return out


def cos_sin(turns):
    quarter = jnp.round(turns * 4.0)
    rest = turns - quarter * 0.25
    u = rest * rest
    cos, sin = polynomial(COS_COEFS, u), polynomial(SIN_COEFS, u) * rest
    odd = jnp.abs(quarter) == 1.0
    far = jnp.abs(quarter) == 2.0
    flip_cos = jnp.logical_or(quarter == 1.0, far)
    flip_sin = jnp.logical_or(quarter == -1.0, far)
    out_cos, out_sin = jnp.where(odd, sin, cos), jnp.where(odd, cos, sin)
    return jnp.where(flip_cos, -out_cos, out_cos), jnp.where(flip_sin, -out_sin, out_sin)


def mod_turns(x):
    return (x - jnp.round(x * (1.0 / PRIME)) * float(PRIME)) * (1.0 / PRIME)


def channel_values(n_freq, n_blocks, freq, step, sine):
    turns = ((2 * freq + 1) * step % (4 * n_freq)).astype(F32) * (0.25 / n_freq)
    cos, sin = cos_sin(turns - jnp.round(turns))
    values = jnp.where(sine, sin, cos) * jnp.exp(step.astype(F32) * (-math.log(3.0) / n_blocks))
    return values


def split(values):
    high = values.astype(BF16).astype(F32)
    return high, values - high


def separate(x, local):
    return jnp.swapaxes(x.reshape(x.shape[0] // local, local, x.shape[1]), 0, 1)


def iotas(rows, cols):
    return (lax.broadcasted_iota(jnp.int32, (rows, cols), d) for d in range(2))


def place(rows, cols, test):
    r = lax.broadcasted_iota(jnp.int32, (rows, cols), 0)
    c = lax.broadcasted_iota(jnp.int32, (rows, cols), 1)
    return test(r, c).astype(F32)


def less_turns(x):
    return x - (x.astype(F32) * (1.0 / PRIME)).astype(jnp.int32) * PRIME


def forward_kernel(local, n_freq, seeds_ref, d_ref, t_ref, held, by_freq, acc, probes, cos_shift, sin_shift, state, spread, q_all, own, sems, sem):
    n_chunks, rows, m = held.shape
    block_c = rows // local
    channels = 2 * local
    n_blocks, lanes = cos_shift.shape[1:]
    group = 8
    tiles = P_SIZE // 8
    width, lane_w = by_freq.shape[3], acc.shape[3]
    passes, per_pass = m // width, width // lane_w

    n_parts = sems.shape[1]

    def copy(b, i):
        part = (slice(b * rows, (b + 1) * rows), slice(i * m // n_parts, (i + 1) * m // n_parts))
        return pltpu.make_async_copy(d_ref.at[part], held.at[b, :, part[1]], sems.at[b, i])

    fetch = pltpu.make_async_copy(seeds_ref, own, sem)
    fetch.start()
    for b in range(n_chunks):
        for i in range(n_parts):
            copy(b, i).start()

    row, col = iotas(channels, n_blocks)
    table = channel_values(n_freq, n_blocks, lax.axis_index("row") * local + row % local, col, row >= local)
    left = place(channels * group, channels, lambda r, c: r // group == c)
    right = place(n_blocks, group * n_blocks, lambda r, c: r == c % n_blocks)
    same = place(channels * group, group * n_blocks, lambda r, c: r % group == c // n_blocks)
    for part, w in enumerate(split(table)):
        w = jnp.dot(w, right, preferred_element_type=F32)
        spread[part] = (jnp.dot(left, w, preferred_element_type=F32) * same).astype(BF16)

    fetch.wait()
    line, lane = iotas(n_blocks, lanes)
    seeds = jnp.zeros((n_blocks, lanes), jnp.int32)
    for j in range(n_blocks):
        seeds = jnp.where(line == j, own[j], seeds)
    steps = (lane + 1).astype(F32)
    shift = mod_turns(seeds.astype(F32) * steps) * float(PRIME)
    shift_parts = cos_sin(mod_turns(jnp.round(shift) * (steps + 1.0)))
    for p in range(P_SIZE):
        for part, out in zip(shift_parts, (cos_shift, sin_shift)):
            out[p] = jnp.broadcast_to(part[:, p : p + 1], (n_blocks, lanes))

    start = lax.axis_index("col") * (n_chunks * block_c)
    spans = [(at, p) for at in range(0, block_c, lanes) for p in range(0, P_SIZE, 8)]

    def make_probes(b, span):
        at, first = span
        if first == 0:
            column = start + b * block_c + at + lane
            inner = less_turns(less_turns(seeds * (column + 1)) * (column + 3)).astype(F32)
            turn_cos, turn_sin = cos_sin(mod_turns(inner))
            cos, sin = turn_cos, turn_sin
        else:
            cos, sin, turn_cos, turn_sin = (state[i] for i in range(4))
        for p in range(first, first + 8):
            value = cos * cos_shift[p] - sin * sin_shift[p]
            probes[p * n_blocks : (p + 1) * n_blocks, at : at + lanes] = value.astype(BF16)
            cos, sin = cos * turn_cos - sin * turn_sin, sin * turn_cos + cos * turn_sin
        for i, x in enumerate((cos, sin, turn_cos, turn_sin)):
            state[i] = x

    def make_channels(b):
        for g in range(P_SIZE // group):
            block = probes[g * group * n_blocks : (g + 1) * group * n_blocks, :]
            q = jnp.dot(spread[0], block, preferred_element_type=F32) + jnp.dot(
                spread[1], block, preferred_element_type=F32
            )
            q = q.astype(BF16)
            for part in range(2):
                for k in range(local):
                    at = (part * local + k) * group
                    to = part * P_SIZE + g * group
                    q_all[b % 2, k, to : to + group, :] = q[at : at + group]

    for span in spans:
        make_probes(0, span)
    make_channels(0)
    for b in range(n_chunks):
        for i in range(passes):
            if i * n_parts % passes == 0:
                copy(b, i * n_parts // passes).wait()
            if b + 1 < n_chunks:
                for span in spans[len(spans) * i // passes : len(spans) * (i + 1) // passes]:
                    make_probes(b + 1, span)
            at = slice(i * width, (i + 1) * width)
            for c in range(0, block_c, 16):
                by_freq[i % 2, :, c : c + 16, :] = separate(held[b, c * local : (c + 16) * local, at], local)
            for k in range(local):
                o = jnp.dot(q_all[b % 2, k], by_freq[i % 2, k], preferred_element_type=F32)
                for l in range(per_pass):
                    for t in range(2 * tiles):
                        piece = o[t * 8 : t * 8 + 8, l * lane_w : (l + 1) * lane_w]
                        if b > 0:
                            piece += acc[i * per_pass + l, t, k * 8 : k * 8 + 8, :]
                        acc[i * per_pass + l, t, k * 8 : k * 8 + 8, :] = piece
            if b + 1 == n_chunks:
                for l in range(i * per_pass, (i + 1) * per_pass):
                    for p in range(P_SIZE):
                        t = jnp.concatenate(
                            [acc[l, part * tiles + p // 8, pl.ds(p % 8, local, stride=8), :] for part in range(2)],
                            axis=0,
                        )
                        t_ref[p, :, l * lane_w : (l + 1) * lane_w] = t.astype(BF16)
        if b + 1 < n_chunks:
            make_channels(b + 1)


def half_of(n_row):
    return lax.axis_index("row") // (n_row // 2)


def gather_kernel(n_row, c_ref, x_ref, keep_ref, send_ref):
    n_src, p_own, channels, lanes = x_ref.shape
    table = c_ref[half_of(n_row)]
    n = table.shape[0] // 2
    for p in range(p_own):
        x = x_ref[:, p].reshape(n_src * channels, lanes)
        both = jnp.dot(table, x, preferred_element_type=F32)
        out = both[:n] + both[n:]
        keep_ref[p] = out
        send_ref[p] = out.astype(BF16)


def scatter_kernel(n_row, b_ref, keep_ref, got_ref, f_ref):
    n_rows, n_cols, p_own, channels, lanes = f_ref.shape
    table = b_ref[half_of(n_row)]
    for p in range(p_own):
        forward = keep_ref[p] + got_ref[p].astype(F32)
        high = forward.astype(BF16)
        low = (forward - high.astype(F32)).astype(BF16)
        out = jnp.dot(table, jnp.concatenate([high, low, high], axis=0), preferred_element_type=F32)
        out = out.astype(BF16).reshape(n_rows, channels, lanes)
        for col in range(n_cols):
            f_ref[:, col, p] = out


def join_kernel(x_ref, keep_ref, send_ref):
    x = x_ref[...].astype(F32)
    total = jnp.sum(x, axis=0)
    keep_ref[...] = total[0]
    send_ref[...] = total[1].astype(BF16)


def blocks_kernel(local, n_row, n_blocks, amp, k_ref):
    channels = 2 * local
    row_at = lax.axis_index("row")
    half, per_owner, quarter = n_blocks // 2, n_blocks // n_row, n_row // 4
    r, c = iotas(n_blocks, channels)
    rest = r % half
    chip = rest // (2 * per_owner) + quarter * ((rest // per_owner + half_of(n_row)) % 2)
    block_at = (2 * chip + (r // half + row_at) % 2) * per_owner + rest % per_owner
    sine = c % 2 == 1
    table = channel_values(local * n_row, n_blocks, row_at * local + c // 2, block_at + 1, sine)
    table = table * jnp.where(sine, -amp, amp)
    left = place(n_blocks * 16, n_blocks, lambda r, c: r // 16 == c)
    right = place(channels, channels * 16, lambda r, c: r == c // 32 * 2 + c // 8 % 2)
    same = place(n_blocks * 16, channels * 16, lambda r, c: r % 16 == c // 16 % 2 * 8 + c % 8)
    for part, k in enumerate(split(table)):
        k = jnp.dot(left, jnp.dot(k, right, preferred_element_type=F32), preferred_element_type=F32)
        k_ref[part] = (k * same).astype(BF16)


def separate_kernel(local, d_ref, o_ref):
    rows, m = d_ref.shape
    for i in range(0, m, 256):
        for c in range(0, rows // local, 16):
            piece = d_ref[c * local : (c + 16) * local, i : i + 256]
            o_ref[:, c : c + 16, i : i + 256] = separate(piece, local)


def backward_kernel(local, n_blocks, n_ready, f_ref, k_ref, d_ref, *refs):
    ready_ref = refs[0] if n_ready else None
    keep_ref, send_ref, raw, held, sums, f_by, k_parts, sems, sem = refs[bool(n_ready) :]
    n_chunks, _, block_c, m = held.shape
    n_subs, n_parts = sems.shape
    n_raw, sub = n_subs - n_ready, block_c * n_chunks // n_subs
    width = m // n_parts
    step = 256 if width % 256 == 0 else width
    tall = sub * local
    rows = f_ref.shape[0] // 4
    half = n_blocks // 2

    def spot(s):
        return s * sub // block_c, slice(s * sub % block_c, s * sub % block_c + sub)

    def copy(s, i):
        at = slice(i * width, (i + 1) * width)
        if s < n_raw:
            return pltpu.make_async_copy(d_ref.at[pl.ds(s * tall, tall), at], raw.at[s, :, at], sems.at[s, i])
        b, columns = spot(s)
        source = ready_ref.at[:, pl.ds((s - n_raw) * sub, sub), at]
        return pltpu.make_async_copy(source, held.at[b, :, columns, at], sems.at[s, i])

    tables = pltpu.make_async_copy(k_ref, k_parts, sem)
    per = n_subs // n_chunks
    order = sorted(range(n_chunks), key=lambda b: (b * per < n_raw, b))
    for i in range(n_parts):
        for b in order:
            for s in range(b * per, (b + 1) * per):
                copy(s, i).start()
    tables.start()

    swap = place(rows, rows, lambda r, c: (r % 8 * 2 + r // 8 % 2) * local + r // 16 == c).astype(BF16)
    for g in range(4):
        out = jnp.dot(swap, f_ref[g * rows : (g + 1) * rows, :], preferred_element_type=F32).astype(BF16)
        for k in range(local):
            f_by[k, g * 16 : g * 16 + 16, :] = out[k * 16 : k * 16 + 16]

    for i in range(n_parts):
        at = slice(i * width, (i + 1) * width)
        for b in order:
            for s in range(b * per, (b + 1) * per):
                copy(s, i).wait()
            for s in range(b * per, min((b + 1) * per, n_raw)):
                base = spot(s)[1].start
                for p in range(i * width, (i + 1) * width, step):
                    for c in range(0, sub, 16):
                        piece = raw[s, c * local : (c + 16) * local, p : p + step]
                        held[b, :, base + c : base + c + 16, p : p + step] = separate(piece, local)
            for k in range(local):
                part = lax.dot_general(f_by[k, :, at], held[b, k, :, at], NT, preferred_element_type=F32)
                sums[b, k] = part if i == 0 else sums[b, k] + part

    tables.wait()
    for b in range(n_chunks):
        at = slice(b * block_c, (b + 1) * block_c)
        u = [sums[b, k].astype(BF16) for k in range(local)]
        for g in range(2):
            block = jnp.concatenate([x[g * 32 : g * 32 + 32] for x in u], axis=0)
            out = jnp.dot(k_parts[0], block, preferred_element_type=F32) + jnp.dot(
                k_parts[1], block, preferred_element_type=F32
            )
            out = out.reshape(2 * half, 16, block_c)
            keep_ref[:, g * 16 : g * 16 + 16, at] = out[:half]
            send_ref[:, g * 16 : g * 16 + 16, at] = out[half:].astype(BF16)


def gram_kernel(keep_ref, got_ref, mine_ref, gram_ref):
    mine = keep_ref[...] + got_ref[...].astype(F32)
    mine_ref[...] = mine
    gram = jnp.zeros((P_SIZE, P_SIZE), F32)
    for j in range(mine.shape[0]):
        gram += lax.dot_general(
            mine[j], mine[j], NT, preferred_element_type=F32, precision=lax.Precision.HIGHEST
        )
    gram = jnp.concatenate([gram[8 * i : 8 * i + 8] for i in range(P_SIZE // 8)], axis=1)
    for i in range(gram_ref.shape[0]):
        gram_ref[i] = gram


def last_kernel(factor, gram_ref, mine_ref, out_ref):
    total = jnp.sum(gram_ref[...], axis=0)
    gram = jnp.concatenate([total[:, P_SIZE * i : P_SIZE * (i + 1)] for i in range(P_SIZE // 8)], axis=0)
    row = lax.broadcasted_iota(jnp.int32, (P_SIZE, P_SIZE), 0)
    col = lax.broadcasted_iota(jnp.int32, (P_SIZE, P_SIZE), 1)
    eye = jnp.where(row == col, 1.0, 0.0).astype(F32)
    scale = jnp.sum(gram * eye, keepdims=True) + 1e-06

    def dot(a, b):
        return jnp.dot(a, b, preferred_element_type=F32, precision=lax.Precision.HIGH)

    current = gram / scale
    inverse = eye
    for _ in range(NSTEPS):
        weight = 1.5 * eye - 0.5 * dot(inverse, current)
        current = dot(current, weight)
        inverse = dot(weight, inverse)
    inverse = inverse * (factor / jnp.sqrt(scale))
    for j in range(mine_ref.shape[0]):
        out_ref[j] = lax.dot_general(
            inverse,
            mine_ref[j],
            (((0,), (0,)), ((), ())),
            preferred_element_type=F32,
            precision=lax.Precision.HIGHEST,
        )


def vmem(n):
    return [pl.BlockSpec(memory_space=pltpu.VMEM)] * n


def shards(damping, block_seeds, n_row, n_col):
    cols, local, m = damping.shape
    n_blocks = block_seeds.shape[0]
    n_freq = local * n_row
    channels = 2 * local
    n_dev = n_row * n_col
    amp = math.sqrt(2.0 / n_freq) / math.sqrt(n_blocks * m)
    most, large, params = (pltpu.CompilerParams(vmem_limit_bytes=x << 20) for x in (54, 46, 20))

    block_c = 256 if cols % 256 == 0 else cols
    lanes_c = 128 if block_c % 128 == 0 else block_c
    lane_w = 128 if m % 128 == 0 else m
    per_pass = 2 if m % (2 * lane_w) == 0 else 1
    halves_m = 2 if m % (4 * lane_w) == 0 else 1
    flat = damping.reshape(cols * local, m)

    w_row = channel_table(n_freq, np.arange(n_freq), np.arange(n_blocks), n_blocks)
    w_row = w_row.reshape(n_row, local, 2, n_blocks).transpose(0, 2, 1, 3)
    sign = np.array([1.0, -1.0])[None, :, None, None] * amp
    per_owner, half, quarter = n_blocks // n_row, n_blocks // 2, n_row // 4

    n_rows = P_SIZE * channels
    whole = lambda *s: pl.BlockSpec(s, lambda i: (0,) * len(s))
    v_one = pl.BlockSpec(memory_space=pltpu.VMEM)
    work = 2 * cols * local * m
    t = pl.pallas_call(
        lambda *refs: forward_kernel(local, n_freq, *refs),
        out_shape=jax.ShapeDtypeStruct((P_SIZE, channels, m), BF16),
        in_specs=[pl.BlockSpec(memory_space=pl.ANY)] * 2,
        out_specs=v_one,
        scratch_shapes=[
            pltpu.VMEM((cols // block_c, block_c * local, m), BF16),
            pltpu.VMEM((2, local, block_c, per_pass * lane_w), BF16),
            pltpu.VMEM((m // lane_w, P_SIZE // 4, 8 * local, lane_w), F32),
            pltpu.VMEM((P_SIZE * n_blocks, block_c), BF16),
            pltpu.VMEM((P_SIZE, n_blocks, lanes_c), F32),
            pltpu.VMEM((P_SIZE, n_blocks, lanes_c), F32),
            pltpu.VMEM((4, n_blocks, lanes_c), F32),
            pltpu.VMEM((2, channels * 8, 8 * n_blocks), BF16),
            pltpu.VMEM((2, local, 2 * P_SIZE, block_c), BF16),
            pltpu.SMEM((n_blocks,), jnp.int32),
            pltpu.SemaphoreType.DMA((cols // block_c, halves_m)),
            pltpu.SemaphoreType.DMA,
        ],
        compiler_params=large,
        cost_estimate=pl.CostEstimate(flops=64 * work, bytes_accessed=work, transcendentals=0),
        name="forward",
    )(pltpu.with_memory_space_constraint(block_seeds, pltpu.HBM), flat)
    n_grp = n_dev // 2
    n_p = math.gcd(P_SIZE, n_grp)
    n_r = n_grp // n_p
    p_own, lanes = P_SIZE // n_p, m // n_r
    halves = [list(range(n_grp)), list(range(n_grp, n_dev))]
    across = [(i, (i + n_row // 2) % n_row) for i in range(n_row)]
    t = t.reshape(n_p, p_own * channels, n_r, lanes).transpose(0, 2, 1, 3)
    t = t.reshape(n_grp, p_own * channels, lanes)
    t = lax.all_to_all(t, ("row", "col"), 0, 0, axis_index_groups=halves, tiled=True)
    t = t.reshape(n_grp, p_own, channels, lanes)

    merge = (w_row * sign).reshape(2, n_row // 2, 1, channels, n_blocks).repeat(n_col, axis=2)
    merge = merge.reshape(2, n_grp * channels, n_blocks).transpose(0, 2, 1)
    merge = np.concatenate(high_low(merge), axis=1)
    b_hi, b_lo = high_low(w_row.reshape(2, n_row // 2 * channels, n_blocks))
    fan = np.concatenate([b_hi, b_hi, b_lo], axis=2)
    keep, send = pl.pallas_call(
        lambda *refs: gather_kernel(n_row, *refs),
        out_shape=(
            jax.ShapeDtypeStruct((p_own, n_blocks, lanes), F32),
            jax.ShapeDtypeStruct((p_own, n_blocks, lanes), BF16),
        ),
        in_specs=vmem(2),
        out_specs=tuple(vmem(2)),
        compiler_params=params,
        name="gather",
    )(jnp.asarray(merge), t)
    send, flat = lax.optimization_barrier((send, flat))
    got = lax.ppermute(send, "row", across)
    sub = block_c // 2
    n_subs = cols // sub
    n_ready = n_subs // 2 if m % 256 == 0 and n_subs > 2 else 0
    n_raw = n_subs - n_ready
    k_tables = pl.pallas_call(
        lambda *refs: blocks_kernel(local, n_row, n_blocks, amp, *refs),
        out_shape=jax.ShapeDtypeStruct((2, n_blocks * 16, channels * 16), BF16),
        in_specs=[],
        out_specs=v_one,
        compiler_params=params,
        cost_estimate=pl.CostEstimate(flops=10**9, bytes_accessed=10**6, transcendentals=0),
        name="blocks",
    )()
    ready = []
    if n_ready:
        ready.append(
            pl.pallas_call(
                lambda *refs: separate_kernel(local, *refs),
                grid=(n_ready,),
                out_shape=jax.ShapeDtypeStruct((local, n_ready * sub, m), BF16),
                in_specs=[pl.BlockSpec((sub * local, m), lambda i: (i + n_raw, 0))],
                out_specs=pl.BlockSpec((local, sub, m), lambda i: (0, i, 0)),
                compiler_params=most,
                cost_estimate=pl.CostEstimate(flops=work, bytes_accessed=2 * work, transcendentals=0),
                name="separate",
            )(flat)
        )
    got, k_tables, *ready = lax.optimization_barrier((got, k_tables, *ready))
    f = pl.pallas_call(
        lambda *refs: scatter_kernel(n_row, *refs),
        out_shape=jax.ShapeDtypeStruct((n_row // 2, n_col, p_own, channels, lanes), BF16),
        in_specs=vmem(3),
        out_specs=v_one,
        compiler_params=params,
        name="scatter",
    )(jnp.asarray(fan), keep, got)
    f = f.reshape(n_grp, p_own * channels, lanes)
    f = lax.all_to_all(f, ("row", "col"), 0, 0, axis_index_groups=halves, tiled=True)
    f = f.reshape(n_p, n_r, p_own * channels, lanes).transpose(0, 2, 1, 3).reshape(n_rows, m)

    n_parts = 3 if m % 768 == 0 else 1
    n_chunks = cols // block_c
    keep, send = pl.pallas_call(
        lambda *refs: backward_kernel(local, n_blocks, n_ready, *refs),
        out_shape=(
            jax.ShapeDtypeStruct((half, P_SIZE, cols), F32),
            jax.ShapeDtypeStruct((half, P_SIZE, cols), BF16),
        ),
        in_specs=vmem(1) + [pl.BlockSpec(memory_space=pl.ANY)] * (2 + len(ready)),
        out_specs=tuple(vmem(2)),
        scratch_shapes=[
            pltpu.VMEM((n_raw, sub * local, m), BF16),
            pltpu.VMEM((n_chunks, local, block_c, m), BF16),
            pltpu.VMEM((n_chunks, local, 2 * P_SIZE, block_c), F32),
            pltpu.VMEM((local, 2 * P_SIZE, m), BF16),
            pltpu.VMEM((2, n_blocks * 16, channels * 16), BF16),
            pltpu.SemaphoreType.DMA((n_subs, n_parts)),
            pltpu.SemaphoreType.DMA,
        ],
        compiler_params=large,
        cost_estimate=pl.CostEstimate(flops=64 * work, bytes_accessed=work, transcendentals=0),
        name="backward",
    )(f, k_tables, flat, *ready)
    got = lax.ppermute(send, "row", [(i, i ^ 1) for i in range(n_row)])
    summed = (keep + got.astype(F32)).astype(BF16)
    groups = [[core + 2 * (i + quarter * h) for i in range(quarter)] for h in range(2) for core in range(2)]
    summed = lax.all_to_all(summed, "row", 0, 0, axis_index_groups=groups, tiled=True)
    summed = summed.reshape(quarter, 2, per_owner, P_SIZE, cols)
    keep, send = pl.pallas_call(
        join_kernel,
        out_shape=(
            jax.ShapeDtypeStruct((per_owner, P_SIZE, cols), F32),
            jax.ShapeDtypeStruct((per_owner, P_SIZE, cols), BF16),
        ),
        in_specs=vmem(1),
        out_specs=tuple(vmem(2)),
        compiler_params=params,
        name="join",
    )(summed)
    got = lax.ppermute(send, "row", across)

    mine, gram = pl.pallas_call(
        gram_kernel,
        out_shape=(
            jax.ShapeDtypeStruct((per_owner, P_SIZE, cols), F32),
            jax.ShapeDtypeStruct((n_dev, 8, 4 * P_SIZE), F32),
        ),
        in_specs=vmem(2),
        out_specs=tuple(vmem(2)),
        compiler_params=params,
        name="gram",
    )(keep, got)
    gram = lax.all_to_all(gram, ("row", "col"), 0, 0, tiled=True)
    out = pl.pallas_call(
        lambda *refs: last_kernel(math.sqrt(n_blocks * m), *refs),
        out_shape=jax.ShapeDtypeStruct((per_owner, P_SIZE, cols), F32),
        in_specs=vmem(2),
        out_specs=vmem(1)[0],
        compiler_params=params,
        name="last",
    )(gram, mine)
    return out.transpose(0, 2, 1)


def solution(mesh):
    n_row, n_col = mesh.shape["row"], mesh.shape["col"]
    return jax.shard_map(
        lambda damping, block_seeds: shards(damping, block_seeds, n_row, n_col),
        mesh=mesh,
        in_specs=(P("col", "row", None), P()),
        out_specs=P("row", "col", None),
        check_vma=False,
    )
```

```python
import math

import numpy as np
import jax
import jax.numpy as jnp
from jax import lax
from jax.experimental import pallas as pl
from jax.experimental.pallas import tpu as pltpu
from jax.sharding import PartitionSpec as P

NSTEPS = 12
PRIME = 65521
P_SIZE = 32
BF16 = jnp.bfloat16
F32 = jnp.float32
NT = (((1,), (1,)), ((), ()))


def channel_table(n_freq, freqs, steps, n_blocks):
    angle = math.pi * (np.asarray(freqs)[:, None] + 0.5) / n_freq * np.asarray(steps)[None, :]
    decay = 3.0 ** (-np.asarray(steps) / n_blocks)
    return np.stack([decay * np.cos(angle), decay * np.sin(angle)], axis=1)


def high_low(values):
    high = values.astype(np.float32).astype(jnp.bfloat16)
    low = (values - high.astype(np.float64)).astype(np.float32).astype(jnp.bfloat16)
    return high, low


def _fit(fn, degree):
    nodes = np.cos(np.pi * (np.arange(64) + 0.5) / 64)
    u = (nodes + 1.0) / 128
    series = np.polynomial.chebyshev.Chebyshev.fit(u, fn(np.sqrt(u)), degree, domain=[0.0, 1 / 64])
    return [float(x) for x in series.convert(kind=np.polynomial.Polynomial, domain=[-1, 1], window=[-1, 1]).coef]


COS_COEFS = _fit(lambda t: np.cos(2 * np.pi * t), 5)
SIN_COEFS = _fit(lambda t: np.sin(2 * np.pi * t) / t, 5)


def polynomial(coefs, u):
    out = jnp.full_like(u, coefs[-1])
    for coef in coefs[-2::-1]:
        out = out * u + coef
    return out


def cos_sin(turns):
    quarter = jnp.round(turns * 4.0)
    rest = turns - quarter * 0.25
    u = rest * rest
    cos, sin = polynomial(COS_COEFS, u), polynomial(SIN_COEFS, u) * rest
    odd = jnp.abs(quarter) == 1.0
    far = jnp.abs(quarter) == 2.0
    flip_cos = jnp.logical_or(quarter == 1.0, far)
    flip_sin = jnp.logical_or(quarter == -1.0, far)
    out_cos, out_sin = jnp.where(odd, sin, cos), jnp.where(odd, cos, sin)
    return jnp.where(flip_cos, -out_cos, out_cos), jnp.where(flip_sin, -out_sin, out_sin)


def mod_turns(x):
    return (x - jnp.round(x * (1.0 / PRIME)) * float(PRIME)) * (1.0 / PRIME)


def channel_values(n_freq, n_blocks, freq, step, sine):
    turns = ((2 * freq + 1) * step % (4 * n_freq)).astype(F32) * (0.25 / n_freq)
    cos, sin = cos_sin(turns - jnp.round(turns))
    values = jnp.where(sine, sin, cos) * jnp.exp(step.astype(F32) * (-math.log(3.0) / n_blocks))
    return values


def split(values):
    high = values.astype(BF16).astype(F32)
    return high, values - high


def separate(x, local):
    return jnp.swapaxes(x.reshape(x.shape[0] // local, local, x.shape[1]), 0, 1)


def iotas(rows, cols):
    return (lax.broadcasted_iota(jnp.int32, (rows, cols), d) for d in range(2))


def place(rows, cols, test):
    r = lax.broadcasted_iota(jnp.int32, (rows, cols), 0)
    c = lax.broadcasted_iota(jnp.int32, (rows, cols), 1)
    return test(r, c).astype(F32)


def less_turns(x):
    return x - (x.astype(F32) * (1.0 / PRIME)).astype(jnp.int32) * PRIME


def forward_kernel(local, n_freq, seeds_ref, d_ref, t_ref, held, by_freq, acc, probes, cos_shift, sin_shift, state, spread, q_all, own, sems, sem):
    n_chunks, rows, m = held.shape
    block_c = rows // local
    channels = 2 * local
    n_blocks, lanes = cos_shift.shape[1:]
    group = 8
    tiles = P_SIZE // 8
    width, lane_w = by_freq.shape[3], acc.shape[3]
    passes, per_pass = m // width, width // lane_w

    n_parts = sems.shape[1]

    def copy(b, i):
        part = (slice(b * rows, (b + 1) * rows), slice(i * m // n_parts, (i + 1) * m // n_parts))
        return pltpu.make_async_copy(d_ref.at[part], held.at[b, :, part[1]], sems.at[b, i])

    fetch = pltpu.make_async_copy(seeds_ref, own, sem)
    fetch.start()
    for b in range(n_chunks):
        for i in range(n_parts):
            copy(b, i).start()

    row, col = iotas(channels, n_blocks)
    table = channel_values(n_freq, n_blocks, lax.axis_index("row") * local + row % local, col, row >= local)
    left = place(channels * group, channels, lambda r, c: r // group == c)
    right = place(n_blocks, group * n_blocks, lambda r, c: r == c % n_blocks)
    same = place(channels * group, group * n_blocks, lambda r, c: r % group == c // n_blocks)
    for part, w in enumerate(split(table)):
        w = jnp.dot(w, right, preferred_element_type=F32)
        spread[part] = (jnp.dot(left, w, preferred_element_type=F32) * same).astype(BF16)

    fetch.wait()
    line, lane = iotas(n_blocks, lanes)
    seeds = jnp.zeros((n_blocks, lanes), jnp.int32)
    for j in range(n_blocks):
        seeds = jnp.where(line == j, own[j], seeds)
    steps = (lane + 1).astype(F32)
    shift = mod_turns(seeds.astype(F32) * steps) * float(PRIME)
    shift_parts = cos_sin(mod_turns(jnp.round(shift) * (steps + 1.0)))
    for p in range(P_SIZE):
        for part, out in zip(shift_parts, (cos_shift, sin_shift)):
            out[p] = jnp.broadcast_to(part[:, p : p + 1], (n_blocks, lanes))

    start = lax.axis_index("col") * (n_chunks * block_c)
    spans = [(at, p) for at in range(0, block_c, lanes) for p in range(0, P_SIZE, 8)]

    def make_probes(b, span):
        at, first = span
        if first == 0:
            column = start + b * block_c + at + lane
            inner = less_turns(less_turns(seeds * (column + 1)) * (column + 3)).astype(F32)
            turn_cos, turn_sin = cos_sin(mod_turns(inner))
            cos, sin = turn_cos, turn_sin
        else:
            cos, sin, turn_cos, turn_sin = (state[i] for i in range(4))
        for p in range(first, first + 8):
            value = cos * cos_shift[p] - sin * sin_shift[p]
            probes[p * n_blocks : (p + 1) * n_blocks, at : at + lanes] = value.astype(BF16)
            cos, sin = cos * turn_cos - sin * turn_sin, sin * turn_cos + cos * turn_sin
        for i, x in enumerate((cos, sin, turn_cos, turn_sin)):
            state[i] = x

    def make_channels(b):
        for g in range(P_SIZE // group):
            block = probes[g * group * n_blocks : (g + 1) * group * n_blocks, :]
            q = jnp.dot(spread[0], block, preferred_element_type=F32) + jnp.dot(
                spread[1], block, preferred_element_type=F32
            )
            q = q.astype(BF16)
            for part in range(2):
                for k in range(local):
                    at = (part * local + k) * group
                    to = part * P_SIZE + g * group
                    q_all[b % 2, k, to : to + group, :] = q[at : at + group]

    for span in spans:
        make_probes(0, span)
    make_channels(0)
    for b in range(n_chunks):
        for i in range(passes):
            if i * n_parts % passes == 0:
                copy(b, i * n_parts // passes).wait()
            if b + 1 < n_chunks:
                for span in spans[len(spans) * i // passes : len(spans) * (i + 1) // passes]:
                    make_probes(b + 1, span)
            at = slice(i * width, (i + 1) * width)
            for c in range(0, block_c, 16):
                by_freq[i % 2, :, c : c + 16, :] = separate(held[b, c * local : (c + 16) * local, at], local)
            for k in range(local):
                o = jnp.dot(q_all[b % 2, k], by_freq[i % 2, k], preferred_element_type=F32)
                for l in range(per_pass):
                    for t in range(2 * tiles):
                        piece = o[t * 8 : t * 8 + 8, l * lane_w : (l + 1) * lane_w]
                        if b > 0:
                            piece += acc[i * per_pass + l, t, k * 8 : k * 8 + 8, :]
                        acc[i * per_pass + l, t, k * 8 : k * 8 + 8, :] = piece
            if b + 1 == n_chunks:
                for l in range(i * per_pass, (i + 1) * per_pass):
                    for p in range(P_SIZE):
                        t = jnp.concatenate(
                            [acc[l, part * tiles + p // 8, pl.ds(p % 8, local, stride=8), :] for part in range(2)],
                            axis=0,
                        )
                        t_ref[p, :, l * lane_w : (l + 1) * lane_w] = t.astype(BF16)
        if b + 1 < n_chunks:
            make_channels(b + 1)


def half_of(n_row):
    return lax.axis_index("row") // (n_row // 2)


def gather_kernel(n_row, c_ref, x_ref, keep_ref, send_ref):
    n_src, p_own, channels, lanes = x_ref.shape
    table = c_ref[half_of(n_row)]
    n = table.shape[0] // 2
    for p in range(p_own):
        x = x_ref[:, p].reshape(n_src * channels, lanes)
        both = jnp.dot(table, x, preferred_element_type=F32)
        out = both[:n] + both[n:]
        keep_ref[p] = out
        send_ref[p] = out.astype(BF16)


def scatter_kernel(n_row, b_ref, keep_ref, got_ref, f_ref):
    n_rows, n_cols, p_own, channels, lanes = f_ref.shape
    table = b_ref[half_of(n_row)]
    for p in range(p_own):
        forward = keep_ref[p] + got_ref[p].astype(F32)
        high = forward.astype(BF16)
        low = (forward - high.astype(F32)).astype(BF16)
        out = jnp.dot(table, jnp.concatenate([high, low, high], axis=0), preferred_element_type=F32)
        out = out.astype(BF16).reshape(n_rows, channels, lanes)
        for col in range(n_cols):
            f_ref[:, col, p] = out


def join_kernel(x_ref, keep_ref, send_ref):
    x = x_ref[...].astype(F32)
    total = jnp.sum(x, axis=0)
    keep_ref[...] = total[0]
    send_ref[...] = total[1].astype(BF16)


def blocks_kernel(local, n_row, n_blocks, amp, k_ref):
    channels = 2 * local
    row_at = lax.axis_index("row")
    half, per_owner, quarter = n_blocks // 2, n_blocks // n_row, n_row // 4
    r, c = iotas(n_blocks, channels)
    rest = r % half
    chip = rest // (2 * per_owner) + quarter * ((rest // per_owner + half_of(n_row)) % 2)
    block_at = (2 * chip + (r // half + row_at) % 2) * per_owner + rest % per_owner
    sine = c % 2 == 1
    table = channel_values(local * n_row, n_blocks, row_at * local + c // 2, block_at + 1, sine)
    table = table * jnp.where(sine, -amp, amp)
    left = place(n_blocks * 16, n_blocks, lambda r, c: r // 16 == c)
    right = place(channels, channels * 16, lambda r, c: r == c // 32 * 2 + c // 8 % 2)
    same = place(n_blocks * 16, channels * 16, lambda r, c: r % 16 == c // 16 % 2 * 8 + c % 8)
    for part, k in enumerate(split(table)):
        k = jnp.dot(left, jnp.dot(k, right, preferred_element_type=F32), preferred_element_type=F32)
        k_ref[part] = (k * same).astype(BF16)


def separate_kernel(local, d_ref, o_ref):
    rows, m = d_ref.shape
    for i in range(0, m, 256):
        for c in range(0, rows // local, 16):
            piece = d_ref[c * local : (c + 16) * local, i : i + 256]
            o_ref[:, c : c + 16, i : i + 256] = separate(piece, local)


def backward_kernel(local, n_blocks, n_ready, f_ref, k_ref, d_ref, *refs):
    ready_ref = refs[0] if n_ready else None
    keep_ref, send_ref, raw, held, sums, f_by, k_parts, sems, sem = refs[bool(n_ready) :]
    n_chunks, _, block_c, m = held.shape
    n_subs, n_parts = sems.shape
    n_raw, sub = n_subs - n_ready, block_c * n_chunks // n_subs
    width = m // n_parts
    step = 256 if width % 256 == 0 else width
    tall = sub * local
    rows = f_ref.shape[0] // 4
    half = n_blocks // 2

    def spot(s):
        return s * sub // block_c, slice(s * sub % block_c, s * sub % block_c + sub)

    def copy(s, i):
        at = slice(i * width, (i + 1) * width)
        if s < n_raw:
            return pltpu.make_async_copy(d_ref.at[pl.ds(s * tall, tall), at], raw.at[s, :, at], sems.at[s, i])
        b, columns = spot(s)
        source = ready_ref.at[:, pl.ds((s - n_raw) * sub, sub), at]
        return pltpu.make_async_copy(source, held.at[b, :, columns, at], sems.at[s, i])

    tables = pltpu.make_async_copy(k_ref, k_parts, sem)
    per = n_subs // n_chunks
    order = range(n_chunks)
    for i in range(n_parts):
        for b in order:
            for s in range(b * per, (b + 1) * per):
                copy(s, i).start()
    tables.start()

    swap = place(rows, rows, lambda r, c: (r % 8 * 2 + r // 8 % 2) * local + r // 16 == c).astype(BF16)
    for g in range(4):
        out = jnp.dot(swap, f_ref[g * rows : (g + 1) * rows, :], preferred_element_type=F32).astype(BF16)
        for k in range(local):
            f_by[k, g * 16 : g * 16 + 16, :] = out[k * 16 : k * 16 + 16]

    for i in range(n_parts):
        at = slice(i * width, (i + 1) * width)
        for b in order:
            for s in range(b * per, (b + 1) * per):
                copy(s, i).wait()
            for s in range(b * per, min((b + 1) * per, n_raw)):
                base = spot(s)[1].start
                for p in range(i * width, (i + 1) * width, step):
                    for c in range(0, sub, 16):
                        piece = raw[s, c * local : (c + 16) * local, p : p + step]
                        held[b, :, base + c : base + c + 16, p : p + step] = separate(piece, local)
            for k in range(local):
                part = lax.dot_general(f_by[k, :, at], held[b, k, :, at], NT, preferred_element_type=F32)
                sums[b, k] = part if i == 0 else sums[b, k] + part

    tables.wait()
    for b in range(n_chunks):
        at = slice(b * block_c, (b + 1) * block_c)
        u = [sums[b, k].astype(BF16) for k in range(local)]
        for g in range(2):
            block = jnp.concatenate([x[g * 32 : g * 32 + 32] for x in u], axis=0)
            out = jnp.dot(k_parts[0], block, preferred_element_type=F32) + jnp.dot(
                k_parts[1], block, preferred_element_type=F32
            )
            out = out.reshape(2 * half, 16, block_c)
            keep_ref[:, g * 16 : g * 16 + 16, at] = out[:half]
            send_ref[:, g * 16 : g * 16 + 16, at] = out[half:].astype(BF16)


def gram_kernel(keep_ref, got_ref, mine_ref, gram_ref):
    mine = keep_ref[...] + got_ref[...].astype(F32)
    mine_ref[...] = mine
    gram = jnp.zeros((P_SIZE, P_SIZE), F32)
    for j in range(mine.shape[0]):
        gram += lax.dot_general(
            mine[j], mine[j], NT, preferred_element_type=F32, precision=lax.Precision.HIGHEST
        )
    gram = jnp.concatenate([gram[8 * i : 8 * i + 8] for i in range(P_SIZE // 8)], axis=1)
    for i in range(gram_ref.shape[0]):
        gram_ref[i] = gram


def last_kernel(factor, gram_ref, mine_ref, out_ref):
    total = jnp.sum(gram_ref[...], axis=0)
    gram = jnp.concatenate([total[:, P_SIZE * i : P_SIZE * (i + 1)] for i in range(P_SIZE // 8)], axis=0)
    row = lax.broadcasted_iota(jnp.int32, (P_SIZE, P_SIZE), 0)
    col = lax.broadcasted_iota(jnp.int32, (P_SIZE, P_SIZE), 1)
    eye = jnp.where(row == col, 1.0, 0.0).astype(F32)
    scale = jnp.sum(gram * eye, keepdims=True) + 1e-06

    def dot(a, b):
        return jnp.dot(a, b, preferred_element_type=F32, precision=lax.Precision.HIGH)

    current = gram / scale
    inverse = eye
    for _ in range(NSTEPS):
        weight = 1.5 * eye - 0.5 * dot(inverse, current)
        current = dot(current, weight)
        inverse = dot(weight, inverse)
    inverse = inverse * (factor / jnp.sqrt(scale))
    for j in range(mine_ref.shape[0]):
        out_ref[j] = lax.dot_general(
            inverse,
            mine_ref[j],
            (((0,), (0,)), ((), ())),
            preferred_element_type=F32,
            precision=lax.Precision.HIGHEST,
        )


def vmem(n):
    return [pl.BlockSpec(memory_space=pltpu.VMEM)] * n


def shards(damping, block_seeds, n_row, n_col):
    cols, local, m = damping.shape
    n_blocks = block_seeds.shape[0]
    n_freq = local * n_row
    channels = 2 * local
    n_dev = n_row * n_col
    amp = math.sqrt(2.0 / n_freq) / math.sqrt(n_blocks * m)
    most, large, params = (pltpu.CompilerParams(vmem_limit_bytes=x << 20) for x in (54, 46, 20))

    block_c = 256 if cols % 256 == 0 else cols
    lanes_c = 128 if block_c % 128 == 0 else block_c
    lane_w = 128 if m % 128 == 0 else m
    per_pass = 2 if m % (2 * lane_w) == 0 else 1
    halves_m = 2 if m % (4 * lane_w) == 0 else 1
    flat = damping.reshape(cols * local, m)

    w_row = channel_table(n_freq, np.arange(n_freq), np.arange(n_blocks), n_blocks)
    w_row = w_row.reshape(n_row, local, 2, n_blocks).transpose(0, 2, 1, 3)
    sign = np.array([1.0, -1.0])[None, :, None, None] * amp
    per_owner, half, quarter = n_blocks // n_row, n_blocks // 2, n_row // 4

    n_rows = P_SIZE * channels
    whole = lambda *s: pl.BlockSpec(s, lambda i: (0,) * len(s))
    v_one = pl.BlockSpec(memory_space=pltpu.VMEM)
    work = 2 * cols * local * m
    t = pl.pallas_call(
        lambda *refs: forward_kernel(local, n_freq, *refs),
        out_shape=jax.ShapeDtypeStruct((P_SIZE, channels, m), BF16),
        in_specs=[pl.BlockSpec(memory_space=pl.ANY)] * 2,
        out_specs=v_one,
        scratch_shapes=[
            pltpu.VMEM((cols // block_c, block_c * local, m), BF16),
            pltpu.VMEM((2, local, block_c, per_pass * lane_w), BF16),
            pltpu.VMEM((m // lane_w, P_SIZE // 4, 8 * local, lane_w), F32),
            pltpu.VMEM((P_SIZE * n_blocks, block_c), BF16),
            pltpu.VMEM((P_SIZE, n_blocks, lanes_c), F32),
            pltpu.VMEM((P_SIZE, n_blocks, lanes_c), F32),
            pltpu.VMEM((4, n_blocks, lanes_c), F32),
            pltpu.VMEM((2, channels * 8, 8 * n_blocks), BF16),
            pltpu.VMEM((2, local, 2 * P_SIZE, block_c), BF16),
            pltpu.SMEM((n_blocks,), jnp.int32),
            pltpu.SemaphoreType.DMA((cols // block_c, halves_m)),
            pltpu.SemaphoreType.DMA,
        ],
        compiler_params=large,
        cost_estimate=pl.CostEstimate(flops=64 * work, bytes_accessed=work, transcendentals=0),
        name="forward",
    )(pltpu.with_memory_space_constraint(block_seeds, pltpu.HBM), flat)
    n_grp = n_dev // 2
    n_p = math.gcd(P_SIZE, n_grp)
    n_r = n_grp // n_p
    p_own, lanes = P_SIZE // n_p, m // n_r
    halves = [list(range(n_grp)), list(range(n_grp, n_dev))]
    across = [(i, (i + n_row // 2) % n_row) for i in range(n_row)]
    t = t.reshape(n_p, p_own * channels, n_r, lanes).transpose(0, 2, 1, 3)
    t = t.reshape(n_grp, p_own * channels, lanes)
    t = lax.all_to_all(t, ("row", "col"), 0, 0, axis_index_groups=halves, tiled=True)
    t = t.reshape(n_grp, p_own, channels, lanes)

    merge = (w_row * sign).reshape(2, n_row // 2, 1, channels, n_blocks).repeat(n_col, axis=2)
    merge = merge.reshape(2, n_grp * channels, n_blocks).transpose(0, 2, 1)
    merge = np.concatenate(high_low(merge), axis=1)
    b_hi, b_lo = high_low(w_row.reshape(2, n_row // 2 * channels, n_blocks))
    fan = np.concatenate([b_hi, b_hi, b_lo], axis=2)
    keep, send = pl.pallas_call(
        lambda *refs: gather_kernel(n_row, *refs),
        out_shape=(
            jax.ShapeDtypeStruct((p_own, n_blocks, lanes), F32),
            jax.ShapeDtypeStruct((p_own, n_blocks, lanes), BF16),
        ),
        in_specs=vmem(2),
        out_specs=tuple(vmem(2)),
        compiler_params=params,
        name="gather",
    )(jnp.asarray(merge), t)
    send, flat = lax.optimization_barrier((send, flat))
    got = lax.ppermute(send, "row", across)
    sub = block_c // 2
    n_subs = cols // sub
    n_ready = n_subs // 2 if m % 256 == 0 and n_subs > 2 else 0
    n_raw = n_subs - n_ready
    k_tables = pl.pallas_call(
        lambda *refs: blocks_kernel(local, n_row, n_blocks, amp, *refs),
        out_shape=jax.ShapeDtypeStruct((2, n_blocks * 16, channels * 16), BF16),
        in_specs=[],
        out_specs=v_one,
        compiler_params=params,
        cost_estimate=pl.CostEstimate(flops=10**9, bytes_accessed=10**6, transcendentals=0),
        name="blocks",
    )()
    ready = []
    if n_ready:
        ready.append(
            pl.pallas_call(
                lambda *refs: separate_kernel(local, *refs),
                grid=(n_ready,),
                out_shape=jax.ShapeDtypeStruct((local, n_ready * sub, m), BF16),
                in_specs=[pl.BlockSpec((sub * local, m), lambda i: (i + n_raw, 0))],
                out_specs=pl.BlockSpec((local, sub, m), lambda i: (0, i, 0)),
                compiler_params=most,
                cost_estimate=pl.CostEstimate(flops=work, bytes_accessed=2 * work, transcendentals=0),
                name="separate",
            )(flat)
        )
    got, k_tables, *ready = lax.optimization_barrier((got, k_tables, *ready))
    f = pl.pallas_call(
        lambda *refs: scatter_kernel(n_row, *refs),
        out_shape=jax.ShapeDtypeStruct((n_row // 2, n_col, p_own, channels, lanes), BF16),
        in_specs=vmem(3),
        out_specs=v_one,
        compiler_params=params,
        name="scatter",
    )(jnp.asarray(fan), keep, got)
    f = f.reshape(n_grp, p_own * channels, lanes)
    f = lax.all_to_all(f, ("row", "col"), 0, 0, axis_index_groups=halves, tiled=True)
    f = f.reshape(n_p, n_r, p_own * channels, lanes).transpose(0, 2, 1, 3).reshape(n_rows, m)

    n_parts = 3 if m % 768 == 0 else 1
    n_chunks = cols // block_c
    keep, send = pl.pallas_call(
        lambda *refs: backward_kernel(local, n_blocks, n_ready, *refs),
        out_shape=(
            jax.ShapeDtypeStruct((half, P_SIZE, cols), F32),
            jax.ShapeDtypeStruct((half, P_SIZE, cols), BF16),
        ),
        in_specs=vmem(1) + [pl.BlockSpec(memory_space=pl.ANY)] * (2 + len(ready)),
        out_specs=tuple(vmem(2)),
        scratch_shapes=[
            pltpu.VMEM((n_raw, sub * local, m), BF16),
            pltpu.VMEM((n_chunks, local, block_c, m), BF16),
            pltpu.VMEM((n_chunks, local, 2 * P_SIZE, block_c), F32),
            pltpu.VMEM((local, 2 * P_SIZE, m), BF16),
            pltpu.VMEM((2, n_blocks * 16, channels * 16), BF16),
            pltpu.SemaphoreType.DMA((n_subs, n_parts)),
            pltpu.SemaphoreType.DMA,
        ],
        compiler_params=large,
        cost_estimate=pl.CostEstimate(flops=64 * work, bytes_accessed=work, transcendentals=0),
        name="backward",
    )(f, k_tables, flat, *ready)
    got = lax.ppermute(send, "row", [(i, i ^ 1) for i in range(n_row)])
    summed = (keep + got.astype(F32)).astype(BF16)
    groups = [[core + 2 * (i + quarter * h) for i in range(quarter)] for h in range(2) for core in range(2)]
    summed = lax.all_to_all(summed, "row", 0, 0, axis_index_groups=groups, tiled=True)
    summed = summed.reshape(quarter, 2, per_owner, P_SIZE, cols)
    keep, send = pl.pallas_call(
        join_kernel,
        out_shape=(
            jax.ShapeDtypeStruct((per_owner, P_SIZE, cols), F32),
            jax.ShapeDtypeStruct((per_owner, P_SIZE, cols), BF16),
        ),
        in_specs=vmem(1),
        out_specs=tuple(vmem(2)),
        compiler_params=params,
        name="join",
    )(summed)
    got = lax.ppermute(send, "row", across)

    mine, gram = pl.pallas_call(
        gram_kernel,
        out_shape=(
            jax.ShapeDtypeStruct((per_owner, P_SIZE, cols), F32),
            jax.ShapeDtypeStruct((n_dev, 8, 4 * P_SIZE), F32),
        ),
        in_specs=vmem(2),
        out_specs=tuple(vmem(2)),
        compiler_params=params,
        name="gram",
    )(keep, got)
    gram = lax.all_to_all(gram, ("row", "col"), 0, 0, tiled=True)
    out = pl.pallas_call(
        lambda *refs: last_kernel(math.sqrt(n_blocks * m), *refs),
        out_shape=jax.ShapeDtypeStruct((per_owner, P_SIZE, cols), F32),
        in_specs=vmem(2),
        out_specs=vmem(1)[0],
        compiler_params=params,
        name="last",
    )(gram, mine)
    return out.transpose(0, 2, 1)


def solution(mesh):
    n_row, n_col = mesh.shape["row"], mesh.shape["col"]
    return jax.shard_map(
        lambda damping, block_seeds: shards(damping, block_seeds, n_row, n_col),
        mesh=mesh,
        in_specs=(P("col", "row", None), P()),
        out_specs=P("row", "col", None),
        check_vma=False,
    )
```

```python
import math

import numpy as np
import jax
import jax.numpy as jnp
from jax import lax
from jax.experimental import pallas as pl
from jax.experimental.pallas import tpu as pltpu
from jax.sharding import PartitionSpec as P

NSTEPS = 12
PRIME = 65521
P_SIZE = 32
BF16 = jnp.bfloat16
F32 = jnp.float32
NT = (((1,), (1,)), ((), ()))


def channel_table(n_freq, freqs, steps, n_blocks):
    angle = math.pi * (np.asarray(freqs)[:, None] + 0.5) / n_freq * np.asarray(steps)[None, :]
    decay = 3.0 ** (-np.asarray(steps) / n_blocks)
    return np.stack([decay * np.cos(angle), decay * np.sin(angle)], axis=1)


def high_low(values):
    high = values.astype(np.float32).astype(jnp.bfloat16)
    low = (values - high.astype(np.float64)).astype(np.float32).astype(jnp.bfloat16)
    return high, low


def _fit(fn, degree):
    nodes = np.cos(np.pi * (np.arange(64) + 0.5) / 64)
    u = (nodes + 1.0) / 128
    series = np.polynomial.chebyshev.Chebyshev.fit(u, fn(np.sqrt(u)), degree, domain=[0.0, 1 / 64])
    return [float(x) for x in series.convert(kind=np.polynomial.Polynomial, domain=[-1, 1], window=[-1, 1]).coef]


COS_COEFS = _fit(lambda t: np.cos(2 * np.pi * t), 5)
SIN_COEFS = _fit(lambda t: np.sin(2 * np.pi * t) / t, 5)


def polynomial(coefs, u):
    out = jnp.full_like(u, coefs[-1])
    for coef in coefs[-2::-1]:
        out = out * u + coef
    return out


def cos_sin(turns):
    quarter = jnp.round(turns * 4.0)
    rest = turns - quarter * 0.25
    u = rest * rest
    cos, sin = polynomial(COS_COEFS, u), polynomial(SIN_COEFS, u) * rest
    odd = jnp.abs(quarter) == 1.0
    far = jnp.abs(quarter) == 2.0
    flip_cos = jnp.logical_or(quarter == 1.0, far)
    flip_sin = jnp.logical_or(quarter == -1.0, far)
    out_cos, out_sin = jnp.where(odd, sin, cos), jnp.where(odd, cos, sin)
    return jnp.where(flip_cos, -out_cos, out_cos), jnp.where(flip_sin, -out_sin, out_sin)


def mod_turns(x):
    return (x - jnp.round(x * (1.0 / PRIME)) * float(PRIME)) * (1.0 / PRIME)


def channel_values(n_freq, n_blocks, freq, step, sine):
    turns = ((2 * freq + 1) * step % (4 * n_freq)).astype(F32) * (0.25 / n_freq)
    cos, sin = cos_sin(turns - jnp.round(turns))
    values = jnp.where(sine, sin, cos) * jnp.exp(step.astype(F32) * (-math.log(3.0) / n_blocks))
    return values


def split(values):
    high = values.astype(BF16).astype(F32)
    return high, values - high


def separate(x, local):
    return jnp.swapaxes(x.reshape(x.shape[0] // local, local, x.shape[1]), 0, 1)


def iotas(rows, cols):
    return (lax.broadcasted_iota(jnp.int32, (rows, cols), d) for d in range(2))


def place(rows, cols, test):
    r = lax.broadcasted_iota(jnp.int32, (rows, cols), 0)
    c = lax.broadcasted_iota(jnp.int32, (rows, cols), 1)
    return test(r, c).astype(F32)


def less_turns(x):
    return x - (x.astype(F32) * (1.0 / PRIME)).astype(jnp.int32) * PRIME


def forward_kernel(local, n_freq, seeds_ref, d_ref, t_ref, held, by_freq, acc, probes, cos_shift, sin_shift, state, spread, q_all, own, sems, sem):
    n_chunks, rows, m = held.shape
    block_c = rows // local
    channels = 2 * local
    n_blocks, lanes = cos_shift.shape[1:]
    group = 8
    tiles = P_SIZE // 8
    width, lane_w = by_freq.shape[3], acc.shape[3]
    passes, per_pass = m // width, width // lane_w

    n_parts = sems.shape[1]

    def copy(b, i):
        part = (slice(b * rows, (b + 1) * rows), slice(i * m // n_parts, (i + 1) * m // n_parts))
        return pltpu.make_async_copy(d_ref.at[part], held.at[b, :, part[1]], sems.at[b, i])

    fetch = pltpu.make_async_copy(seeds_ref, own, sem)
    fetch.start()
    for b in range(n_chunks):
        for i in range(n_parts):
            copy(b, i).start()

    row, col = iotas(channels, n_blocks)
    table = channel_values(n_freq, n_blocks, lax.axis_index("row") * local + row % local, col, row >= local)
    left = place(channels * group, channels, lambda r, c: r // group == c)
    right = place(n_blocks, group * n_blocks, lambda r, c: r == c % n_blocks)
    same = place(channels * group, group * n_blocks, lambda r, c: r % group == c // n_blocks)
    for part, w in enumerate(split(table)):
        w = jnp.dot(w, right, preferred_element_type=F32)
        spread[part] = (jnp.dot(left, w, preferred_element_type=F32) * same).astype(BF16)

    fetch.wait()
    line, lane = iotas(n_blocks, lanes)
    seeds = jnp.zeros((n_blocks, lanes), jnp.int32)
    for j in range(n_blocks):
        seeds = jnp.where(line == j, own[j], seeds)
    steps = (lane + 1).astype(F32)
    shift = mod_turns(seeds.astype(F32) * steps) * float(PRIME)
    shift_parts = cos_sin(mod_turns(jnp.round(shift) * (steps + 1.0)))
    for p in range(P_SIZE):
        for part, out in zip(shift_parts, (cos_shift, sin_shift)):
            out[p] = jnp.broadcast_to(part[:, p : p + 1], (n_blocks, lanes))

    start = lax.axis_index("col") * (n_chunks * block_c)
    spans = [(at, p) for at in range(0, block_c, lanes) for p in range(0, P_SIZE, 8)]

    def make_probes(b, span):
        at, first = span
        if first == 0:
            column = start + b * block_c + at + lane
            inner = less_turns(less_turns(seeds * (column + 1)) * (column + 3)).astype(F32)
            turn_cos, turn_sin = cos_sin(mod_turns(inner))
            cos, sin = turn_cos, turn_sin
        else:
            cos, sin, turn_cos, turn_sin = (state[i] for i in range(4))
        for p in range(first, first + 8):
            value = cos * cos_shift[p] - sin * sin_shift[p]
            probes[p * n_blocks : (p + 1) * n_blocks, at : at + lanes] = value.astype(BF16)
            cos, sin = cos * turn_cos - sin * turn_sin, sin * turn_cos + cos * turn_sin
        for i, x in enumerate((cos, sin, turn_cos, turn_sin)):
            state[i] = x

    def make_channels(b):
        for g in range(P_SIZE // group):
            block = probes[g * group * n_blocks : (g + 1) * group * n_blocks, :]
            q = jnp.dot(spread[0], block, preferred_element_type=F32) + jnp.dot(
                spread[1], block, preferred_element_type=F32
            )
            q = q.astype(BF16)
            for part in range(2):
                for k in range(local):
                    at = (part * local + k) * group
                    to = part * P_SIZE + g * group
                    q_all[b % 2, k, to : to + group, :] = q[at : at + group]

    for span in spans:
        make_probes(0, span)
    make_channels(0)
    for b in range(n_chunks):
        for i in range(passes):
            if i * n_parts % passes == 0:
                copy(b, i * n_parts // passes).wait()
            if b + 1 < n_chunks:
                for span in spans[len(spans) * i // passes : len(spans) * (i + 1) // passes]:
                    make_probes(b + 1, span)
            at = slice(i * width, (i + 1) * width)
            for c in range(0, block_c, 16):
                by_freq[i % 2, :, c : c + 16, :] = separate(held[b, c * local : (c + 16) * local, at], local)
            for k in range(local):
                o = jnp.dot(q_all[b % 2, k], by_freq[i % 2, k], preferred_element_type=F32)
                for l in range(per_pass):
                    for t in range(2 * tiles):
                        piece = o[t * 8 : t * 8 + 8, l * lane_w : (l + 1) * lane_w]
                        if b > 0:
                            piece += acc[i * per_pass + l, t, k * 8 : k * 8 + 8, :]
                        acc[i * per_pass + l, t, k * 8 : k * 8 + 8, :] = piece
            if b + 1 == n_chunks:
                for l in range(i * per_pass, (i + 1) * per_pass):
                    for p in range(P_SIZE):
                        t = jnp.concatenate(
                            [acc[l, part * tiles + p // 8, pl.ds(p % 8, local, stride=8), :] for part in range(2)],
                            axis=0,
                        )
                        t_ref[p, :, l * lane_w : (l + 1) * lane_w] = t.astype(BF16)
        if b + 1 < n_chunks:
            make_channels(b + 1)


def half_of(n_row):
    return lax.axis_index("row") // (n_row // 2)


def gather_kernel(n_row, c_ref, x_ref, keep_ref, send_ref):
    n_src, p_own, channels, lanes = x_ref.shape
    table = c_ref[half_of(n_row)]
    n = table.shape[0] // 2
    for p in range(p_own):
        x = x_ref[:, p].reshape(n_src * channels, lanes)
        both = jnp.dot(table, x, preferred_element_type=F32)
        out = both[:n] + both[n:]
        keep_ref[p] = out
        send_ref[p] = out.astype(BF16)


def scatter_kernel(n_row, b_ref, keep_ref, got_ref, f_ref):
    n_rows, n_cols, p_own, channels, lanes = f_ref.shape
    table = b_ref[half_of(n_row)]
    for p in range(p_own):
        forward = keep_ref[p] + got_ref[p].astype(F32)
        high = forward.astype(BF16)
        low = (forward - high.astype(F32)).astype(BF16)
        out = jnp.dot(table, jnp.concatenate([high, low, high], axis=0), preferred_element_type=F32)
        out = out.astype(BF16).reshape(n_rows, channels, lanes)
        for col in range(n_cols):
            f_ref[:, col, p] = out


def join_kernel(x_ref, keep_ref, send_ref):
    x = x_ref[...].astype(F32)
    total = jnp.sum(x, axis=0)
    keep_ref[...] = total[0]
    send_ref[...] = total[1].astype(BF16)


def blocks_kernel(local, n_row, n_blocks, amp, k_ref):
    channels = 2 * local
    row_at = lax.axis_index("row")
    half, per_owner, quarter = n_blocks // 2, n_blocks // n_row, n_row // 4
    r, c = iotas(n_blocks, channels)
    rest = r % half
    chip = rest // (2 * per_owner) + quarter * ((rest // per_owner + half_of(n_row)) % 2)
    block_at = (2 * chip + (r // half + row_at) % 2) * per_owner + rest % per_owner
    sine = c % 2 == 1
    table = channel_values(local * n_row, n_blocks, row_at * local + c // 2, block_at + 1, sine)
    table = table * jnp.where(sine, -amp, amp)
    left = place(n_blocks * 16, n_blocks, lambda r, c: r // 16 == c)
    right = place(channels, channels * 16, lambda r, c: r == c // 32 * 2 + c // 8 % 2)
    same = place(n_blocks * 16, channels * 16, lambda r, c: r % 16 == c // 16 % 2 * 8 + c % 8)
    for part, k in enumerate(split(table)):
        k = jnp.dot(left, jnp.dot(k, right, preferred_element_type=F32), preferred_element_type=F32)
        k_ref[part] = (k * same).astype(BF16)


def separate_kernel(local, d_ref, o_ref):
    rows, m = d_ref.shape
    for i in range(0, m, 256):
        for c in range(0, rows // local, 16):
            piece = d_ref[c * local : (c + 16) * local, i : i + 256]
            o_ref[:, c : c + 16, i : i + 256] = separate(piece, local)


def backward_kernel(local, n_blocks, n_ready, f_ref, k_ref, d_ref, *refs):
    ready_ref = refs[0] if n_ready else None
    keep_ref, send_ref, raw, held, sums, f_by, k_parts, sems, sem = refs[bool(n_ready) :]
    n_chunks, _, block_c, m = held.shape
    n_parts = sems.shape[1]
    width = m // n_parts
    tall = block_c * local
    rows = f_ref.shape[0] // 4
    half = n_blocks // 2

    def copy(b, i):
        at = slice(i * width, (i + 1) * width)
        if b == 0:
            return pltpu.make_async_copy(d_ref.at[pl.ds(0, tall), at], raw.at[:, at], sems.at[b, i])
        source = ready_ref.at[:, pl.ds((b - 1) * block_c, block_c), at]
        return pltpu.make_async_copy(source, held.at[b, :, :, at], sems.at[b, i])

    tables = pltpu.make_async_copy(k_ref, k_parts, sem)
    for i in range(n_parts):
        for b in range(n_chunks):
            copy(b, i).start()
    tables.start()

    swap = place(rows, rows, lambda r, c: (r % 8 * 2 + r // 8 % 2) * local + r // 16 == c).astype(BF16)
    for g in range(4):
        out = jnp.dot(swap, f_ref[g * rows : (g + 1) * rows, :], preferred_element_type=F32).astype(BF16)
        for k in range(local):
            f_by[k, g * 16 : g * 16 + 16, :] = out[k * 16 : k * 16 + 16]

    for i in range(n_parts):
        at = slice(i * width, (i + 1) * width)
        for b in range(n_chunks):
            copy(b, i).wait()
        for c in range(0, block_c, 16):
            held[0, :, c : c + 16, at] = separate(raw[c * local : (c + 16) * local, at], local)
        for b in (*range(1, n_chunks), 0):
            for k in range(local):
                part = lax.dot_general(f_by[k, :, at], held[b, k, :, at], NT, preferred_element_type=F32)
                sums[b, k] = part if i == 0 else sums[b, k] + part

    tables.wait()
    for b in range(n_chunks):
        at = slice(b * block_c, (b + 1) * block_c)
        u = [sums[b, k].astype(BF16) for k in range(local)]
        for g in range(2):
            block = jnp.concatenate([x[g * 32 : g * 32 + 32] for x in u], axis=0)
            out = jnp.dot(k_parts[0], block, preferred_element_type=F32) + jnp.dot(
                k_parts[1], block, preferred_element_type=F32
            )
            out = out.reshape(2 * half, 16, block_c)
            keep_ref[:, g * 16 : g * 16 + 16, at] = out[:half]
            send_ref[:, g * 16 : g * 16 + 16, at] = out[half:].astype(BF16)


def gram_kernel(keep_ref, got_ref, mine_ref, gram_ref):
    mine = keep_ref[...] + got_ref[...].astype(F32)
    mine_ref[...] = mine
    gram = jnp.zeros((P_SIZE, P_SIZE), F32)
    for j in range(mine.shape[0]):
        gram += lax.dot_general(
            mine[j], mine[j], NT, preferred_element_type=F32, precision=lax.Precision.HIGHEST
        )
    gram = jnp.concatenate([gram[8 * i : 8 * i + 8] for i in range(P_SIZE // 8)], axis=1)
    for i in range(gram_ref.shape[0]):
        gram_ref[i] = gram


def last_kernel(factor, gram_ref, mine_ref, out_ref):
    total = jnp.sum(gram_ref[...], axis=0)
    gram = jnp.concatenate([total[:, P_SIZE * i : P_SIZE * (i + 1)] for i in range(P_SIZE // 8)], axis=0)
    row = lax.broadcasted_iota(jnp.int32, (P_SIZE, P_SIZE), 0)
    col = lax.broadcasted_iota(jnp.int32, (P_SIZE, P_SIZE), 1)
    eye = jnp.where(row == col, 1.0, 0.0).astype(F32)
    scale = jnp.sum(gram * eye, keepdims=True) + 1e-06

    def dot(a, b):
        return jnp.dot(a, b, preferred_element_type=F32, precision=lax.Precision.HIGH)

    current = gram / scale
    inverse = eye
    for _ in range(NSTEPS):
        weight = 1.5 * eye - 0.5 * dot(inverse, current)
        current = dot(current, weight)
        inverse = dot(weight, inverse)
    inverse = inverse * (factor / jnp.sqrt(scale))
    for j in range(mine_ref.shape[0]):
        out_ref[j] = lax.dot_general(
            inverse,
            mine_ref[j],
            (((0,), (0,)), ((), ())),
            preferred_element_type=F32,
            precision=lax.Precision.HIGHEST,
        )


def vmem(n):
    return [pl.BlockSpec(memory_space=pltpu.VMEM)] * n


def shards(damping, block_seeds, n_row, n_col):
    cols, local, m = damping.shape
    n_blocks = block_seeds.shape[0]
    n_freq = local * n_row
    channels = 2 * local
    n_dev = n_row * n_col
    amp = math.sqrt(2.0 / n_freq) / math.sqrt(n_blocks * m)
    most, large, params = (pltpu.CompilerParams(vmem_limit_bytes=x << 20) for x in (54, 44, 20))

    block_c = 256 if cols % 256 == 0 else cols
    lanes_c = 128 if block_c % 128 == 0 else block_c
    lane_w = 128 if m % 128 == 0 else m
    per_pass = 2 if m % (2 * lane_w) == 0 else 1
    halves_m = 2 if m % (4 * lane_w) == 0 else 1
    flat = damping.reshape(cols * local, m)

    w_row = channel_table(n_freq, np.arange(n_freq), np.arange(n_blocks), n_blocks)
    w_row = w_row.reshape(n_row, local, 2, n_blocks).transpose(0, 2, 1, 3)
    sign = np.array([1.0, -1.0])[None, :, None, None] * amp
    per_owner, half, quarter = n_blocks // n_row, n_blocks // 2, n_row // 4

    n_rows = P_SIZE * channels
    whole = lambda *s: pl.BlockSpec(s, lambda i: (0,) * len(s))
    v_one = pl.BlockSpec(memory_space=pltpu.VMEM)
    work = 2 * cols * local * m
    t = pl.pallas_call(
        lambda *refs: forward_kernel(local, n_freq, *refs),
        out_shape=jax.ShapeDtypeStruct((P_SIZE, channels, m), BF16),
        in_specs=[pl.BlockSpec(memory_space=pl.ANY)] * 2,
        out_specs=v_one,
        scratch_shapes=[
            pltpu.VMEM((cols // block_c, block_c * local, m), BF16),
            pltpu.VMEM((2, local, block_c, per_pass * lane_w), BF16),
            pltpu.VMEM((m // lane_w, P_SIZE // 4, 8 * local, lane_w), F32),
            pltpu.VMEM((P_SIZE * n_blocks, block_c), BF16),
            pltpu.VMEM((P_SIZE, n_blocks, lanes_c), F32),
            pltpu.VMEM((P_SIZE, n_blocks, lanes_c), F32),
            pltpu.VMEM((4, n_blocks, lanes_c), F32),
            pltpu.VMEM((2, channels * 8, 8 * n_blocks), BF16),
            pltpu.VMEM((2, local, 2 * P_SIZE, block_c), BF16),
            pltpu.SMEM((n_blocks,), jnp.int32),
            pltpu.SemaphoreType.DMA((cols // block_c, halves_m)),
            pltpu.SemaphoreType.DMA,
        ],
        compiler_params=large,
        cost_estimate=pl.CostEstimate(flops=64 * work, bytes_accessed=work, transcendentals=0),
        name="forward",
    )(pltpu.with_memory_space_constraint(block_seeds, pltpu.HBM), flat)
    n_grp = n_dev // 2
    n_p = math.gcd(P_SIZE, n_grp)
    n_r = n_grp // n_p
    p_own, lanes = P_SIZE // n_p, m // n_r
    halves = [list(range(n_grp)), list(range(n_grp, n_dev))]
    across = [(i, (i + n_row // 2) % n_row) for i in range(n_row)]
    t = t.reshape(n_p, p_own * channels, n_r, lanes).transpose(0, 2, 1, 3)
    t = t.reshape(n_grp, p_own * channels, lanes)
    t = lax.all_to_all(t, ("row", "col"), 0, 0, axis_index_groups=halves, tiled=True)
    t = t.reshape(n_grp, p_own, channels, lanes)

    merge = (w_row * sign).reshape(2, n_row // 2, 1, channels, n_blocks).repeat(n_col, axis=2)
    merge = merge.reshape(2, n_grp * channels, n_blocks).transpose(0, 2, 1)
    merge = np.concatenate(high_low(merge), axis=1)
    b_hi, b_lo = high_low(w_row.reshape(2, n_row // 2 * channels, n_blocks))
    fan = np.concatenate([b_hi, b_hi, b_lo], axis=2)
    keep, send = pl.pallas_call(
        lambda *refs: gather_kernel(n_row, *refs),
        out_shape=(
            jax.ShapeDtypeStruct((p_own, n_blocks, lanes), F32),
            jax.ShapeDtypeStruct((p_own, n_blocks, lanes), BF16),
        ),
        in_specs=vmem(2),
        out_specs=tuple(vmem(2)),
        compiler_params=params,
        name="gather",
    )(jnp.asarray(merge), t)
    send, flat = lax.optimization_barrier((send, flat))
    got = lax.ppermute(send, "row", across)
    n_ready = cols // block_c - 1 if m % 256 == 0 else 0
    k_tables = pl.pallas_call(
        lambda *refs: blocks_kernel(local, n_row, n_blocks, amp, *refs),
        out_shape=jax.ShapeDtypeStruct((2, n_blocks * 16, channels * 16), BF16),
        in_specs=[],
        out_specs=v_one,
        compiler_params=params,
        cost_estimate=pl.CostEstimate(flops=10**9, bytes_accessed=10**6, transcendentals=0),
        name="blocks",
    )()
    ready = []
    if n_ready:
        ready.append(
            pl.pallas_call(
                lambda *refs: separate_kernel(local, *refs),
                grid=(2 * n_ready,),
                out_shape=jax.ShapeDtypeStruct((local, n_ready * block_c, m), BF16),
                in_specs=[pl.BlockSpec((block_c // 2 * local, m), lambda i: (i + 2, 0))],
                out_specs=pl.BlockSpec((local, block_c // 2, m), lambda i: (0, i, 0)),
                compiler_params=most,
                cost_estimate=pl.CostEstimate(flops=work, bytes_accessed=2 * work, transcendentals=0),
                name="separate",
            )(flat)
        )
    got, k_tables, *ready = lax.optimization_barrier((got, k_tables, *ready))
    f = pl.pallas_call(
        lambda *refs: scatter_kernel(n_row, *refs),
        out_shape=jax.ShapeDtypeStruct((n_row // 2, n_col, p_own, channels, lanes), BF16),
        in_specs=vmem(3),
        out_specs=v_one,
        compiler_params=params,
        name="scatter",
    )(jnp.asarray(fan), keep, got)
    f = f.reshape(n_grp, p_own * channels, lanes)
    f = lax.all_to_all(f, ("row", "col"), 0, 0, axis_index_groups=halves, tiled=True)
    f = f.reshape(n_p, n_r, p_own * channels, lanes).transpose(0, 2, 1, 3).reshape(n_rows, m)

    n_parts = m // 256 if m % 256 == 0 else 1
    n_chunks = n_ready + 1
    deep = cols // n_chunks
    keep, send = pl.pallas_call(
        lambda *refs: backward_kernel(local, n_blocks, n_ready, *refs),
        out_shape=(
            jax.ShapeDtypeStruct((half, P_SIZE, cols), F32),
            jax.ShapeDtypeStruct((half, P_SIZE, cols), BF16),
        ),
        in_specs=vmem(1) + [pl.BlockSpec(memory_space=pl.ANY)] * (2 + len(ready)),
        out_specs=tuple(vmem(2)),
        scratch_shapes=[
            pltpu.VMEM((deep * local, m), BF16),
            pltpu.VMEM((n_chunks, local, deep, m), BF16),
            pltpu.VMEM((n_chunks, local, 2 * P_SIZE, deep), F32),
            pltpu.VMEM((local, 2 * P_SIZE, m), BF16),
            pltpu.VMEM((2, n_blocks * 16, channels * 16), BF16),
            pltpu.SemaphoreType.DMA((n_chunks, n_parts)),
            pltpu.SemaphoreType.DMA,
        ],
        compiler_params=large,
        cost_estimate=pl.CostEstimate(flops=64 * work, bytes_accessed=work, transcendentals=0),
        name="backward",
    )(f, k_tables, flat, *ready)
    got = lax.ppermute(send, "row", [(i, i ^ 1) for i in range(n_row)])
    summed = (keep + got.astype(F32)).astype(BF16)
    groups = [[core + 2 * (i + quarter * h) for i in range(quarter)] for h in range(2) for core in range(2)]
    summed = lax.all_to_all(summed, "row", 0, 0, axis_index_groups=groups, tiled=True)
    summed = summed.reshape(quarter, 2, per_owner, P_SIZE, cols)
    keep, send = pl.pallas_call(
        join_kernel,
        out_shape=(
            jax.ShapeDtypeStruct((per_owner, P_SIZE, cols), F32),
            jax.ShapeDtypeStruct((per_owner, P_SIZE, cols), BF16),
        ),
        in_specs=vmem(1),
        out_specs=tuple(vmem(2)),
        compiler_params=params,
        name="join",
    )(summed)
    got = lax.ppermute(send, "row", across)

    mine, gram = pl.pallas_call(
        gram_kernel,
        out_shape=(
            jax.ShapeDtypeStruct((per_owner, P_SIZE, cols), F32),
            jax.ShapeDtypeStruct((n_dev, 8, 4 * P_SIZE), F32),
        ),
        in_specs=vmem(2),
        out_specs=tuple(vmem(2)),
        compiler_params=params,
        name="gram",
    )(keep, got)
    gram = lax.all_to_all(gram, ("row", "col"), 0, 0, tiled=True)
    out = pl.pallas_call(
        lambda *refs: last_kernel(math.sqrt(n_blocks * m), *refs),
        out_shape=jax.ShapeDtypeStruct((per_owner, P_SIZE, cols), F32),
        in_specs=vmem(2),
        out_specs=vmem(1)[0],
        compiler_params=params,
        name="last",
    )(gram, mine)
    return out.transpose(0, 2, 1)


def solution(mesh):
    n_row, n_col = mesh.shape["row"], mesh.shape["col"]
    return jax.shard_map(
        lambda damping, block_seeds: shards(damping, block_seeds, n_row, n_col),
        mesh=mesh,
        in_specs=(P("col", "row", None), P()),
        out_specs=P("row", "col", None),
        check_vma=False,
    )
```
